32 devices in a mesh: groups: 2 (over y), tensor: 4 (over z), section: 4 (over x, core).
Axes of the slice: x: 2, y: 2, z: 4, core: 2. Of those that a mesh axis runs over, the one named last changes fastest.
Arguments:
- inputs: bfloat16 [4, 64, 8192], P('groups', None, 'tensor'), parts along dimension 0, may hold values from -6 to 6
- gains: bfloat16 [4, 8192], P('section'), may hold values from 0.099609375 to 1.8984375
- keep_mask: int32 [4, 128, 128], P('section', 'tensor'), may hold values from 0 to 1, as said below
- block_values: bfloat16 [4, 12288, 4096], P('section', 'tensor'), may hold values from -0.09375 to 0.09375
- head: bfloat16 [32000, 8192], P(('tensor', 'section')), may hold values from -30 to 30
- targets: int32 [4, 64], P('groups'), parts along dimension 0, may hold values from 0 to 31999
Outputs:
- token_loss: float32 [4, 64], P('groups'), parts along dimension 0
- mean_loss: float32 [2], P('groups'), parts along dimension 0
The draws below stay inside these ranges and needn't reach their ends.
There are 2 independent parts, one for each index of `groups`. The reference program is written for one: setup_inputs(seed, part) draws one part's arguments, and reference() takes and returns one part's arrays. A program takes and returns all parts, laid end to end along the dimension named above; an argument that names none is the same for every part. Nothing has to cross between parts.
Inputs may be any that keep to these rules, and one draw needn't show every extreme that they name: `keep_mask`: in each section, band t (block rows t * 32 to (t + 1) * 32 - 1) keeps between 1024 and 3072 blocks, and some band of each section keeps exactly 3072. List slots past a band's count of kept blocks are not read.
All inputs are finite; a program needn't handle non-finite values.
Results may differ from the reference program's by a relative error of at most 0.0044.
The reference program's roundings to bfloat16 on the way count: a program that leaves them out, or rounds other values in their place, can miss the bound.
Values may be sent and summed in bfloat16 or wider, within the bound.
A program may use at most 320 MiB of HBM per device.

```python
import math
import jax
import jax.numpy as jnp
import numpy as np
from jax import lax

D = 8192
VOCAB = 32000
BLK = 64
MICRO = 2
MB = 64
SECTIONS = 4
NB = 128
RB = 32
BAND = 4096
NBMAX = 3072
N_TENSOR = 4


def draw_keep_mask(key, part):
    key_count, key_extra, key_most, key_order = jax.random.split(key, 4)
    quarter = BAND // 4
    counts = quarter + jax.random.randint(key_count, (SECTIONS, N_TENSOR), 0, quarter + 1) + jax.random.randint(key_extra, (SECTIONS, N_TENSOR), 0, quarter + 1)
    fullest = jax.random.randint(key_most, (SECTIONS, 1), 0, N_TENSOR)
    counts = jnp.where(jnp.arange(N_TENSOR)[None, :] == fullest, NBMAX, counts)
    order_keys = jax.random.split(key_order, SECTIONS * N_TENSOR)
    orders = jax.vmap(lambda subkey: jax.random.permutation(subkey, BAND))(order_keys)
    ranks = jnp.argsort(orders, axis=1)
    kept = (ranks < counts.reshape(-1, 1)).astype(jnp.int32)
    return kept.reshape(SECTIONS, NB, NB)


def draw_head(key, part):
    key_base = jax.random.fold_in(key, 0)
    key_jitter = jax.random.fold_in(key, 5)
    spread = 1.0 / math.sqrt(D)
    position = jnp.arange(VOCAB, dtype=jnp.float32)[:, None] / VOCAB
    jitter = jnp.exp(jax.random.uniform(key_jitter, (VOCAB, 1), jnp.float32, 0.0, math.log(1.5)))
    row_scale = 0.8 * jnp.exp(position * math.log(10.0)) * jitter
    base = jnp.clip(jax.random.normal(key_base, (VOCAB, D), jnp.float32), -6.0, 6.0) * spread * row_scale
    return base.astype(jnp.bfloat16)


def plant(result, key, smallest, largest):
    longest = result.shape.index(max(result.shape))
    spots = []
    for shift in (0, 1):
        where = [jax.random.randint(jax.random.fold_in(key, axis), (), 0, length) for axis, length in enumerate(result.shape)]
        where[longest] = (where[longest] + shift) % result.shape[longest]
        spots.append(tuple(where))
    return result.at[spots[0]].set(smallest).at[spots[1]].set(largest)


def block_levels(key, extent, pieces, least, top_value):
    level = 1.0
    for axis_at, blocks in pieces:
        steps = jax.random.uniform(jax.random.fold_in(jax.random.fold_in(key, 6), axis_at), (blocks,), jnp.float32, least / len(pieces), top_value / len(pieces))
        level = level * jnp.repeat(jnp.exp(steps), extent[axis_at] // blocks).reshape((-1,) + (1,) * (len(extent) - 1 - axis_at))
    return level


def cumulative_ranks(count, lean):
    loads = [(1 << 20) // math.isqrt(rank ** lean) + 1 for rank in range(1, count + 1)]
    scale = 1 + sum(loads) // (1 << 30)
    return np.cumsum(np.array([max(1, weight // scale) for weight in loads]))


def ranked_ids(stream_key, shape, count, lean):
    table = cumulative_ranks(count, lean)
    ticket = jax.random.randint(jax.random.fold_in(stream_key, 1), shape, 0, int(table[count - 1]))
    rank = jnp.searchsorted(jnp.asarray(table, jnp.int32), ticket, side="right")
    return jax.random.permutation(jax.random.fold_in(stream_key, 2), count)[rank].astype(jnp.int32)


def centred(own_key, extent, width, most, cuts=(), held_as=jnp.bfloat16):
    array = width * jax.random.normal(own_key, extent, jnp.float32)
    if cuts:
        array = array * block_levels(own_key, extent, cuts, -0.22, 0.18)
    return jnp.clip(array, -most, most).astype(held_as)


def setup_inputs(seed: int = 0, part: int = 0) -> dict:
    streams_of = jax.random.split(jax.random.key(seed), 7)
    own_keys = jax.random.split(jax.random.fold_in(streams_of[6], part), 7)
    return {
        "inputs": centred(own_keys[0], (MICRO, MB, D), 1.0, 6.0, ((2, 4),)),
        "gains": jnp.clip(1.0 + 0.18 * jax.random.normal(streams_of[1], (SECTIONS, D), jnp.float32), 0.099609375, 1.8984375).astype(jnp.bfloat16),
        "keep_mask": draw_keep_mask(jax.random.fold_in(streams_of[6], 71), part),
        "block_values": centred(streams_of[3], (SECTIONS, N_TENSOR * NBMAX, BLK * BLK), (D // 2) ** -0.5, 0.09375, ((0, 4), (1, 4))),
        "head": draw_head(jax.random.fold_in(streams_of[6], 71), part),
        "targets": plant(ranked_ids(own_keys[5], (MICRO, MB), VOCAB, 2), jax.random.fold_in(own_keys[5], 3), 0, VOCAB - 1).astype(jnp.int32),
    }


epsilon = 1e-05

def section_weight(mask_section, values_section):
    flat_mask = mask_section.reshape(N_TENSOR, BAND)
    slots = jnp.cumsum(flat_mask, axis=1, dtype=jnp.int32) - 1
    slots = jnp.clip(slots, 0, NBMAX - 1).astype(jnp.int32)
    lists = values_section.reshape(N_TENSOR, NBMAX, BLK * BLK)
    picked = jax.vmap(lambda table, where: table[where])(lists, slots)
    picked = picked * flat_mask[:, :, None].astype(jnp.bfloat16)
    blocks = picked.reshape(N_TENSOR, RB, NB, BLK, BLK)
    return blocks.transpose(0, 1, 3, 2, 4).reshape(D, D)

def reference(inputs, gains, keep_mask, block_values, head, targets):
    hidden = inputs.reshape(MICRO * MB, D)
    for section_number in range(SECTIONS):
        weight_matrix = section_weight(keep_mask[section_number], block_values[section_number])
        wide = hidden.astype(jnp.float32)
        sumsq = lax.optimization_barrier(jnp.sum(wide * wide, axis=1, keepdims=True))
        scaled = (wide * gains[section_number].astype(jnp.float32)).astype(jnp.bfloat16)
        product = jnp.dot(scaled, weight_matrix, preferred_element_type=jnp.float32)
        hidden = (wide + product * lax.rsqrt(sumsq / D + epsilon)).astype(jnp.bfloat16)
    wide = hidden.astype(jnp.float32)
    final_sumsq = lax.optimization_barrier(jnp.sum(wide * wide, axis=1, keepdims=True))
    logits = jnp.dot(hidden, head.T, preferred_element_type=jnp.float32) * lax.rsqrt(final_sumsq / D + epsilon)
    top = lax.optimization_barrier(jnp.max(logits, axis=1))
    total = lax.optimization_barrier(jnp.sum(jnp.exp(logits - top[:, None]), axis=1))
    flat_targets = targets.reshape(-1).astype(jnp.int32)
    chosen = jnp.take_along_axis(logits, flat_targets[:, None], axis=1)[:, 0]
    token_loss = (top + jnp.log(total) - chosen).reshape(MICRO, MB)
    mean_loss = jnp.mean(token_loss).reshape(1)
    return (token_loss, mean_loss)
```

```python
import functools

import jax
import jax.numpy as jnp
from jax import lax
from jax.experimental import pallas as pl
from jax.experimental.pallas import tpu as pltpu
from jax.sharding import PartitionSpec as P

BLK = 64
PAIR = 2 * BLK
HALF = BLK // 2

epsilon = 1e-05
MESH = pl.DeviceIdType.MESH


def shifted(block, axis, distance):
    devices = range(lax.axis_size(axis))
    route = [(i - distance, i) for i in devices if i - distance in devices]
    return lax.ppermute(block, axis, route)


def slot_index(mask, slot_count):
    band_rows, block_count = mask.shape
    kept = (mask > 0).astype(jnp.float32)
    upper = (jnp.arange(block_count)[:, None] <= jnp.arange(block_count)[None, :]).astype(jnp.float32)
    within = jnp.dot(kept, upper)
    lower = (jnp.arange(band_rows)[:, None] > jnp.arange(band_rows)[None, :]).astype(jnp.float32)
    before = jnp.dot(lower, within[:, -1:])
    running = (within + before).astype(jnp.int32)
    slots = jnp.clip(running - 1, 0, slot_count - 1)
    return jnp.where(mask > 0, slots, -1), before[:, 0].astype(jnp.int32)


def build_body(block_count, index_ref, start_ref, window_ref, panel_ref):
    row = pl.program_id(0)
    start = start_ref[row]
    low = lax.broadcasted_iota(jnp.int32, (HALF, PAIR), 1) < BLK

    def picked(column):
        slot = index_ref[row * block_count + column]
        near = jnp.clip(slot - start, 0, window_ref.shape[0] - 1)
        keep = jnp.where(slot >= 0, 1.0, 0.0).astype(jnp.float32)
        factor = jnp.full((HALF, PAIR), keep, jnp.float32).astype(jnp.bfloat16)
        block = window_ref[near] * factor
        return block, jnp.concatenate([block[:, BLK:], block[:, :BLK]], axis=1)

    for pair in range(block_count // 2):
        left, left_turned = picked(2 * pair)
        right, right_turned = picked(2 * pair + 1)
        lanes = slice(pair * PAIR, (pair + 1) * PAIR)
        panel_ref[:HALF, lanes] = jnp.where(low, left, right_turned)
        panel_ref[HALF:, lanes] = jnp.where(low, left_turned, right)


def build_panel(mask, values):
    band_rows, block_count = mask.shape
    slot_count = values.shape[0]
    index, before = slot_index(mask, slot_count)
    window = min(block_count, slot_count)
    starts = jnp.clip(before, 0, slot_count - window)
    lists = values.reshape(slot_count, HALF, PAIR)
    spec = pltpu.PrefetchScalarGridSpec(
        num_scalar_prefetch=2,
        grid=(band_rows,),
        in_specs=[
            pl.BlockSpec(
                (pl.Element(window), pl.Element(HALF), pl.Element(PAIR)),
                lambda r, index_ref, start_ref: (start_ref[r], 0, 0),
            )
        ],
        out_specs=pl.BlockSpec((BLK, block_count * BLK), lambda r, *_: (r, 0)),
    )
    return pl.pallas_call(
        functools.partial(build_body, block_count),
        grid_spec=spec,
        out_shape=jax.ShapeDtypeStruct((band_rows * BLK, block_count * BLK), jnp.bfloat16),
        compiler_params=pltpu.CompilerParams(
            dimension_semantics=("arbitrary",), vmem_limit_bytes=40 << 20
        ),
    )(index.reshape(-1), starts, lists)


SUBS = 2
HEAD_SLOTS = 8


def chain_kernel(
    tensors, inputs_ref, gains_ref, targets_ref, panel_ref, head_ref, out_ref,
    panel, heads, lhs, turn, hidden, sums, outgoing, relayed, arrived, residual, ahead, gathered, squares, total,
    square_out, square_in, stats_out, stats_in,
    panel_sem, head_sem, part_send, part_recv, relay_send, relay_recv, rest_send, rest_recv, square_send, square_recv,
    ahead_send, ahead_recv, own_send, cross_send, core_send, gather_recv, stats_send, stats_recv,
):
    sections = 4
    rows, width = inputs_ref.shape
    pieces, _, piece = panel.shape
    full = width * tensors
    vocab_rows = head_ref.shape[0]
    z = lax.axis_index("tensor")
    q = lax.axis_index("section")
    column = q // 2
    core = q % 2

    def remote(src, dst, send, recv, t, s):
        return pltpu.make_async_remote_copy(
            src_ref=src, dst_ref=dst, send_sem=send, recv_sem=recv,
            device_id={"tensor": t, "section": s}, device_id_type=MESH,
        )

    def piece_at(t, half, sub):
        return (t * 2 + half) * SUBS + sub

    def out_order(j):
        sub, rest = j // (2 * tensors), j % (2 * tensors)
        return (z + 2 + rest // 2) % tensors, rest % 2, sub

    def in_order(j):
        sub, rest = j // (2 * tensors), j % (2 * tensors)
        half = jnp.where(rest < tensors, column, 1 - column)
        return (z + rest) % tensors, half, sub

    def panel_copy(j):
        t, half, sub = out_order(j)
        at = piece_at(t, half, sub)
        return pltpu.make_async_copy(
            panel_ref.at[:, pl.ds(pl.multiple_of(at * piece, piece), piece)], panel.at[at], panel_sem.at[at]
        )

    def head_copy(j):
        t, half, sub = in_order(j)
        at = piece_at(t, half, sub)
        slot = j % HEAD_SLOTS
        return pltpu.make_async_copy(
            head_ref.at[:, pl.ds(pl.multiple_of(at * piece, piece), piece)], heads.at[slot], head_sem.at[slot]
        )

    @pl.loop(0, pieces)
    def _(j):
        panel_copy(j).start()

    @pl.loop(0, HEAD_SLOTS)
    def _(j):
        head_copy(j).start()

    barrier = pltpu.get_barrier_semaphore()
    me = z * sections + q
    everyone = tensors * sections

    @pl.loop(1, everyone)
    def _(k):
        other = (me + k) % everyone
        pl.semaphore_signal(
            barrier, inc=1, device_id={"tensor": other // sections, "section": other % sections},
            device_id_type=MESH,
        )

    wide_row = lax.broadcasted_iota(jnp.int32, turn.shape, 0)
    wide_lane = lax.broadcasted_iota(jnp.int32, turn.shape, 1)
    inside = wide_lane % BLK
    comes_from = wide_lane - inside + 2 * (inside % HALF) + inside // HALF
    turn[...] = jnp.where(wide_row == comes_from, 1.0, 0.0).astype(jnp.bfloat16)
    total[...] = jnp.zeros_like(total)
    squares[...] = jnp.zeros_like(squares)

    @pl.when(q == 0)
    def _():
        for k in range(2 * SUBS):
            hidden[k] = inputs_ref[:, k * piece : (k + 1) * piece]

    pl.semaphore_wait(barrier, everyone - 1)

    def lane_sums(value):
        folded = value[:, :128]
        for k in range(1, value.shape[1] // 128):
            folded += value[:, k * 128 : (k + 1) * 128]
        return folded

    def summing(s, half):
        return jnp.where(s % 2 == 0, s + 1, half * 2), jnp.where(s % 2 == 0, half, s // 2)

    def source(s):
        @pl.when(s == 2)
        def _():
            for sub in range(SUBS):
                remote(ahead.at[sub], hidden.at[sub], ahead_send.at[sub], ahead_recv.at[sub], z, q).wait_recv()

        for half in range(2):
            target, slot = summing(s, half)
            remote(
                hidden.at[pl.ds(half * SUBS, SUBS)], residual.at[slot], rest_send.at[half], rest_recv.at[slot], z, target
            ).start()
        folded = jnp.zeros((rows, 128), jnp.float32)
        for k in range(2 * SUBS):
            wide = hidden[k].astype(jnp.float32)
            folded += lane_sums(wide * wide)
            gain = gains_ref[:, pl.ds(pl.multiple_of(z * width + k * piece, piece), piece)].astype(jnp.float32)
            scaled = (wide * gain).astype(jnp.bfloat16)
            for b in range(piece // 256):
                turned = jnp.dot(
                    scaled[:, b * 256 : (b + 1) * 256], turn[...], preferred_element_type=jnp.float32
                )
                lhs[:, k * piece + b * 256 : k * piece + (b + 1) * 256] = turned.astype(jnp.bfloat16)
        row = jnp.sum(folded.T, axis=0, keepdims=True)
        square_out[...] = jnp.broadcast_to(row, square_out.shape)

        @pl.loop(0, 2 * tensors)
        def _(j):
            @pl.when(jnp.logical_or(s % 2 == 1, j < tensors))
            def _():
                remote(
                    square_out, square_in.at[s // 2, z], square_send.at[j], square_recv.at[s // 2, z],
                    j % tensors, summing(s, j // tensors)[0],
                ).start()

        @pl.loop(0, pieces)
        def _(j):
            t, half, sub = out_order(j)
            at = piece_at(t, half, sub)
            panel_copy(j).wait()
            part = jnp.dot(lhs[...], panel[at], preferred_element_type=jnp.float32)
            outgoing[at] = (part * jnp.abs(part)).astype(jnp.bfloat16)
            straight = jnp.logical_or(t == z, half == column)

            @pl.when(straight)
            def _():
                target, slot = summing(s, half)
                remote(
                    outgoing.at[at], arrived.at[slot, z, sub], part_send.at[at], part_recv.at[slot, z, sub], t, target
                ).start()

            @pl.when(jnp.logical_not(straight))
            def _():
                by = t * SUBS + sub
                remote(
                    outgoing.at[at], relayed.at[s % 2, by], part_send.at[at], relay_recv.at[s % 2, by],
                    z, (1 - column) * 2 + 1,
                ).start()

    def relay(s):
        @pl.loop(0, tensors * SUBS)
        def _(j):
            t, sub = (z + 2 + j % tensors) % tensors, j // tensors
            by = t * SUBS + sub

            @pl.when(t != z)
            def _():
                remote(
                    relayed.at[s % 2, by], relayed.at[s % 2, by], relay_send.at[s % 2, by], relay_recv.at[s % 2, by], z, q
                ).wait_recv()
                target, slot = summing(s, column)
                remote(
                    relayed.at[s % 2, by], arrived.at[slot, z, sub], relay_send.at[s % 2, by],
                    part_recv.at[slot, z, sub], t, target,
                ).start()

    def reduce_half(s, half):
        slot = summing(s, half)[1]
        is_final = s == sections - 1
        remote(
            residual.at[slot], residual.at[slot], rest_send.at[0], rest_recv.at[slot], z, q
        ).wait_recv()
        for sub in range(SUBS):
            for t in range(tensors):
                remote(
                    outgoing.at[0], arrived.at[slot, t, sub], part_send.at[0], part_recv.at[slot, t, sub], z, q
                ).wait_recv()
            for b in range(piece // 128):
                lanes = slice(b * 128, (b + 1) * 128)
                product = jnp.zeros((rows, 128), jnp.float32)
                for t in range(tensors):
                    coded = arrived[slot, t, sub, :, lanes].astype(jnp.float32)
                    product += coded * lax.rsqrt(jnp.maximum(jnp.abs(coded), 1e-37))
                wide = residual[slot, sub, :, lanes].astype(jnp.float32)
                ahead[sub, :, lanes] = (wide + product * sums[...]).astype(jnp.bfloat16)

            @pl.when(q == s + 1)
            def _():
                hidden[half * SUBS + sub] = ahead[sub]

            @pl.when(jnp.logical_and(q == 0, s == 1))
            def _():
                remote(
                    ahead.at[sub], hidden.at[half * SUBS + sub], ahead_send.at[sub], ahead_recv.at[sub], z, 2
                ).start()

            @pl.when(is_final)
            def _():
                at = piece_at(z, column, sub)
                gathered[at] = ahead[sub]
                for k in range(1, tensors):
                    remote(
                        gathered.at[at], gathered.at[at], own_send.at[sub, k], gather_recv.at[at], (z + k) % tensors, q
                    ).start()
                remote(
                    gathered.at[at], gathered.at[at], cross_send.at[at], gather_recv.at[at], z, (q + 2) % sections
                ).start()
                remote(
                    gathered.at[at], gathered.at[at], core_send.at[at], gather_recv.at[at], z, column * 2 + 1
                ).start()

    def reducer(s):
        row = jnp.zeros(square_out.shape, jnp.float32)
        for t in range(tensors):
            remote(
                square_out, square_in.at[s // 2, t], square_send.at[0], square_recv.at[s // 2, t], z, q
            ).wait_recv()
            row += square_in[s // 2, t]
        scale = lax.rsqrt(row / full + epsilon)
        sums[...] = jnp.concatenate([scale] * (rows // 8), axis=0).T

        @pl.when(jnp.logical_and(s == 3, q == 0))
        def _():
            for sub in range(SUBS):
                remote(ahead.at[sub], hidden.at[sub], ahead_send.at[sub], ahead_recv.at[sub], z, 2).wait_send()

        @pl.loop(0, 2)
        def _(half):
            @pl.when(jnp.logical_or(s % 2 == 0, half == column))
            def _():
                reduce_half(s, half)

    @pl.loop(0, sections)
    def _(s):
        @pl.when(q == s)
        def _():
            source(s)

        @pl.when(q == 3 - 2 * (s // 2))
        def _():
            relay(s)

        @pl.when(jnp.where(s % 2 == 0, q == s + 1, core == 0))
        def _():
            reducer(s)

    @pl.loop(0, pieces)
    def _(j):
        t, half, sub = in_order(j)
        at = piece_at(t, half, sub)
        rest = j % (2 * tensors)

        def come(send):
            return remote(gathered.at[at], gathered.at[at], send, gather_recv.at[at], z, column * 2 + 1)

        @pl.when(jnp.logical_or(core == 1, rest > 0))
        def _():
            come(core_send.at[at]).wait_recv()

        @pl.when(jnp.logical_and(core == 0, rest > 0))
        def _():
            come(core_send.at[at]).start()

            @pl.when(rest < tensors)
            def _():
                remote(
                    gathered.at[at], gathered.at[at], cross_send.at[at], gather_recv.at[at], z, (q + 2) % sections
                ).start()

        head_copy(j).wait()
        mine = gathered[at]
        total[...] += lax.dot_general(
            heads[j % HEAD_SLOTS], mine, (((1,), (1,)), ((), ())), preferred_element_type=jnp.float32
        )
        wide = mine.astype(jnp.float32)
        squares[...] += lane_sums(wide * wide)

        @pl.when(j + HEAD_SLOTS < pieces)
        def _():
            head_copy(j + HEAD_SLOTS).start()

    final = jnp.sum(squares[...].T, axis=0, keepdims=True)
    scale = lax.rsqrt(final / full + epsilon)
    logits = total[...] * scale
    top = jnp.max(logits, axis=0, keepdims=True)
    count = jnp.sum(jnp.exp(logits - top), axis=0, keepdims=True)
    ids = lax.broadcasted_iota(jnp.int32, logits.shape, 0) + me * vocab_rows
    chosen = jnp.sum(jnp.where(ids == targets_ref[...], logits, 0.0), axis=0, keepdims=True)
    stats_out[...] = jnp.concatenate([top, count, chosen, jnp.zeros((5, rows), jnp.float32)], axis=0)

    @pl.loop(1, everyone)
    def _(k):
        other = (me + k) % everyone
        remote(
            stats_out, stats_in.at[me], stats_send.at[k], stats_recv.at[me], other // sections, other % sections
        ).start()

    stats_in[me] = stats_out[...]

    @pl.loop(1, everyone)
    def _(k):
        other = (me + k) % everyone
        remote(stats_out, stats_in.at[other], stats_send.at[k], stats_recv.at[other], z, q).wait_recv()

    highest = stats_in[0]
    for k in range(1, everyone):
        highest = jnp.maximum(highest, stats_in[k])
    highest = highest[0:1]
    exps = jnp.zeros((1, rows), jnp.float32)
    hit = jnp.zeros((1, rows), jnp.float32)
    for k in range(everyone):
        stat = stats_in[k]
        exps += stat[1:2] * jnp.exp(stat[0:1] - highest)
        hit += stat[2:3]
    loss = highest + jnp.log(exps) - hit
    mean = jnp.sum(loss, axis=1, keepdims=True) / rows
    out_ref[...] = jnp.concatenate(
        [loss, jnp.broadcast_to(mean, (1, rows)), jnp.zeros((6, rows), jnp.float32)], axis=0
    )

    @pl.loop(0, pieces)
    def _(j):
        remote(outgoing.at[j], arrived.at[0, 0, 0], part_send.at[j], part_recv.at[0, 0, 0], z, q).wait_send()

    @pl.loop(0, 2 * tensors)
    def _(j):
        @pl.when(jnp.logical_or(core == 1, j < tensors))
        def _():
            remote(square_out, square_in.at[0, 0], square_send.at[j], square_recv.at[0, 0], z, q).wait_send()

    for half in range(2):
        remote(
            hidden.at[pl.ds(half * SUBS, SUBS)], residual.at[0], rest_send.at[half], rest_recv.at[0], z, q
        ).wait_send()

    @pl.when(core == 1)
    def _():
        @pl.loop(0, 2 * tensors * SUBS)
        def _(j):
            kind, by = j // (tensors * SUBS), j % (tensors * SUBS)

            @pl.when(by // SUBS != z)
            def _():
                remote(
                    relayed.at[kind, by], relayed.at[kind, by], relay_send.at[kind, by], relay_recv.at[kind, by], z, q
                ).wait_send()

    @pl.when(core == 0)
    def _():
        for sub in range(SUBS):
            for k in range(1, tensors):
                remote(
                    gathered.at[0], gathered.at[0], own_send.at[sub, k], gather_recv.at[0], z, q
                ).wait_send()

        @pl.loop(0, pieces)
        def _(j):
            remote(gathered.at[j], gathered.at[j], core_send.at[j], gather_recv.at[j], z, q).wait_send()

        @pl.loop(0, tensors * SUBS)
        def _(j):
            at = piece_at(j // SUBS, column, j % SUBS)
            remote(gathered.at[at], gathered.at[at], cross_send.at[at], gather_recv.at[at], z, q).wait_send()

    @pl.loop(1, everyone)
    def _(k):
        remote(stats_out, stats_in.at[0], stats_send.at[k], stats_recv.at[0], z, q).wait_send()


def chain(inputs, gains, targets, panel, head):
    tensors = lax.axis_size("tensor")
    rows, width = inputs.shape
    piece = width // (2 * SUBS)
    pieces = 2 * SUBS * tensors
    everyone = tensors * lax.axis_size("section")
    vocab_rows = head.shape[0]
    half16, single = jnp.bfloat16, jnp.float32
    dma = pltpu.SemaphoreType.DMA
    vmem = pl.BlockSpec(memory_space=pltpu.VMEM)
    anywhere = pl.BlockSpec(memory_space=pl.ANY)
    out = pl.pallas_call(
        functools.partial(chain_kernel, tensors),
        out_shape=jax.ShapeDtypeStruct((8, rows), single),
        in_specs=[vmem, vmem, vmem, anywhere, anywhere],
        out_specs=vmem,
        scratch_shapes=[
            pltpu.VMEM((pieces, width, piece), half16),
            pltpu.VMEM((HEAD_SLOTS, vocab_rows, piece), half16),
            pltpu.VMEM((rows, width), half16),
            pltpu.VMEM((256, 256), half16),
            pltpu.VMEM((2 * SUBS, rows, piece), half16),
            pltpu.VMEM((rows, 128), single),
            pltpu.VMEM((pieces, rows, piece), half16),
            pltpu.VMEM((2, tensors * SUBS, rows, piece), half16),
            pltpu.VMEM((2, tensors, SUBS, rows, piece), half16),
            pltpu.VMEM((2, SUBS, rows, piece), half16),
            pltpu.VMEM((SUBS, rows, piece), half16),
            pltpu.VMEM((pieces, rows, piece), half16),
            pltpu.VMEM((rows, 128), single),
            pltpu.VMEM((vocab_rows, rows), single),
            pltpu.VMEM((8, rows), single),
            pltpu.VMEM((2, tensors, 8, rows), single),
            pltpu.VMEM((8, rows), single),
            pltpu.VMEM((everyone, 8, rows), single),
            dma((pieces,)),
            dma((HEAD_SLOTS,)),
            dma((pieces,)),
            dma((2, tensors, SUBS)),
            dma((2, tensors * SUBS)),
            dma((2, tensors * SUBS)),
            dma((2,)),
            dma((2,)),
            dma((2 * tensors,)),
            dma((2, tensors)),
            dma((SUBS,)),
            dma((SUBS,)),
            dma((SUBS, tensors)),
            dma((pieces,)),
            dma((pieces,)),
            dma((pieces,)),
            dma((everyone,)),
            dma((everyone,)),
        ],
        compiler_params=pltpu.CompilerParams(
            collective_id=0, has_side_effects=True, vmem_limit_bytes=62 << 20
        ),
    )(inputs, gains, targets, panel, head)
    return out[0], out[1, :1]


def joined_loss(logits_top, total, chosen):
    stacked = jnp.stack([logits_top, total, chosen])
    everything = lax.all_gather(stacked, ("tensor", "section"))
    tops = everything[:, 0]
    top = jnp.max(tops, axis=0)
    total = jnp.sum(everything[:, 1] * jnp.exp(tops - top[None, :]), axis=0)
    return top + jnp.log(total) - jnp.sum(everything[:, 2], axis=0)


def general(inputs, gains, panel, head, targets):
    section_count = lax.axis_size("section")
    tensor_index = lax.axis_index("tensor")
    section_index = lax.axis_index("section")
    rows, local_width = inputs.shape
    full = panel.shape[1]
    gain = lax.dynamic_slice(gains, (tensor_index * local_width,), (local_width,))
    gain = gain.astype(jnp.float32)
    incoming = inputs
    for moment in range(section_count):
        current = jnp.where(section_index == 0, inputs, incoming) if moment else inputs
        wide = current.astype(jnp.float32)
        sumsq = lax.psum(jnp.sum(wide * wide, axis=1), "tensor")
        scaled = (wide * gain).astype(jnp.bfloat16)
        turned = scaled.reshape(rows, local_width // BLK, HALF, 2).transpose(0, 1, 3, 2)
        partial = jnp.dot(turned.reshape(rows, local_width), panel, preferred_element_type=jnp.float32)
        product = lax.psum_scatter(partial, "tensor", scatter_dimension=1, tiled=True)
        update = product * lax.rsqrt(sumsq[:, None] / full + epsilon)
        outgoing = (wide + update).astype(jnp.bfloat16)
        if moment < section_count - 1:
            incoming = shifted(outgoing, "section", 1)
    vocab_rows = head.shape[0]
    final = jnp.where(section_index == section_count - 1, outgoing, jnp.zeros_like(outgoing))
    relayed = lax.psum(final, "section")
    portion = lax.all_gather(relayed, "tensor", axis=1, tiled=True)
    raw_logits = lax.dot_general(
        portion, head, (((1,), (1,)), ((), ())), preferred_element_type=jnp.float32
    )
    widened = portion.astype(jnp.float32)
    final_sumsq = jnp.sum(widened * widened, axis=1)
    logits = raw_logits * lax.rsqrt(final_sumsq[:, None] / full + epsilon)
    vocab_start = (tensor_index * section_count + section_index) * vocab_rows
    local_ids = targets - vocab_start
    matches = jnp.arange(vocab_rows, dtype=jnp.int32)[None, :] == local_ids[:, None]
    target_logit = jnp.sum(jnp.where(matches, logits, 0.0), axis=1)
    local_top = jnp.max(logits, axis=1)
    local_total = jnp.sum(jnp.exp(logits - local_top[:, None]), axis=1)
    losses = joined_loss(local_top, local_total, target_logit)
    return losses, jnp.mean(losses).reshape(1)


def on_device(inputs, gains, keep_mask, block_values, head, targets):
    micro_count, row_count, width = inputs.shape
    rows = micro_count * row_count
    own = inputs.reshape(rows, width)
    ids = targets.reshape(rows)
    panel = build_panel(keep_mask[0], block_values[0])
    paired = lax.axis_size("section") == 4 and rows == 128 and width % 1024 == 0 and head.shape[0] % 16 == 0
    if paired:
        losses, mean_loss = chain(own, gains, ids.reshape(1, rows), panel, head)
    else:
        losses, mean_loss = general(own, gains[0], panel, head, ids)
    return losses.reshape(micro_count, row_count), mean_loss


def solution(mesh):
    placed = (
        P("groups", None, "tensor"),
        P("section", None),
        P("section", "tensor", None),
        P("section", "tensor", None),
        P(("tensor", "section"), None),
        P("groups", None),
    )
    return jax.shard_map(
        on_device,
        mesh=mesh,
        in_specs=placed,
        out_specs=(P("groups", None), P("groups")),
        check_vma=False,
    )
```

```python
import functools

import jax
import jax.numpy as jnp
from jax import lax
from jax.experimental import pallas as pl
from jax.experimental.pallas import tpu as pltpu
from jax.sharding import PartitionSpec as P

BLK = 64
PAIR = 2 * BLK
HALF = BLK // 2

epsilon = 1e-05
MESH = pl.DeviceIdType.MESH


def shifted(block, axis, distance):
    devices = range(lax.axis_size(axis))
    route = [(i - distance, i) for i in devices if i - distance in devices]
    return lax.ppermute(block, axis, route)


def slot_index(mask, slot_count):
    band_rows, block_count = mask.shape
    kept = (mask > 0).astype(jnp.float32)
    upper = (jnp.arange(block_count)[:, None] <= jnp.arange(block_count)[None, :]).astype(jnp.float32)
    within = jnp.dot(kept, upper)
    lower = (jnp.arange(band_rows)[:, None] > jnp.arange(band_rows)[None, :]).astype(jnp.float32)
    running = within + jnp.dot(lower, within[:, -1:])
    slots = jnp.clip(running.astype(jnp.int32) - 1, 0, slot_count - 1)
    return jnp.where(mask > 0, slots, slot_count)


def build_body(chunks, index_ref, values_ref, panel_ref, listed):
    step = pl.program_id(0)
    chunk = values_ref.shape[0]
    slot_count = chunks * chunk
    block_count = panel_ref.shape[1] // BLK
    band = panel_ref.shape[0] // BLK

    @pl.when(step == 0)
    def _():
        listed[slot_count] = jnp.zeros((HALF, PAIR), jnp.bfloat16)

    @pl.when(step < chunks)
    def _():
        groups = chunk // 16

        @pl.loop(0, groups, unroll=4 if groups % 4 == 0 else 1)
        def _(group):
            at = pl.multiple_of(group * 16, 16)
            parts = [values_ref[pl.ds(at, 16), m * PAIR : (m + 1) * PAIR] for m in range(HALF)]
            listed[pl.ds(step * chunk + at, 16)] = jnp.transpose(jnp.stack(parts, axis=0), (1, 0, 2))

    @pl.when(step >= chunks)
    def _():
        low = lax.broadcasted_iota(jnp.int32, (HALF, PAIR), 1) < BLK

        def turned(block):
            return jnp.concatenate([block[:, BLK:], block[:, :BLK]], axis=1)

        @pl.loop(0, band)
        def _(row):
            first = ((step - chunks) * band + row) * block_count
            top = pl.multiple_of(row * BLK, BLK)
            for pair in range(block_count // 2):
                left = listed[index_ref[first + 2 * pair]]
                right = listed[index_ref[first + 2 * pair + 1]]
                lanes = slice(pair * PAIR, (pair + 1) * PAIR)
                panel_ref[pl.ds(top, HALF), lanes] = jnp.where(low, left, turned(right))
                panel_ref[pl.ds(top + HALF, HALF), lanes] = jnp.where(low, turned(left), right)


def build_panel(mask, values):
    band_rows, block_count = mask.shape
    slot_count, size = values.shape
    index = slot_index(mask, slot_count)
    chunk = next(c for c in (512, 192, 64, 32, 16) if slot_count % c == 0)
    chunks = slot_count // chunk
    band = 4 if band_rows % 4 == 0 else 1
    spec = pltpu.PrefetchScalarGridSpec(
        num_scalar_prefetch=1,
        grid=(chunks + band_rows // band,),
        in_specs=[pl.BlockSpec((chunk, size), lambda i, *_: (jnp.minimum(i, chunks - 1), 0))],
        out_specs=pl.BlockSpec((band * BLK, block_count * BLK), lambda i, *_: (jnp.maximum(i - chunks, 0), 0)),
        scratch_shapes=[pltpu.VMEM((slot_count + 1, HALF, PAIR), jnp.bfloat16)],
    )
    return pl.pallas_call(
        functools.partial(build_body, chunks),
        grid_spec=spec,
        out_shape=jax.ShapeDtypeStruct((band_rows * BLK, block_count * BLK), jnp.bfloat16),
        compiler_params=pltpu.CompilerParams(
            dimension_semantics=("arbitrary",), vmem_limit_bytes=50 << 20
        ),
    )(index.reshape(-1), values)


SPREAD = 1024.0


def coded(part):
    wide = part * SPREAD
    wide = wide * jnp.abs(wide)
    return (wide * jnp.abs(wide)).astype(jnp.bfloat16)


def decoded(code):
    wide = code.astype(jnp.float32)
    size = jnp.maximum(jnp.abs(wide), 1e-37)
    once = lax.rsqrt(size)
    return wide * once * lax.rsqrt(size * once)


SUBS = 2
HEAD_SLOTS = 8


def chain_kernel(
    tensors, inputs_ref, gains_ref, targets_ref, panel_ref, head_ref, out_ref,
    panel, heads, lhs, turn, hidden, sums, outgoing, relayed, arrived, residual, ahead, gathered, squares, total,
    square_out, square_in, stats_out, stats_in,
    panel_sem, head_sem, part_send, part_recv, relay_send, relay_recv, rest_send, rest_recv, square_send, square_recv,
    ahead_send, ahead_recv, own_send, cross_send, core_send, gather_recv, stats_send, stats_recv,
):
    sections = 4
    rows, width = inputs_ref.shape
    pieces, _, piece = panel.shape
    full = width * tensors
    vocab_rows = head_ref.shape[0]
    z = lax.axis_index("tensor")
    q = lax.axis_index("section")
    column = q // 2
    core = q % 2

    def remote(src, dst, send, recv, t, s):
        return pltpu.make_async_remote_copy(
            src_ref=src, dst_ref=dst, send_sem=send, recv_sem=recv,
            device_id={"tensor": t, "section": s}, device_id_type=MESH,
        )

    def piece_at(t, half, sub):
        return (t * 2 + half) * SUBS + sub

    def out_order(j):
        sub, rest = j // (2 * tensors), j % (2 * tensors)
        return (z + 2 + rest // 2) % tensors, rest % 2, sub

    def in_order(j):
        sub, rest = j // (2 * tensors), j % (2 * tensors)
        half = jnp.where(rest < tensors, column, 1 - column)
        return (z + rest) % tensors, half, sub

    def panel_copy(j):
        t, half, sub = out_order(j)
        at = piece_at(t, half, sub)
        return pltpu.make_async_copy(
            panel_ref.at[:, pl.ds(pl.multiple_of(at * piece, piece), piece)], panel.at[at], panel_sem.at[at]
        )

    def head_copy(j):
        t, half, sub = in_order(j)
        at = piece_at(t, half, sub)
        slot = j % HEAD_SLOTS
        return pltpu.make_async_copy(
            head_ref.at[:, pl.ds(pl.multiple_of(at * piece, piece), piece)], heads.at[slot], head_sem.at[slot]
        )

    @pl.loop(0, pieces)
    def _(j):
        panel_copy(j).start()

    @pl.loop(0, HEAD_SLOTS)
    def _(j):
        head_copy(j).start()

    barrier = pltpu.get_barrier_semaphore()
    me = z * sections + q
    everyone = tensors * sections

    @pl.loop(1, everyone)
    def _(k):
        other = (me + k) % everyone
        pl.semaphore_signal(
            barrier, inc=1, device_id={"tensor": other // sections, "section": other % sections},
            device_id_type=MESH,
        )

    wide_row = lax.broadcasted_iota(jnp.int32, turn.shape, 0)
    wide_lane = lax.broadcasted_iota(jnp.int32, turn.shape, 1)
    inside = wide_lane % BLK
    comes_from = wide_lane - inside + 2 * (inside % HALF) + inside // HALF
    turn[...] = jnp.where(wide_row == comes_from, 1.0, 0.0).astype(jnp.bfloat16)
    total[...] = jnp.zeros_like(total)
    squares[...] = jnp.zeros_like(squares)

    @pl.when(q == 0)
    def _():
        for k in range(2 * SUBS):
            hidden[k] = inputs_ref[:, k * piece : (k + 1) * piece]

    pl.semaphore_wait(barrier, everyone - 1)

    def lane_sums(value):
        folded = value[:, :128]
        for k in range(1, value.shape[1] // 128):
            folded += value[:, k * 128 : (k + 1) * 128]
        return folded

    def summing(s, half):
        return jnp.where(s % 2 == 0, s + 1, half * 2), jnp.where(s % 2 == 0, half, s // 2)

    def source(s):
        @pl.when(s == 2)
        def _():
            for sub in range(SUBS):
                remote(ahead.at[sub], hidden.at[sub], ahead_send.at[sub], ahead_recv.at[sub], z, q).wait_recv()

        for half in range(2):
            target, slot = summing(s, half)
            remote(
                hidden.at[pl.ds(half * SUBS, SUBS)], residual.at[slot], rest_send.at[half], rest_recv.at[slot], z, target
            ).start()
        folded = jnp.zeros((rows, 128), jnp.float32)
        for k in range(2 * SUBS):
            wide = hidden[k].astype(jnp.float32)
            folded += lane_sums(wide * wide)
            gain = gains_ref[:, pl.ds(pl.multiple_of(z * width + k * piece, piece), piece)].astype(jnp.float32)
            scaled = (wide * gain).astype(jnp.bfloat16)
            for b in range(piece // 256):
                turned = jnp.dot(
                    scaled[:, b * 256 : (b + 1) * 256], turn[...], preferred_element_type=jnp.float32
                )
                lhs[:, k * piece + b * 256 : k * piece + (b + 1) * 256] = turned.astype(jnp.bfloat16)
        row = jnp.sum(folded.T, axis=0, keepdims=True)
        square_out[...] = jnp.broadcast_to(row, square_out.shape)

        @pl.loop(0, 2 * tensors)
        def _(j):
            @pl.when(jnp.logical_or(s % 2 == 1, j < tensors))
            def _():
                remote(
                    square_out, square_in.at[s // 2, z], square_send.at[j], square_recv.at[s // 2, z],
                    j % tensors, summing(s, j // tensors)[0],
                ).start()

        @pl.loop(0, pieces)
        def _(j):
            t, half, sub = out_order(j)
            at = piece_at(t, half, sub)
            panel_copy(j).wait()
            part = jnp.dot(lhs[...], panel[at], preferred_element_type=jnp.float32)
            outgoing[at] = coded(part)
            straight = jnp.logical_or(t == z, half == column)

            @pl.when(straight)
            def _():
                target, slot = summing(s, half)
                remote(
                    outgoing.at[at], arrived.at[slot, z, sub], part_send.at[at], part_recv.at[slot, z, sub], t, target
                ).start()

            @pl.when(jnp.logical_not(straight))
            def _():
                by = t * SUBS + sub
                remote(
                    outgoing.at[at], relayed.at[s % 2, by], part_send.at[at], relay_recv.at[s % 2, by],
                    z, (1 - column) * 2 + 1,
                ).start()

    def relay(s):
        @pl.loop(0, tensors * SUBS)
        def _(j):
            t, sub = (z + 2 + j % tensors) % tensors, j // tensors
            by = t * SUBS + sub

            @pl.when(t != z)
            def _():
                remote(
                    relayed.at[s % 2, by], relayed.at[s % 2, by], relay_send.at[s % 2, by], relay_recv.at[s % 2, by], z, q
                ).wait_recv()
                target, slot = summing(s, column)
                remote(
                    relayed.at[s % 2, by], arrived.at[slot, z, sub], relay_send.at[s % 2, by],
                    part_recv.at[slot, z, sub], t, target,
                ).start()

    def reduce_half(s, half):
        slot = summing(s, half)[1]
        is_final = s == sections - 1
        remote(
            residual.at[slot], residual.at[slot], rest_send.at[0], rest_recv.at[slot], z, q
        ).wait_recv()
        for sub in range(SUBS):
            for t in range(tensors):
                remote(
                    outgoing.at[0], arrived.at[slot, t, sub], part_send.at[0], part_recv.at[slot, t, sub], z, q
                ).wait_recv()
            for b in range(piece // 128):
                lanes = slice(b * 128, (b + 1) * 128)
                product = jnp.zeros((rows, 128), jnp.float32)
                for t in range(tensors):
                    product += decoded(arrived[slot, t, sub, :, lanes])
                wide = residual[slot, sub, :, lanes].astype(jnp.float32)
                ahead[sub, :, lanes] = (wide + product * sums[...]).astype(jnp.bfloat16)

            @pl.when(q == s + 1)
            def _():
                hidden[half * SUBS + sub] = ahead[sub]

            @pl.when(jnp.logical_and(q == 0, s == 1))
            def _():
                remote(
                    ahead.at[sub], hidden.at[half * SUBS + sub], ahead_send.at[sub], ahead_recv.at[sub], z, 2
                ).start()

            @pl.when(is_final)
            def _():
                at = piece_at(z, column, sub)
                gathered[at] = ahead[sub]
                for k in range(1, tensors):
                    remote(
                        gathered.at[at], gathered.at[at], own_send.at[sub, k], gather_recv.at[at], (z + k) % tensors, q
                    ).start()
                remote(
                    gathered.at[at], gathered.at[at], cross_send.at[at], gather_recv.at[at], z, (q + 2) % sections
                ).start()
                remote(
                    gathered.at[at], gathered.at[at], core_send.at[at], gather_recv.at[at], z, column * 2 + 1
                ).start()

    def reducer(s):
        row = jnp.zeros(square_out.shape, jnp.float32)
        for t in range(tensors):
            remote(
                square_out, square_in.at[s // 2, t], square_send.at[0], square_recv.at[s // 2, t], z, q
            ).wait_recv()
            row += square_in[s // 2, t]
        scale = lax.rsqrt(row / full + epsilon) / SPREAD
        sums[...] = jnp.concatenate([scale] * (rows // 8), axis=0).T

        @pl.when(jnp.logical_and(s == 3, q == 0))
        def _():
            for sub in range(SUBS):
                remote(ahead.at[sub], hidden.at[sub], ahead_send.at[sub], ahead_recv.at[sub], z, 2).wait_send()

        @pl.loop(0, 2)
        def _(half):
            @pl.when(jnp.logical_or(s % 2 == 0, half == column))
            def _():
                reduce_half(s, half)

    @pl.loop(0, sections)
    def _(s):
        @pl.when(q == s)
        def _():
            source(s)

        @pl.when(q == 3 - 2 * (s // 2))
        def _():
            relay(s)

        @pl.when(jnp.where(s % 2 == 0, q == s + 1, core == 0))
        def _():
            reducer(s)

    @pl.loop(0, pieces)
    def _(j):
        t, half, sub = in_order(j)
        at = piece_at(t, half, sub)
        rest = j % (2 * tensors)

        def come(send):
            return remote(gathered.at[at], gathered.at[at], send, gather_recv.at[at], z, column * 2 + 1)

        @pl.when(jnp.logical_or(core == 1, rest > 0))
        def _():
            come(core_send.at[at]).wait_recv()

        @pl.when(jnp.logical_and(core == 0, rest > 0))
        def _():
            come(core_send.at[at]).start()

            @pl.when(rest < tensors)
            def _():
                remote(
                    gathered.at[at], gathered.at[at], cross_send.at[at], gather_recv.at[at], z, (q + 2) % sections
                ).start()

        head_copy(j).wait()
        mine = gathered[at]
        total[...] += lax.dot_general(
            heads[j % HEAD_SLOTS], mine, (((1,), (1,)), ((), ())), preferred_element_type=jnp.float32
        )
        wide = mine.astype(jnp.float32)
        squares[...] += lane_sums(wide * wide)

        @pl.when(j + HEAD_SLOTS < pieces)
        def _():
            head_copy(j + HEAD_SLOTS).start()

    final = jnp.sum(squares[...].T, axis=0, keepdims=True)
    scale = lax.rsqrt(final / full + epsilon)
    logits = total[...] * scale
    top = jnp.max(logits, axis=0, keepdims=True)
    count = jnp.sum(jnp.exp(logits - top), axis=0, keepdims=True)
    ids = lax.broadcasted_iota(jnp.int32, logits.shape, 0) + me * vocab_rows
    chosen = jnp.sum(jnp.where(ids == targets_ref[...], logits, 0.0), axis=0, keepdims=True)
    stats_out[...] = jnp.concatenate([top, count, chosen, jnp.zeros((5, rows), jnp.float32)], axis=0)

    @pl.loop(1, everyone)
    def _(k):
        other = (me + k) % everyone
        remote(
            stats_out, stats_in.at[me], stats_send.at[k], stats_recv.at[me], other // sections, other % sections
        ).start()

    stats_in[me] = stats_out[...]

    @pl.loop(1, everyone)
    def _(k):
        other = (me + k) % everyone
        remote(stats_out, stats_in.at[other], stats_send.at[k], stats_recv.at[other], z, q).wait_recv()

    highest = stats_in[0]
    for k in range(1, everyone):
        highest = jnp.maximum(highest, stats_in[k])
    highest = highest[0:1]
    exps = jnp.zeros((1, rows), jnp.float32)
    hit = jnp.zeros((1, rows), jnp.float32)
    for k in range(everyone):
        stat = stats_in[k]
        exps += stat[1:2] * jnp.exp(stat[0:1] - highest)
        hit += stat[2:3]
    loss = highest + jnp.log(exps) - hit
    mean = jnp.sum(loss, axis=1, keepdims=True) / rows
    out_ref[...] = jnp.concatenate(
        [loss, jnp.broadcast_to(mean, (1, rows)), jnp.zeros((6, rows), jnp.float32)], axis=0
    )

    @pl.loop(0, pieces)
    def _(j):
        remote(outgoing.at[j], arrived.at[0, 0, 0], part_send.at[j], part_recv.at[0, 0, 0], z, q).wait_send()

    @pl.loop(0, 2 * tensors)
    def _(j):
        @pl.when(jnp.logical_or(core == 1, j < tensors))
        def _():
            remote(square_out, square_in.at[0, 0], square_send.at[j], square_recv.at[0, 0], z, q).wait_send()

    for half in range(2):
        remote(
            hidden.at[pl.ds(half * SUBS, SUBS)], residual.at[0], rest_send.at[half], rest_recv.at[0], z, q
        ).wait_send()

    @pl.when(core == 1)
    def _():
        @pl.loop(0, 2 * tensors * SUBS)
        def _(j):
            kind, by = j // (tensors * SUBS), j % (tensors * SUBS)

            @pl.when(by // SUBS != z)
            def _():
                remote(
                    relayed.at[kind, by], relayed.at[kind, by], relay_send.at[kind, by], relay_recv.at[kind, by], z, q
                ).wait_send()

    @pl.when(core == 0)
    def _():
        for sub in range(SUBS):
            for k in range(1, tensors):
                remote(
                    gathered.at[0], gathered.at[0], own_send.at[sub, k], gather_recv.at[0], z, q
                ).wait_send()

        @pl.loop(0, pieces)
        def _(j):
            remote(gathered.at[j], gathered.at[j], core_send.at[j], gather_recv.at[j], z, q).wait_send()

        @pl.loop(0, tensors * SUBS)
        def _(j):
            at = piece_at(j // SUBS, column, j % SUBS)
            remote(gathered.at[at], gathered.at[at], cross_send.at[at], gather_recv.at[at], z, q).wait_send()

    @pl.loop(1, everyone)
    def _(k):
        remote(stats_out, stats_in.at[0], stats_send.at[k], stats_recv.at[0], z, q).wait_send()


def chain(inputs, gains, targets, panel, head):
    tensors = lax.axis_size("tensor")
    rows, width = inputs.shape
    piece = width // (2 * SUBS)
    pieces = 2 * SUBS * tensors
    everyone = tensors * lax.axis_size("section")
    vocab_rows = head.shape[0]
    half16, single = jnp.bfloat16, jnp.float32
    dma = pltpu.SemaphoreType.DMA
    vmem = pl.BlockSpec(memory_space=pltpu.VMEM)
    anywhere = pl.BlockSpec(memory_space=pl.ANY)
    out = pl.pallas_call(
        functools.partial(chain_kernel, tensors),
        out_shape=jax.ShapeDtypeStruct((8, rows), single),
        in_specs=[vmem, vmem, vmem, anywhere, anywhere],
        out_specs=vmem,
        scratch_shapes=[
            pltpu.VMEM((pieces, width, piece), half16),
            pltpu.VMEM((HEAD_SLOTS, vocab_rows, piece), half16),
            pltpu.VMEM((rows, width), half16),
            pltpu.VMEM((256, 256), half16),
            pltpu.VMEM((2 * SUBS, rows, piece), half16),
            pltpu.VMEM((rows, 128), single),
            pltpu.VMEM((pieces, rows, piece), half16),
            pltpu.VMEM((2, tensors * SUBS, rows, piece), half16),
            pltpu.VMEM((2, tensors, SUBS, rows, piece), half16),
            pltpu.VMEM((2, SUBS, rows, piece), half16),
            pltpu.VMEM((SUBS, rows, piece), half16),
            pltpu.VMEM((pieces, rows, piece), half16),
            pltpu.VMEM((rows, 128), single),
            pltpu.VMEM((vocab_rows, rows), single),
            pltpu.VMEM((8, rows), single),
            pltpu.VMEM((2, tensors, 8, rows), single),
            pltpu.VMEM((8, rows), single),
            pltpu.VMEM((everyone, 8, rows), single),
            dma((pieces,)),
            dma((HEAD_SLOTS,)),
            dma((pieces,)),
            dma((2, tensors, SUBS)),
            dma((2, tensors * SUBS)),
            dma((2, tensors * SUBS)),
            dma((2,)),
            dma((2,)),
            dma((2 * tensors,)),
            dma((2, tensors)),
            dma((SUBS,)),
            dma((SUBS,)),
            dma((SUBS, tensors)),
            dma((pieces,)),
            dma((pieces,)),
            dma((pieces,)),
            dma((everyone,)),
            dma((everyone,)),
        ],
        compiler_params=pltpu.CompilerParams(
            collective_id=0, has_side_effects=True, vmem_limit_bytes=62 << 20
        ),
    )(inputs, gains, targets, panel, head)
    return out[0], out[1, :1]


def joined_loss(logits_top, total, chosen):
    stacked = jnp.stack([logits_top, total, chosen])
    everything = lax.all_gather(stacked, ("tensor", "section"))
    tops = everything[:, 0]
    top = jnp.max(tops, axis=0)
    total = jnp.sum(everything[:, 1] * jnp.exp(tops - top[None, :]), axis=0)
    return top + jnp.log(total) - jnp.sum(everything[:, 2], axis=0)


def general(inputs, gains, panel, head, targets):
    section_count = lax.axis_size("section")
    tensor_index = lax.axis_index("tensor")
    section_index = lax.axis_index("section")
    rows, local_width = inputs.shape
    full = panel.shape[1]
    gain = lax.dynamic_slice(gains, (tensor_index * local_width,), (local_width,))
    gain = gain.astype(jnp.float32)
    incoming = inputs
    for moment in range(section_count):
        current = jnp.where(section_index == 0, inputs, incoming) if moment else inputs
        wide = current.astype(jnp.float32)
        sumsq = lax.psum(jnp.sum(wide * wide, axis=1), "tensor")
        scaled = (wide * gain).astype(jnp.bfloat16)
        turned = scaled.reshape(rows, local_width // BLK, HALF, 2).transpose(0, 1, 3, 2)
        partial = jnp.dot(turned.reshape(rows, local_width), panel, preferred_element_type=jnp.float32)
        product = lax.psum_scatter(partial, "tensor", scatter_dimension=1, tiled=True)
        update = product * lax.rsqrt(sumsq[:, None] / full + epsilon)
        outgoing = (wide + update).astype(jnp.bfloat16)
        if moment < section_count - 1:
            incoming = shifted(outgoing, "section", 1)
    vocab_rows = head.shape[0]
    final = jnp.where(section_index == section_count - 1, outgoing, jnp.zeros_like(outgoing))
    relayed = lax.psum(final, "section")
    portion = lax.all_gather(relayed, "tensor", axis=1, tiled=True)
    raw_logits = lax.dot_general(
        portion, head, (((1,), (1,)), ((), ())), preferred_element_type=jnp.float32
    )
    widened = portion.astype(jnp.float32)
    final_sumsq = jnp.sum(widened * widened, axis=1)
    logits = raw_logits * lax.rsqrt(final_sumsq[:, None] / full + epsilon)
    vocab_start = (tensor_index * section_count + section_index) * vocab_rows
    local_ids = targets - vocab_start
    matches = jnp.arange(vocab_rows, dtype=jnp.int32)[None, :] == local_ids[:, None]
    target_logit = jnp.sum(jnp.where(matches, logits, 0.0), axis=1)
    local_top = jnp.max(logits, axis=1)
    local_total = jnp.sum(jnp.exp(logits - local_top[:, None]), axis=1)
    losses = joined_loss(local_top, local_total, target_logit)
    return losses, jnp.mean(losses).reshape(1)


def on_device(inputs, gains, keep_mask, block_values, head, targets):
    micro_count, row_count, width = inputs.shape
    rows = micro_count * row_count
    own = inputs.reshape(rows, width)
    ids = targets.reshape(rows)
    panel = build_panel(keep_mask[0], block_values[0])
    paired = lax.axis_size("section") == 4 and rows == 128 and width % 1024 == 0 and head.shape[0] % 16 == 0
    if paired:
        losses, mean_loss = chain(own, gains, ids.reshape(1, rows), panel, head)
    else:
        losses, mean_loss = general(own, gains[0], panel, head, ids)
    return losses.reshape(micro_count, row_count), mean_loss


def solution(mesh):
    placed = (
        P("groups", None, "tensor"),
        P("section", None),
        P("section", "tensor", None),
        P("section", "tensor", None),
        P(("tensor", "section"), None),
        P("groups", None),
    )
    return jax.shard_map(
        on_device,
        mesh=mesh,
        in_specs=placed,
        out_specs=(P("groups", None), P("groups")),
        check_vma=False,
    )
```

```python
import functools

import jax
import jax.numpy as jnp
from jax import lax
from jax.experimental import pallas as pl
from jax.experimental.pallas import tpu as pltpu
from jax.sharding import PartitionSpec as P

BLK = 64
PAIR = 2 * BLK
HALF = BLK // 2

epsilon = 1e-05
MESH = pl.DeviceIdType.MESH


def shifted(block, axis, distance):
    devices = range(lax.axis_size(axis))
    route = [(i - distance, i) for i in devices if i - distance in devices]
    return lax.ppermute(block, axis, route)


def slot_index(mask, slot_count):
    band_rows, block_count = mask.shape
    kept = (mask > 0).astype(jnp.float32)
    upper = (jnp.arange(block_count)[:, None] <= jnp.arange(block_count)[None, :]).astype(jnp.float32)
    within = jnp.dot(kept, upper)
    lower = (jnp.arange(band_rows)[:, None] > jnp.arange(band_rows)[None, :]).astype(jnp.float32)
    running = within + jnp.dot(lower, within[:, -1:])
    slots = jnp.clip(running.astype(jnp.int32) - 1, 0, slot_count - 1)
    return jnp.where(mask > 0, slots, slot_count)


def build_body(chunks, index_ref, values_ref, panel_ref, listed):
    step = pl.program_id(0)
    chunk = values_ref.shape[0]
    slot_count = chunks * chunk
    block_count = panel_ref.shape[1] // BLK
    band = panel_ref.shape[0] // BLK

    @pl.when(step == 0)
    def _():
        listed[slot_count] = jnp.zeros((HALF, PAIR), jnp.bfloat16)

    @pl.when(step < chunks)
    def _():
        groups = chunk // 16

        @pl.loop(0, groups, unroll=4 if groups % 4 == 0 else 1)
        def _(group):
            at = pl.multiple_of(group * 16, 16)
            parts = [values_ref[pl.ds(at, 16), m * PAIR : (m + 1) * PAIR] for m in range(HALF)]
            listed[pl.ds(step * chunk + at, 16)] = jnp.transpose(jnp.stack(parts, axis=0), (1, 0, 2))

    @pl.when(step >= chunks)
    def _():
        low = lax.broadcasted_iota(jnp.int32, (HALF, PAIR), 1) < BLK

        def turned(block):
            return jnp.concatenate([block[:, BLK:], block[:, :BLK]], axis=1)

        @pl.loop(0, band)
        def _(row):
            first = ((step - chunks) * band + row) * block_count
            top = pl.multiple_of(row * BLK, BLK)
            for pair in range(block_count // 2):
                left = listed[index_ref[first + 2 * pair]]
                right = listed[index_ref[first + 2 * pair + 1]]
                lanes = slice(pair * PAIR, (pair + 1) * PAIR)
                panel_ref[pl.ds(top, HALF), lanes] = jnp.where(low, left, turned(right))
                panel_ref[pl.ds(top + HALF, HALF), lanes] = jnp.where(low, turned(left), right)


def build_panel(mask, values):
    band_rows, block_count = mask.shape
    slot_count, size = values.shape
    index = slot_index(mask, slot_count)
    chunk = next(c for c in (512, 192, 64, 32, 16) if slot_count % c == 0)
    chunks = slot_count // chunk
    band = 4 if band_rows % 4 == 0 else 1
    spec = pltpu.PrefetchScalarGridSpec(
        num_scalar_prefetch=1,
        grid=(chunks + band_rows // band,),
        in_specs=[pl.BlockSpec((chunk, size), lambda i, *_: (jnp.minimum(i, chunks - 1), 0))],
        out_specs=pl.BlockSpec((band * BLK, block_count * BLK), lambda i, *_: (jnp.maximum(i - chunks, 0), 0)),
        scratch_shapes=[pltpu.VMEM((slot_count + 1, HALF, PAIR), jnp.bfloat16)],
    )
    return pl.pallas_call(
        functools.partial(build_body, chunks),
        grid_spec=spec,
        out_shape=jax.ShapeDtypeStruct((band_rows * BLK, block_count * BLK), jnp.bfloat16),
        compiler_params=pltpu.CompilerParams(
            dimension_semantics=("arbitrary",), vmem_limit_bytes=50 << 20
        ),
    )(index.reshape(-1), values)


SPREAD = 1024.0


def coded(part):
    wide = part * SPREAD
    wide = wide * jnp.abs(wide)
    return (wide * jnp.abs(wide)).astype(jnp.bfloat16)


def decoded(code):
    wide = code.astype(jnp.float32)
    size = jnp.maximum(jnp.abs(wide), 1e-37)
    once = lax.rsqrt(size)
    return wide * once * lax.rsqrt(size * once)


SUBS = 2
SLOTS = 12


def chain_kernel(
    tensors, index_ref, inputs_ref, gains_ref, targets_ref, values_ref, head_ref, out_ref,
    panel, listed, lhs, turn, hidden, sums, outgoing, relayed, arrived, residual, ahead, gathered, squares, total,
    square_out, square_in, stats_out, stats_in,
    panel_sem, head_sem, part_send, part_recv, relay_send, relay_recv, rest_send, rest_recv, square_send, square_recv,
    ahead_send, ahead_recv, own_send, cross_send, core_send, gather_recv, stats_send, stats_recv,
):
    sections = 4
    rows, width = inputs_ref.shape
    piece = panel.shape[2]
    pieces = width * tensors // piece
    slot_count, size = values_ref.shape
    per = width * piece // size
    stages = slot_count // per
    block_count = index_ref.shape[0] * BLK // width
    full = width * tensors
    vocab_rows = head_ref.shape[0]
    z = lax.axis_index("tensor")
    q = lax.axis_index("section")
    column = q // 2
    core = q % 2

    def remote(src, dst, send, recv, t, s):
        return pltpu.make_async_remote_copy(
            src_ref=src, dst_ref=dst, send_sem=send, recv_sem=recv,
            device_id={"tensor": t, "section": s}, device_id_type=MESH,
        )

    def piece_at(t, half, sub):
        return (t * 2 + half) * SUBS + sub

    def out_order(j):
        sub, rest = j // (2 * tensors), j % (2 * tensors)
        return (z + 2 + rest // 2) % tensors, rest % 2, sub

    def in_order(j):
        sub, rest = j // (2 * tensors), j % (2 * tensors)
        half = jnp.where(rest < tensors, column, 1 - column)
        return (z + rest) % tensors, half, sub

    def build(j):
        t, half, sub = out_order(j)
        low = lax.broadcasted_iota(jnp.int32, (HALF, PAIR), 1) < BLK
        first = piece_at(t, half, sub) * (piece // BLK)

        def turned(block):
            return jnp.concatenate([block[:, BLK:], block[:, :BLK]], axis=1)

        @pl.loop(0, width // BLK, unroll=4)
        def _(row):
            top = pl.multiple_of(row * BLK, BLK)
            for pair in range(piece // PAIR):
                left = listed[index_ref[row * block_count + first + 2 * pair]]
                right = listed[index_ref[row * block_count + first + 2 * pair + 1]]
                lanes = slice(pair * PAIR, (pair + 1) * PAIR)
                panel[j % SLOTS, pl.ds(top, HALF), lanes] = jnp.where(low, left, turned(right))
                panel[j % SLOTS, pl.ds(top + HALF, HALF), lanes] = jnp.where(low, turned(left), right)

    def prebuild():
        @pl.loop(0, SLOTS)
        def _(j):
            build(j)

    def head_copy(j):
        t, half, sub = in_order(j)
        at = piece_at(t, half, sub)
        return pltpu.make_async_copy(
            head_ref.at[:, pl.ds(pl.multiple_of(at * piece, piece), piece)],
            panel.at[j % SLOTS, pl.ds(0, vocab_rows)], head_sem.at[j % SLOTS],
        )

    cuts = size // piece

    @pl.loop(0, stages * cuts)
    def _(k):
        stage, cut = k // cuts, k % cuts
        pltpu.make_async_copy(
            values_ref.at[pl.ds(pl.multiple_of(stage * per, per), per), pl.ds(pl.multiple_of(cut * piece, piece), piece)],
            panel.at[stage, pl.ds(pl.multiple_of(cut * per, per), per)], panel_sem.at[stage],
        ).start()

    barrier = pltpu.get_barrier_semaphore()
    me = z * sections + q
    everyone = tensors * sections

    @pl.loop(1, everyone)
    def _(k):
        other = (me + k) % everyone
        pl.semaphore_signal(
            barrier, inc=1, device_id={"tensor": other // sections, "section": other % sections},
            device_id_type=MESH,
        )

    wide_row = lax.broadcasted_iota(jnp.int32, turn.shape, 0)
    wide_lane = lax.broadcasted_iota(jnp.int32, turn.shape, 1)
    inside = wide_lane % BLK
    comes_from = wide_lane - inside + 2 * (inside % HALF) + inside // HALF
    turn[...] = jnp.where(wide_row == comes_from, 1.0, 0.0).astype(jnp.bfloat16)
    total[...] = jnp.zeros_like(total)
    squares[...] = jnp.zeros_like(squares)

    @pl.when(q == 0)
    def _():
        for k in range(2 * SUBS):
            hidden[k] = inputs_ref[:, k * piece : (k + 1) * piece]

    listed[slot_count] = jnp.zeros((HALF, PAIR), jnp.bfloat16)

    @pl.loop(0, stages)
    def _(stage):
        pltpu.make_async_copy(panel.at[stage], panel.at[stage], panel_sem.at[stage]).wait()

        @pl.loop(0, per // 16, unroll=4)
        def _(group):
            at = pl.multiple_of(group * 16, 16)
            parts = []
            for m in range(HALF):
                cut, lane = m * PAIR // piece, m * PAIR % piece
                parts.append(panel[stage, pl.ds(cut * per + at, 16), lane : lane + PAIR])
            listed[pl.ds(stage * per + at, 16)] = jnp.transpose(jnp.stack(parts, axis=0), (1, 0, 2))

    @pl.when(jnp.logical_or(q == 1, q == 2))
    def _():
        prebuild()

    pl.semaphore_wait(barrier, everyone - 1)

    def lane_sums(value):
        folded = value[:, :128]
        for k in range(1, value.shape[1] // 128):
            folded += value[:, k * 128 : (k + 1) * 128]
        return folded

    def summing(s, half):
        return jnp.where(s % 2 == 0, s + 1, half * 2), jnp.where(s % 2 == 0, half, s // 2)

    def source(s):
        @pl.when(s == 2)
        def _():
            for sub in range(SUBS):
                remote(ahead.at[sub], hidden.at[sub], ahead_send.at[sub], ahead_recv.at[sub], z, q).wait_recv()

        for half in range(2):
            target, slot = summing(s, half)
            remote(
                hidden.at[pl.ds(half * SUBS, SUBS)], residual.at[slot], rest_send.at[half], rest_recv.at[slot], z, target
            ).start()
        folded = jnp.zeros((rows, 128), jnp.float32)
        for k in range(2 * SUBS):
            wide = hidden[k].astype(jnp.float32)
            folded += lane_sums(wide * wide)
            gain = gains_ref[:, pl.ds(pl.multiple_of(z * width + k * piece, piece), piece)].astype(jnp.float32)
            scaled = (wide * gain).astype(jnp.bfloat16)
            for b in range(piece // 256):
                turned = jnp.dot(
                    scaled[:, b * 256 : (b + 1) * 256], turn[...], preferred_element_type=jnp.float32
                )
                lhs[:, k * piece + b * 256 : k * piece + (b + 1) * 256] = turned.astype(jnp.bfloat16)
        row = jnp.sum(folded.T, axis=0, keepdims=True)
        square_out[...] = jnp.broadcast_to(row, square_out.shape)

        @pl.loop(0, 2 * tensors)
        def _(j):
            @pl.when(jnp.logical_or(s % 2 == 1, j < tensors))
            def _():
                remote(
                    square_out, square_in.at[s // 2, z], square_send.at[j], square_recv.at[s // 2, z],
                    j % tensors, summing(s, j // tensors)[0],
                ).start()

        @pl.loop(0, pieces)
        def _(j):
            t, half, sub = out_order(j)
            at = piece_at(t, half, sub)

            @pl.when(jnp.logical_or(s == 0, j >= SLOTS))
            def _():
                build(j)

            part = jnp.dot(lhs[...], panel[j % SLOTS], preferred_element_type=jnp.float32)
            outgoing[at] = coded(part)
            straight = jnp.logical_or(t == z, half == column)

            @pl.when(straight)
            def _():
                target, slot = summing(s, half)
                remote(
                    outgoing.at[at], arrived.at[slot, z, sub], part_send.at[at], part_recv.at[slot, z, sub], t, target
                ).start()

            @pl.when(jnp.logical_not(straight))
            def _():
                by = t * SUBS + sub
                remote(
                    outgoing.at[at], relayed.at[s % 2, by], part_send.at[at], relay_recv.at[s % 2, by],
                    z, (1 - column) * 2 + 1,
                ).start()

        @pl.loop(0, SLOTS)
        def _(j):
            head_copy(j).start()

    def relay(s):
        @pl.loop(0, tensors * SUBS)
        def _(j):
            t, sub = (z + 2 + j % tensors) % tensors, j // tensors
            by = t * SUBS + sub

            @pl.when(t != z)
            def _():
                remote(
                    relayed.at[s % 2, by], relayed.at[s % 2, by], relay_send.at[s % 2, by], relay_recv.at[s % 2, by], z, q
                ).wait_recv()
                target, slot = summing(s, column)
                remote(
                    relayed.at[s % 2, by], arrived.at[slot, z, sub], relay_send.at[s % 2, by],
                    part_recv.at[slot, z, sub], t, target,
                ).start()

    def reduce_half(s, half):
        slot = summing(s, half)[1]
        is_final = s == sections - 1
        remote(
            residual.at[slot], residual.at[slot], rest_send.at[0], rest_recv.at[slot], z, q
        ).wait_recv()
        for sub in range(SUBS):
            for t in range(tensors):
                remote(
                    outgoing.at[0], arrived.at[slot, t, sub], part_send.at[0], part_recv.at[slot, t, sub], z, q
                ).wait_recv()
            for b in range(piece // 128):
                lanes = slice(b * 128, (b + 1) * 128)
                product = jnp.zeros((rows, 128), jnp.float32)
                for t in range(tensors):
                    product += decoded(arrived[slot, t, sub, :, lanes])
                wide = residual[slot, sub, :, lanes].astype(jnp.float32)
                ahead[sub, :, lanes] = (wide + product * sums[...]).astype(jnp.bfloat16)

            @pl.when(q == s + 1)
            def _():
                hidden[half * SUBS + sub] = ahead[sub]

            @pl.when(jnp.logical_and(q == 0, s == 1))
            def _():
                remote(
                    ahead.at[sub], hidden.at[half * SUBS + sub], ahead_send.at[sub], ahead_recv.at[sub], z, 2
                ).start()

            @pl.when(is_final)
            def _():
                at = piece_at(z, column, sub)
                gathered[at] = ahead[sub]
                for k in range(1, tensors):
                    remote(
                        gathered.at[at], gathered.at[at], own_send.at[sub, k], gather_recv.at[at], (z + k) % tensors, q
                    ).start()
                remote(
                    gathered.at[at], gathered.at[at], cross_send.at[at], gather_recv.at[at], z, (q + 2) % sections
                ).start()
                remote(
                    gathered.at[at], gathered.at[at], core_send.at[at], gather_recv.at[at], z, column * 2 + 1
                ).start()

    def reducer(s):
        row = jnp.zeros(square_out.shape, jnp.float32)
        for t in range(tensors):
            remote(
                square_out, square_in.at[s // 2, t], square_send.at[0], square_recv.at[s // 2, t], z, q
            ).wait_recv()
            row += square_in[s // 2, t]
        scale = lax.rsqrt(row / full + epsilon) / SPREAD
        sums[...] = jnp.concatenate([scale] * (rows // 8), axis=0).T

        @pl.when(jnp.logical_and(s == 3, q == 0))
        def _():
            for sub in range(SUBS):
                remote(ahead.at[sub], hidden.at[sub], ahead_send.at[sub], ahead_recv.at[sub], z, 2).wait_send()

        @pl.loop(0, 2)
        def _(half):
            @pl.when(jnp.logical_or(s % 2 == 0, half == column))
            def _():
                reduce_half(s, half)

    @pl.loop(0, sections)
    def _(s):
        @pl.when(q == s)
        def _():
            source(s)

        @pl.when(q == 3 - 2 * (s // 2))
        def _():
            relay(s)

        @pl.when(jnp.logical_and(q == 3, s == 1))
        def _():
            prebuild()

        @pl.when(jnp.where(s % 2 == 0, q == s + 1, core == 0))
        def _():
            reducer(s)

    @pl.loop(0, pieces)
    def _(j):
        t, half, sub = in_order(j)
        at = piece_at(t, half, sub)
        rest = j % (2 * tensors)

        def come(send):
            return remote(gathered.at[at], gathered.at[at], send, gather_recv.at[at], z, column * 2 + 1)

        @pl.when(jnp.logical_or(core == 1, rest > 0))
        def _():
            come(core_send.at[at]).wait_recv()

        @pl.when(jnp.logical_and(core == 0, rest > 0))
        def _():
            come(core_send.at[at]).start()

            @pl.when(rest < tensors)
            def _():
                remote(
                    gathered.at[at], gathered.at[at], cross_send.at[at], gather_recv.at[at], z, (q + 2) % sections
                ).start()

        head_copy(j).wait()
        mine = gathered[at]
        total[...] += lax.dot_general(
            panel[j % SLOTS, :vocab_rows], mine, (((1,), (1,)), ((), ())), preferred_element_type=jnp.float32
        )
        wide = mine.astype(jnp.float32)
        squares[...] += lane_sums(wide * wide)

        @pl.when(j + SLOTS < pieces)
        def _():
            head_copy(j + SLOTS).start()

    final = jnp.sum(squares[...].T, axis=0, keepdims=True)
    scale = lax.rsqrt(final / full + epsilon)
    logits = total[...] * scale
    top = jnp.max(logits, axis=0, keepdims=True)
    count = jnp.sum(jnp.exp(logits - top), axis=0, keepdims=True)
    ids = lax.broadcasted_iota(jnp.int32, logits.shape, 0) + me * vocab_rows
    chosen = jnp.sum(jnp.where(ids == targets_ref[...], logits, 0.0), axis=0, keepdims=True)
    stats_out[...] = jnp.concatenate([top, count, chosen, jnp.zeros((5, rows), jnp.float32)], axis=0)

    @pl.loop(1, everyone)
    def _(k):
        other = (me + k) % everyone
        remote(
            stats_out, stats_in.at[me], stats_send.at[k], stats_recv.at[me], other // sections, other % sections
        ).start()

    stats_in[me] = stats_out[...]

    @pl.loop(1, everyone)
    def _(k):
        other = (me + k) % everyone
        remote(stats_out, stats_in.at[other], stats_send.at[k], stats_recv.at[other], z, q).wait_recv()

    highest = stats_in[0]
    for k in range(1, everyone):
        highest = jnp.maximum(highest, stats_in[k])
    highest = highest[0:1]
    exps = jnp.zeros((1, rows), jnp.float32)
    hit = jnp.zeros((1, rows), jnp.float32)
    for k in range(everyone):
        stat = stats_in[k]
        exps += stat[1:2] * jnp.exp(stat[0:1] - highest)
        hit += stat[2:3]
    loss = highest + jnp.log(exps) - hit
    mean = jnp.sum(loss, axis=1, keepdims=True) / rows
    out_ref[...] = jnp.concatenate(
        [loss, jnp.broadcast_to(mean, (1, rows)), jnp.zeros((6, rows), jnp.float32)], axis=0
    )

    @pl.loop(0, pieces)
    def _(j):
        remote(outgoing.at[j], arrived.at[0, 0, 0], part_send.at[j], part_recv.at[0, 0, 0], z, q).wait_send()

    @pl.loop(0, 2 * tensors)
    def _(j):
        @pl.when(jnp.logical_or(core == 1, j < tensors))
        def _():
            remote(square_out, square_in.at[0, 0], square_send.at[j], square_recv.at[0, 0], z, q).wait_send()

    for half in range(2):
        remote(
            hidden.at[pl.ds(half * SUBS, SUBS)], residual.at[0], rest_send.at[half], rest_recv.at[0], z, q
        ).wait_send()

    @pl.when(core == 1)
    def _():
        @pl.loop(0, 2 * tensors * SUBS)
        def _(j):
            kind, by = j // (tensors * SUBS), j % (tensors * SUBS)

            @pl.when(by // SUBS != z)
            def _():
                remote(
                    relayed.at[kind, by], relayed.at[kind, by], relay_send.at[kind, by], relay_recv.at[kind, by], z, q
                ).wait_send()

    @pl.when(core == 0)
    def _():
        for sub in range(SUBS):
            for k in range(1, tensors):
                remote(
                    gathered.at[0], gathered.at[0], own_send.at[sub, k], gather_recv.at[0], z, q
                ).wait_send()

        @pl.loop(0, pieces)
        def _(j):
            remote(gathered.at[j], gathered.at[j], core_send.at[j], gather_recv.at[j], z, q).wait_send()

        @pl.loop(0, tensors * SUBS)
        def _(j):
            at = piece_at(j // SUBS, column, j % SUBS)
            remote(gathered.at[at], gathered.at[at], cross_send.at[at], gather_recv.at[at], z, q).wait_send()

    @pl.loop(1, everyone)
    def _(k):
        remote(stats_out, stats_in.at[0], stats_send.at[k], stats_recv.at[0], z, q).wait_send()


def chain(index, inputs, gains, targets, values, head):
    tensors = lax.axis_size("tensor")
    rows, width = inputs.shape
    piece = width // (2 * SUBS)
    pieces = 2 * SUBS * tensors
    everyone = tensors * lax.axis_size("section")
    vocab_rows = head.shape[0]
    half16, single = jnp.bfloat16, jnp.float32
    dma = pltpu.SemaphoreType.DMA
    vmem = pl.BlockSpec(memory_space=pltpu.VMEM)
    anywhere = pl.BlockSpec(memory_space=pl.ANY)
    out = pl.pallas_call(
        functools.partial(chain_kernel, tensors),
        out_shape=jax.ShapeDtypeStruct((8, rows), single),
        in_specs=[pl.BlockSpec(memory_space=pltpu.SMEM), vmem, vmem, vmem, anywhere, anywhere],
        out_specs=vmem,
        scratch_shapes=[
            pltpu.VMEM((SLOTS, width, piece), half16),
            pltpu.VMEM((values.shape[0] + 16, HALF, PAIR), half16),
            pltpu.VMEM((rows, width), half16),
            pltpu.VMEM((256, 256), half16),
            pltpu.VMEM((2 * SUBS, rows, piece), half16),
            pltpu.VMEM((rows, 128), single),
            pltpu.VMEM((pieces, rows, piece), half16),
            pltpu.VMEM((2, tensors * SUBS, rows, piece), half16),
            pltpu.VMEM((2, tensors, SUBS, rows, piece), half16),
            pltpu.VMEM((2, SUBS, rows, piece), half16),
            pltpu.VMEM((SUBS, rows, piece), half16),
            pltpu.VMEM((pieces, rows, piece), half16),
            pltpu.VMEM((rows, 128), single),
            pltpu.VMEM((vocab_rows, rows), single),
            pltpu.VMEM((8, rows), single),
            pltpu.VMEM((2, tensors, 8, rows), single),
            pltpu.VMEM((8, rows), single),
            pltpu.VMEM((everyone, 8, rows), single),
            dma((SLOTS,)),
            dma((SLOTS,)),
            dma((pieces,)),
            dma((2, tensors, SUBS)),
            dma((2, tensors * SUBS)),
            dma((2, tensors * SUBS)),
            dma((2,)),
            dma((2,)),
            dma((2 * tensors,)),
            dma((2, tensors)),
            dma((SUBS,)),
            dma((SUBS,)),
            dma((SUBS, tensors)),
            dma((pieces,)),
            dma((pieces,)),
            dma((pieces,)),
            dma((everyone,)),
            dma((everyone,)),
        ],
        compiler_params=pltpu.CompilerParams(
            collective_id=0, has_side_effects=True, vmem_limit_bytes=62 << 20
        ),
    )(index, inputs, gains, targets, values, head)
    return out[0], out[1, :1]


def joined_loss(logits_top, total, chosen):
    stacked = jnp.stack([logits_top, total, chosen])
    everything = lax.all_gather(stacked, ("tensor", "section"))
    tops = everything[:, 0]
    top = jnp.max(tops, axis=0)
    total = jnp.sum(everything[:, 1] * jnp.exp(tops - top[None, :]), axis=0)
    return top + jnp.log(total) - jnp.sum(everything[:, 2], axis=0)


def general(inputs, gains, panel, head, targets):
    section_count = lax.axis_size("section")
    tensor_index = lax.axis_index("tensor")
    section_index = lax.axis_index("section")
    rows, local_width = inputs.shape
    full = panel.shape[1]
    gain = lax.dynamic_slice(gains, (tensor_index * local_width,), (local_width,))
    gain = gain.astype(jnp.float32)
    incoming = inputs
    for moment in range(section_count):
        current = jnp.where(section_index == 0, inputs, incoming) if moment else inputs
        wide = current.astype(jnp.float32)
        sumsq = lax.psum(jnp.sum(wide * wide, axis=1), "tensor")
        scaled = (wide * gain).astype(jnp.bfloat16)
        turned = scaled.reshape(rows, local_width // BLK, HALF, 2).transpose(0, 1, 3, 2)
        partial = jnp.dot(turned.reshape(rows, local_width), panel, preferred_element_type=jnp.float32)
        product = lax.psum_scatter(partial, "tensor", scatter_dimension=1, tiled=True)
        update = product * lax.rsqrt(sumsq[:, None] / full + epsilon)
        outgoing = (wide + update).astype(jnp.bfloat16)
        if moment < section_count - 1:
            incoming = shifted(outgoing, "section", 1)
    vocab_rows = head.shape[0]
    final = jnp.where(section_index == section_count - 1, outgoing, jnp.zeros_like(outgoing))
    relayed = lax.psum(final, "section")
    portion = lax.all_gather(relayed, "tensor", axis=1, tiled=True)
    raw_logits = lax.dot_general(
        portion, head, (((1,), (1,)), ((), ())), preferred_element_type=jnp.float32
    )
    widened = portion.astype(jnp.float32)
    final_sumsq = jnp.sum(widened * widened, axis=1)
    logits = raw_logits * lax.rsqrt(final_sumsq[:, None] / full + epsilon)
    vocab_start = (tensor_index * section_count + section_index) * vocab_rows
    local_ids = targets - vocab_start
    matches = jnp.arange(vocab_rows, dtype=jnp.int32)[None, :] == local_ids[:, None]
    target_logit = jnp.sum(jnp.where(matches, logits, 0.0), axis=1)
    local_top = jnp.max(logits, axis=1)
    local_total = jnp.sum(jnp.exp(logits - local_top[:, None]), axis=1)
    losses = joined_loss(local_top, local_total, target_logit)
    return losses, jnp.mean(losses).reshape(1)


def on_device(inputs, gains, keep_mask, block_values, head, targets):
    micro_count, row_count, width = inputs.shape
    rows = micro_count * row_count
    own = inputs.reshape(rows, width)
    ids = targets.reshape(rows)
    mask, values = keep_mask[0], block_values[0]
    piece = width // (2 * SUBS)
    fits = lax.axis_size("section") == 4 and rows == 128 and piece % 256 == 0 and head.shape[0] <= width
    if fits and head.shape[0] % 16 == 0 and values.shape[0] * values.shape[1] == SLOTS * width * piece:
        index = slot_index(mask, values.shape[0]).reshape(-1)
        losses, mean_loss = chain(index, own, gains, ids.reshape(1, rows), values, head)
    else:
        losses, mean_loss = general(own, gains[0], build_panel(mask, values), head, ids)
    return losses.reshape(micro_count, row_count), mean_loss


def solution(mesh):
    placed = (
        P("groups", None, "tensor"),
        P("section", None),
        P("section", "tensor", None),
        P("section", "tensor", None),
        P(("tensor", "section"), None),
        P("groups", None),
    )
    return jax.shard_map(
        on_device,
        mesh=mesh,
        in_specs=placed,
        out_specs=(P("groups", None), P("groups")),
        check_vma=False,
    )
```

```python
import functools

import jax
import jax.numpy as jnp
from jax import lax
from jax.experimental import pallas as pl
from jax.experimental.pallas import tpu as pltpu
from jax.sharding import PartitionSpec as P

BLK = 64
PAIR = 2 * BLK
HALF = BLK // 2

epsilon = 1e-05
MESH = pl.DeviceIdType.MESH


def shifted(block, axis, distance):
    devices = range(lax.axis_size(axis))
    route = [(i - distance, i) for i in devices if i - distance in devices]
    return lax.ppermute(block, axis, route)


def slot_index(mask, slot_count):
    band_rows, block_count = mask.shape
    kept = (mask > 0).astype(jnp.float32)
    upper = (jnp.arange(block_count)[:, None] <= jnp.arange(block_count)[None, :]).astype(jnp.float32)
    within = jnp.dot(kept, upper)
    lower = (jnp.arange(band_rows)[:, None] > jnp.arange(band_rows)[None, :]).astype(jnp.float32)
    running = within + jnp.dot(lower, within[:, -1:])
    slots = jnp.clip(running.astype(jnp.int32) - 1, 0, slot_count - 1)
    return jnp.where(mask > 0, slots, slot_count)


def build_body(chunks, index_ref, values_ref, panel_ref, listed):
    step = pl.program_id(0)
    chunk = values_ref.shape[0]
    slot_count = chunks * chunk
    block_count = panel_ref.shape[1] // BLK
    band = panel_ref.shape[0] // BLK

    @pl.when(step == 0)
    def _():
        listed[slot_count] = jnp.zeros((HALF, PAIR), jnp.bfloat16)

    @pl.when(step < chunks)
    def _():
        groups = chunk // 16

        @pl.loop(0, groups, unroll=4 if groups % 4 == 0 else 1)
        def _(group):
            at = pl.multiple_of(group * 16, 16)
            parts = [values_ref[pl.ds(at, 16), m * PAIR : (m + 1) * PAIR] for m in range(HALF)]
            listed[pl.ds(step * chunk + at, 16)] = jnp.transpose(jnp.stack(parts, axis=0), (1, 0, 2))

    @pl.when(step >= chunks)
    def _():
        low = lax.broadcasted_iota(jnp.int32, (HALF, PAIR), 1) < BLK

        def turned(block):
            return jnp.concatenate([block[:, BLK:], block[:, :BLK]], axis=1)

        @pl.loop(0, band)
        def _(row):
            first = ((step - chunks) * band + row) * block_count
            top = pl.multiple_of(row * BLK, BLK)
            for pair in range(block_count // 2):
                left = listed[index_ref[first + 2 * pair]]
                right = listed[index_ref[first + 2 * pair + 1]]
                lanes = slice(pair * PAIR, (pair + 1) * PAIR)
                panel_ref[pl.ds(top, HALF), lanes] = jnp.where(low, left, turned(right))
                panel_ref[pl.ds(top + HALF, HALF), lanes] = jnp.where(low, turned(left), right)


def build_panel(mask, values):
    band_rows, block_count = mask.shape
    slot_count, size = values.shape
    index = slot_index(mask, slot_count)
    chunk = next(c for c in (512, 192, 64, 32, 16) if slot_count % c == 0)
    chunks = slot_count // chunk
    band = 4 if band_rows % 4 == 0 else 1
    spec = pltpu.PrefetchScalarGridSpec(
        num_scalar_prefetch=1,
        grid=(chunks + band_rows // band,),
        in_specs=[pl.BlockSpec((chunk, size), lambda i, *_: (jnp.minimum(i, chunks - 1), 0))],
        out_specs=pl.BlockSpec((band * BLK, block_count * BLK), lambda i, *_: (jnp.maximum(i - chunks, 0), 0)),
        scratch_shapes=[pltpu.VMEM((slot_count + 1, HALF, PAIR), jnp.bfloat16)],
    )
    return pl.pallas_call(
        functools.partial(build_body, chunks),
        grid_spec=spec,
        out_shape=jax.ShapeDtypeStruct((band_rows * BLK, block_count * BLK), jnp.bfloat16),
        compiler_params=pltpu.CompilerParams(
            dimension_semantics=("arbitrary",), vmem_limit_bytes=50 << 20
        ),
    )(index.reshape(-1), values)


SPREAD = 1024.0


def coded(part):
    wide = part * SPREAD
    wide = wide * jnp.abs(wide)
    return (wide * jnp.abs(wide)).astype(jnp.bfloat16)


def decoded(code):
    wide = code.astype(jnp.float32)
    size = jnp.maximum(jnp.abs(wide), 1e-37)
    once = lax.rsqrt(size)
    return wide * once * lax.rsqrt(size * once)


SUBS = 2
SLOTS = 12


def chain_kernel(
    tensors, mask_ref, inputs_ref, gains_ref, targets_ref, values_ref, head_ref, out_ref,
    panel, listed, index, index_wide, index_sem, lhs, turn, hidden, sums, outgoing, relayed, arrived, residual, ahead, gathered, squares, total,
    square_out, square_in, stats_out, stats_in,
    panel_sem, head_sem, part_send, part_recv, relay_send, relay_recv, rest_send, rest_recv, square_send, square_recv,
    ahead_send, ahead_recv, own_send, cross_send, core_send, gather_recv, stats_send, stats_recv,
):
    sections = 4
    rows, width = inputs_ref.shape
    piece = panel.shape[2]
    pieces = width * tensors // piece
    slot_count, size = values_ref.shape
    per = width * piece // size
    stages = slot_count // per
    band_rows, block_count = mask_ref.shape
    full = width * tensors
    vocab_rows = head_ref.shape[0]
    z = lax.axis_index("tensor")
    q = lax.axis_index("section")
    column = q // 2
    core = q % 2

    def remote(src, dst, send, recv, t, s):
        return pltpu.make_async_remote_copy(
            src_ref=src, dst_ref=dst, send_sem=send, recv_sem=recv,
            device_id={"tensor": t, "section": s}, device_id_type=MESH,
        )

    def piece_at(t, half, sub):
        return (t * 2 + half) * SUBS + sub

    def out_order(j):
        sub, rest = j // (2 * tensors), j % (2 * tensors)
        return (z + 2 + rest // 2) % tensors, rest % 2, sub

    def in_order(j):
        sub, rest = j // (2 * tensors), j % (2 * tensors)
        half = jnp.where(rest < tensors, column, 1 - column)
        return (z + rest) % tensors, half, sub

    low = lax.broadcasted_iota(jnp.int32, (HALF, PAIR), 1) < BLK

    def block_row(row, first):
        evens, odds = [], []
        for pair in range(piece // PAIR):
            left = listed[index[row, first + 2 * pair]]
            right = listed[index[row, first + 2 * pair + 1]]
            evens.append(jnp.where(low, left, pltpu.roll(right, BLK, 1)))
            odds.append(jnp.where(low, pltpu.roll(left, BLK, 1), right))
        return jnp.concatenate(evens, axis=1), jnp.concatenate(odds, axis=1)

    def first_block(j):
        t, half, sub = out_order(j)
        return piece_at(t, half, sub) * (piece // BLK)

    def build(j):
        @pl.loop(0, width // BLK, unroll=4)
        def _(row):
            top = pl.multiple_of(row * BLK, BLK)
            even, odd = block_row(row, first_block(j))
            panel[j % SLOTS, pl.ds(top, HALF)] = even
            panel[j % SLOTS, pl.ds(top + HALF, HALF)] = odd

    def product_from_list(j):
        part = jnp.zeros((rows, piece), jnp.float32)
        for k in range(width // 256):
            tiles = []
            for row in range(256 // BLK):
                tiles += block_row(k * (256 // BLK) + row, first_block(j))
            part += jnp.dot(
                lhs[:, k * 256 : (k + 1) * 256], jnp.concatenate(tiles, axis=0), preferred_element_type=jnp.float32
            )
        return part

    def prebuild():
        @pl.loop(0, SLOTS)
        def _(j):
            build(j)

    def head_copy(j):
        t, half, sub = in_order(j)
        at = piece_at(t, half, sub)
        return pltpu.make_async_copy(
            head_ref.at[:, pl.ds(pl.multiple_of(at * piece, piece), piece)],
            panel.at[j % SLOTS, pl.ds(0, vocab_rows)], head_sem.at[j % SLOTS],
        )

    cuts = size // piece

    @pl.loop(0, stages * cuts)
    def _(k):
        stage, cut = k // cuts, k % cuts
        pltpu.make_async_copy(
            values_ref.at[pl.ds(pl.multiple_of(stage * per, per), per), pl.ds(pl.multiple_of(cut * piece, piece), piece)],
            panel.at[stage, pl.ds(pl.multiple_of(cut * per, per), per)], panel_sem.at[stage],
        ).start()

    barrier = pltpu.get_barrier_semaphore()
    me = z * sections + q
    everyone = tensors * sections

    @pl.loop(1, everyone)
    def _(k):
        other = (me + k) % everyone
        pl.semaphore_signal(
            barrier, inc=1, device_id={"tensor": other // sections, "section": other % sections},
            device_id_type=MESH,
        )

    kept = (mask_ref[...] > 0).astype(jnp.float32)
    across = lax.broadcasted_iota(jnp.int32, (block_count, block_count), 0)
    along = lax.broadcasted_iota(jnp.int32, (block_count, block_count), 1)
    within = jnp.dot(kept, jnp.where(across <= along, 1.0, 0.0), preferred_element_type=jnp.float32)
    across = lax.broadcasted_iota(jnp.int32, (band_rows, band_rows), 0)
    along = lax.broadcasted_iota(jnp.int32, (band_rows, band_rows), 1)
    counts = jnp.broadcast_to(within[:, block_count - 1 :], (band_rows, block_count))
    before = jnp.dot(jnp.where(across > along, 1.0, 0.0), counts, preferred_element_type=jnp.float32)
    running = (within + before).astype(jnp.int32)
    index_wide[...] = jnp.where(kept > 0, jnp.clip(running - 1, 0, slot_count - 1), slot_count)
    index_copy = pltpu.make_async_copy(index_wide, index, index_sem)
    index_copy.start()

    wide_row = lax.broadcasted_iota(jnp.int32, turn.shape, 0)
    wide_lane = lax.broadcasted_iota(jnp.int32, turn.shape, 1)
    inside = wide_lane % BLK
    comes_from = wide_lane - inside + 2 * (inside % HALF) + inside // HALF
    turn[...] = jnp.where(wide_row == comes_from, 1.0, 0.0).astype(jnp.bfloat16)
    total[...] = jnp.zeros_like(total)
    squares[...] = jnp.zeros_like(squares)

    @pl.when(q == 0)
    def _():
        for k in range(2 * SUBS):
            hidden[k] = inputs_ref[:, k * piece : (k + 1) * piece]

    def lane_sums(value):
        folded = value[:, :128]
        for k in range(1, value.shape[1] // 128):
            folded += value[:, k * 128 : (k + 1) * 128]
        return folded

    def summing(s, half):
        return jnp.where(s % 2 == 0, s + 1, half * 2), jnp.where(s % 2 == 0, half, s // 2)

    def prepare(s):
        @pl.when(s == 2)
        def _():
            for sub in range(SUBS):
                remote(ahead.at[sub], hidden.at[sub], ahead_send.at[sub], ahead_recv.at[sub], z, q).wait_recv()

        folded = jnp.zeros((rows, 128), jnp.float32)
        for k in range(2 * SUBS):
            wide = hidden[k].astype(jnp.float32)
            folded += lane_sums(wide * wide)
            gain = gains_ref[:, pl.ds(pl.multiple_of(z * width + k * piece, piece), piece)].astype(jnp.float32)
            scaled = (wide * gain).astype(jnp.bfloat16)
            for b in range(piece // 256):
                turned = jnp.dot(
                    scaled[:, b * 256 : (b + 1) * 256], turn[...], preferred_element_type=jnp.float32
                )
                lhs[:, k * piece + b * 256 : k * piece + (b + 1) * 256] = turned.astype(jnp.bfloat16)
        row = jnp.sum(folded.T, axis=0, keepdims=True)
        square_out[...] = jnp.broadcast_to(row, square_out.shape)

        @pl.loop(0, 2 * tensors)
        def _(j):
            @pl.when(jnp.logical_or(s % 2 == 1, j < tensors))
            def _():
                remote(
                    square_out, square_in.at[s // 2, z], square_send.at[j], square_recv.at[s // 2, z],
                    j % tensors, summing(s, j // tensors)[0],
                ).start()

    pl.semaphore_wait(barrier, everyone - 1)

    @pl.when(q == 0)
    def _():
        prepare(0)

    listed[slot_count] = jnp.zeros((HALF, PAIR), jnp.bfloat16)

    @pl.loop(0, stages)
    def _(stage):
        pltpu.make_async_copy(panel.at[stage], panel.at[stage], panel_sem.at[stage]).wait()

        @pl.loop(0, per // 16, unroll=4)
        def _(group):
            at = pl.multiple_of(group * 16, 16)
            parts = []
            for m in range(HALF):
                cut, lane = m * PAIR // piece, m * PAIR % piece
                parts.append(panel[stage, pl.ds(cut * per + at, 16), lane : lane + PAIR])
            listed[pl.ds(stage * per + at, 16)] = jnp.transpose(jnp.stack(parts, axis=0), (1, 0, 2))

    index_copy.wait()

    @pl.when(jnp.logical_or(q == 1, q == 2))
    def _():
        prebuild()

    def source(s):
        @pl.loop(0, pieces)
        def _(j):
            t, half, sub = out_order(j)
            at = piece_at(t, half, sub)

            late = jnp.logical_or(s == 0, j >= SLOTS)

            @pl.when(late)
            def _():
                outgoing[at] = coded(product_from_list(j))

            @pl.when(jnp.logical_not(late))
            def _():
                part = jnp.dot(lhs[...], panel[j % SLOTS], preferred_element_type=jnp.float32)
                outgoing[at] = coded(part)
            straight = jnp.logical_or(t == z, half == column)

            @pl.when(straight)
            def _():
                target, slot = summing(s, half)
                remote(
                    outgoing.at[at], arrived.at[slot, z, sub], part_send.at[at], part_recv.at[slot, z, sub], t, target
                ).start()

            @pl.when(jnp.logical_not(straight))
            def _():
                by = t * SUBS + sub
                remote(
                    outgoing.at[at], relayed.at[s % 2, by], part_send.at[at], relay_recv.at[s % 2, by],
                    z, (1 - column) * 2 + 1,
                ).start()

        for half in range(2):
            target, slot = summing(s, half)
            remote(
                hidden.at[pl.ds(half * SUBS, SUBS)], residual.at[slot], rest_send.at[half], rest_recv.at[slot], z, target
            ).start()
        @pl.loop(0, SLOTS)
        def _(j):
            head_copy(j).start()

    def relay(s):
        @pl.loop(0, tensors * SUBS)
        def _(j):
            t, sub = (z + 2 + j % tensors) % tensors, j // tensors
            by = t * SUBS + sub

            @pl.when(t != z)
            def _():
                remote(
                    relayed.at[s % 2, by], relayed.at[s % 2, by], relay_send.at[s % 2, by], relay_recv.at[s % 2, by], z, q
                ).wait_recv()
                target, slot = summing(s, column)
                remote(
                    relayed.at[s % 2, by], arrived.at[slot, z, sub], relay_send.at[s % 2, by],
                    part_recv.at[slot, z, sub], t, target,
                ).start()

    def reduce_half(s, half):
        slot = summing(s, half)[1]
        is_final = s == sections - 1
        remote(
            residual.at[slot], residual.at[slot], rest_send.at[0], rest_recv.at[slot], z, q
        ).wait_recv()
        for sub in range(SUBS):
            for t in range(tensors):
                remote(
                    outgoing.at[0], arrived.at[slot, t, sub], part_send.at[0], part_recv.at[slot, t, sub], z, q
                ).wait_recv()
            for b in range(piece // 128):
                lanes = slice(b * 128, (b + 1) * 128)
                product = jnp.zeros((rows, 128), jnp.float32)
                for t in range(tensors):
                    product += decoded(arrived[slot, t, sub, :, lanes])
                wide = residual[slot, sub, :, lanes].astype(jnp.float32)
                ahead[sub, :, lanes] = (wide + product * sums[...]).astype(jnp.bfloat16)

            @pl.when(q == s + 1)
            def _():
                hidden[half * SUBS + sub] = ahead[sub]

            @pl.when(jnp.logical_and(q == 0, s == 1))
            def _():
                remote(
                    ahead.at[sub], hidden.at[half * SUBS + sub], ahead_send.at[sub], ahead_recv.at[sub], z, 2
                ).start()

            @pl.when(is_final)
            def _():
                at = piece_at(z, column, sub)
                gathered[at] = ahead[sub]
                for k in range(1, tensors):
                    remote(
                        gathered.at[at], gathered.at[at], own_send.at[sub, k], gather_recv.at[at], (z + k) % tensors, q
                    ).start()
                remote(
                    gathered.at[at], gathered.at[at], cross_send.at[at], gather_recv.at[at], z, (q + 2) % sections
                ).start()
                remote(
                    gathered.at[at], gathered.at[at], core_send.at[at], gather_recv.at[at], z, column * 2 + 1
                ).start()

    def reducer(s):
        row = jnp.zeros(square_out.shape, jnp.float32)
        for t in range(tensors):
            remote(
                square_out, square_in.at[s // 2, t], square_send.at[0], square_recv.at[s // 2, t], z, q
            ).wait_recv()
            row += square_in[s // 2, t]
        scale = lax.rsqrt(row / full + epsilon) / SPREAD
        sums[...] = jnp.concatenate([scale] * (rows // 8), axis=0).T

        @pl.when(jnp.logical_and(s == 3, q == 0))
        def _():
            for sub in range(SUBS):
                remote(ahead.at[sub], hidden.at[sub], ahead_send.at[sub], ahead_recv.at[sub], z, 2).wait_send()

        @pl.loop(0, 2)
        def _(half):
            @pl.when(jnp.logical_or(s % 2 == 0, half == column))
            def _():
                reduce_half(s, half)

    @pl.loop(0, sections)
    def _(s):
        @pl.when(q == s)
        def _():
            @pl.when(s > 0)
            def _():
                prepare(s)

            source(s)

        @pl.when(q == 3 - 2 * (s // 2))
        def _():
            relay(s)

        @pl.when(jnp.logical_and(q == 3, s == 1))
        def _():
            prebuild()

        @pl.when(jnp.where(s % 2 == 0, q == s + 1, core == 0))
        def _():
            reducer(s)

    @pl.loop(0, pieces)
    def _(j):
        t, half, sub = in_order(j)
        at = piece_at(t, half, sub)
        rest = j % (2 * tensors)

        def come(send):
            return remote(gathered.at[at], gathered.at[at], send, gather_recv.at[at], z, column * 2 + 1)

        @pl.when(jnp.logical_or(core == 1, rest > 0))
        def _():
            come(core_send.at[at]).wait_recv()

        @pl.when(jnp.logical_and(core == 0, rest > 0))
        def _():
            come(core_send.at[at]).start()

            @pl.when(rest < tensors)
            def _():
                remote(
                    gathered.at[at], gathered.at[at], cross_send.at[at], gather_recv.at[at], z, (q + 2) % sections
                ).start()

        head_copy(j).wait()
        mine = gathered[at]
        total[...] += lax.dot_general(
            panel[j % SLOTS, :vocab_rows], mine, (((1,), (1,)), ((), ())), preferred_element_type=jnp.float32
        )
        wide = mine.astype(jnp.float32)
        squares[...] += lane_sums(wide * wide)

        @pl.when(j + SLOTS < pieces)
        def _():
            head_copy(j + SLOTS).start()

    final = jnp.sum(squares[...].T, axis=0, keepdims=True)
    scale = lax.rsqrt(final / full + epsilon)
    logits = total[...] * scale
    top = jnp.max(logits, axis=0, keepdims=True)
    count = jnp.sum(jnp.exp(logits - top), axis=0, keepdims=True)
    wanted = jnp.concatenate([targets_ref[k : k + 1] for k in range(targets_ref.shape[0])], axis=1)
    ids = lax.broadcasted_iota(jnp.int32, logits.shape, 0) + me * vocab_rows
    chosen = jnp.sum(jnp.where(ids == wanted, logits, 0.0), axis=0, keepdims=True)
    stats_out[...] = jnp.concatenate([top, count, chosen, jnp.zeros((5, rows), jnp.float32)], axis=0)

    @pl.loop(1, everyone)
    def _(k):
        other = (me + k) % everyone
        remote(
            stats_out, stats_in.at[me], stats_send.at[k], stats_recv.at[me], other // sections, other % sections
        ).start()

    stats_in[me] = stats_out[...]

    @pl.loop(1, everyone)
    def _(k):
        other = (me + k) % everyone
        remote(stats_out, stats_in.at[other], stats_send.at[k], stats_recv.at[other], z, q).wait_recv()

    highest = stats_in[0]
    for k in range(1, everyone):
        highest = jnp.maximum(highest, stats_in[k])
    highest = highest[0:1]
    exps = jnp.zeros((1, rows), jnp.float32)
    hit = jnp.zeros((1, rows), jnp.float32)
    for k in range(everyone):
        stat = stats_in[k]
        exps += stat[1:2] * jnp.exp(stat[0:1] - highest)
        hit += stat[2:3]
    loss = highest + jnp.log(exps) - hit
    mean = jnp.sum(loss, axis=1, keepdims=True) / rows
    out_ref[...] = jnp.concatenate(
        [loss, jnp.broadcast_to(mean, (1, rows)), jnp.zeros((6, rows), jnp.float32)], axis=0
    )

    @pl.loop(0, pieces)
    def _(j):
        remote(outgoing.at[j], arrived.at[0, 0, 0], part_send.at[j], part_recv.at[0, 0, 0], z, q).wait_send()

    @pl.loop(0, 2 * tensors)
    def _(j):
        @pl.when(jnp.logical_or(core == 1, j < tensors))
        def _():
            remote(square_out, square_in.at[0, 0], square_send.at[j], square_recv.at[0, 0], z, q).wait_send()

    for half in range(2):
        remote(
            hidden.at[pl.ds(half * SUBS, SUBS)], residual.at[0], rest_send.at[half], rest_recv.at[0], z, q
        ).wait_send()

    @pl.when(core == 1)
    def _():
        @pl.loop(0, 2 * tensors * SUBS)
        def _(j):
            kind, by = j // (tensors * SUBS), j % (tensors * SUBS)

            @pl.when(by // SUBS != z)
            def _():
                remote(
                    relayed.at[kind, by], relayed.at[kind, by], relay_send.at[kind, by], relay_recv.at[kind, by], z, q
                ).wait_send()

    @pl.when(core == 0)
    def _():
        for sub in range(SUBS):
            for k in range(1, tensors):
                remote(
                    gathered.at[0], gathered.at[0], own_send.at[sub, k], gather_recv.at[0], z, q
                ).wait_send()

        @pl.loop(0, pieces)
        def _(j):
            remote(gathered.at[j], gathered.at[j], core_send.at[j], gather_recv.at[j], z, q).wait_send()

        @pl.loop(0, tensors * SUBS)
        def _(j):
            at = piece_at(j // SUBS, column, j % SUBS)
            remote(gathered.at[at], gathered.at[at], cross_send.at[at], gather_recv.at[at], z, q).wait_send()

    @pl.loop(1, everyone)
    def _(k):
        remote(stats_out, stats_in.at[0], stats_send.at[k], stats_recv.at[0], z, q).wait_send()


def chain(mask, inputs, gains, targets, values, head):
    tensors = lax.axis_size("tensor")
    rows, width = inputs.shape
    piece = width // (2 * SUBS)
    pieces = 2 * SUBS * tensors
    everyone = tensors * lax.axis_size("section")
    vocab_rows = head.shape[0]
    half16, single = jnp.bfloat16, jnp.float32
    dma = pltpu.SemaphoreType.DMA
    vmem = pl.BlockSpec(memory_space=pltpu.VMEM)
    anywhere = pl.BlockSpec(memory_space=pl.ANY)
    out = pl.pallas_call(
        functools.partial(chain_kernel, tensors),
        out_shape=jax.ShapeDtypeStruct((8, rows), single),
        in_specs=[vmem, vmem, vmem, vmem, anywhere, anywhere],
        out_specs=vmem,
        scratch_shapes=[
            pltpu.VMEM((SLOTS, width, piece), half16),
            pltpu.VMEM((values.shape[0] + 16, HALF, PAIR), half16),
            pltpu.SMEM(mask.shape, jnp.int32),
            pltpu.VMEM(mask.shape, jnp.int32),
            dma(()),
            pltpu.VMEM((rows, width), half16),
            pltpu.VMEM((256, 256), half16),
            pltpu.VMEM((2 * SUBS, rows, piece), half16),
            pltpu.VMEM((rows, 128), single),
            pltpu.VMEM((pieces, rows, piece), half16),
            pltpu.VMEM((2, tensors * SUBS, rows, piece), half16),
            pltpu.VMEM((2, tensors, SUBS, rows, piece), half16),
            pltpu.VMEM((2, SUBS, rows, piece), half16),
            pltpu.VMEM((SUBS, rows, piece), half16),
            pltpu.VMEM((pieces, rows, piece), half16),
            pltpu.VMEM((rows, 128), single),
            pltpu.VMEM((vocab_rows, rows), single),
            pltpu.VMEM((8, rows), single),
            pltpu.VMEM((2, tensors, 8, rows), single),
            pltpu.VMEM((8, rows), single),
            pltpu.VMEM((everyone, 8, rows), single),
            dma((SLOTS,)),
            dma((SLOTS,)),
            dma((pieces,)),
            dma((2, tensors, SUBS)),
            dma((2, tensors * SUBS)),
            dma((2, tensors * SUBS)),
            dma((2,)),
            dma((2,)),
            dma((2 * tensors,)),
            dma((2, tensors)),
            dma((SUBS,)),
            dma((SUBS,)),
            dma((SUBS, tensors)),
            dma((pieces,)),
            dma((pieces,)),
            dma((pieces,)),
            dma((everyone,)),
            dma((everyone,)),
        ],
        compiler_params=pltpu.CompilerParams(
            collective_id=0, has_side_effects=True, vmem_limit_bytes=62 << 20
        ),
    )(mask, inputs, gains, targets, values, head)
    return out[0], out[1, :1]


def joined_loss(logits_top, total, chosen):
    stacked = jnp.stack([logits_top, total, chosen])
    everything = lax.all_gather(stacked, ("tensor", "section"))
    tops = everything[:, 0]
    top = jnp.max(tops, axis=0)
    total = jnp.sum(everything[:, 1] * jnp.exp(tops - top[None, :]), axis=0)
    return top + jnp.log(total) - jnp.sum(everything[:, 2], axis=0)


def general(inputs, gains, panel, head, targets):
    section_count = lax.axis_size("section")
    tensor_index = lax.axis_index("tensor")
    section_index = lax.axis_index("section")
    rows, local_width = inputs.shape
    full = panel.shape[1]
    gain = lax.dynamic_slice(gains, (tensor_index * local_width,), (local_width,))
    gain = gain.astype(jnp.float32)
    incoming = inputs
    for moment in range(section_count):
        current = jnp.where(section_index == 0, inputs, incoming) if moment else inputs
        wide = current.astype(jnp.float32)
        sumsq = lax.psum(jnp.sum(wide * wide, axis=1), "tensor")
        scaled = (wide * gain).astype(jnp.bfloat16)
        turned = scaled.reshape(rows, local_width // BLK, HALF, 2).transpose(0, 1, 3, 2)
        partial = jnp.dot(turned.reshape(rows, local_width), panel, preferred_element_type=jnp.float32)
        product = lax.psum_scatter(partial, "tensor", scatter_dimension=1, tiled=True)
        update = product * lax.rsqrt(sumsq[:, None] / full + epsilon)
        outgoing = (wide + update).astype(jnp.bfloat16)
        if moment < section_count - 1:
            incoming = shifted(outgoing, "section", 1)
    vocab_rows = head.shape[0]
    final = jnp.where(section_index == section_count - 1, outgoing, jnp.zeros_like(outgoing))
    relayed = lax.psum(final, "section")
    portion = lax.all_gather(relayed, "tensor", axis=1, tiled=True)
    raw_logits = lax.dot_general(
        portion, head, (((1,), (1,)), ((), ())), preferred_element_type=jnp.float32
    )
    widened = portion.astype(jnp.float32)
    final_sumsq = jnp.sum(widened * widened, axis=1)
    logits = raw_logits * lax.rsqrt(final_sumsq[:, None] / full + epsilon)
    vocab_start = (tensor_index * section_count + section_index) * vocab_rows
    local_ids = targets - vocab_start
    matches = jnp.arange(vocab_rows, dtype=jnp.int32)[None, :] == local_ids[:, None]
    target_logit = jnp.sum(jnp.where(matches, logits, 0.0), axis=1)
    local_top = jnp.max(logits, axis=1)
    local_total = jnp.sum(jnp.exp(logits - local_top[:, None]), axis=1)
    losses = joined_loss(local_top, local_total, target_logit)
    return losses, jnp.mean(losses).reshape(1)


def on_device(inputs, gains, keep_mask, block_values, head, targets):
    micro_count, row_count, width = inputs.shape
    rows = micro_count * row_count
    own = inputs.reshape(rows, width)
    ids = targets.reshape(rows)
    mask, values = keep_mask[0], block_values[0]
    piece = width // (2 * SUBS)
    fits = lax.axis_size("section") == 4 and rows == 128 and piece % 256 == 0 and head.shape[0] <= width
    if fits and head.shape[0] % 16 == 0 and values.shape[0] * values.shape[1] == SLOTS * width * piece:
        losses, mean_loss = chain(mask, own, gains, targets, values, head)
    else:
        losses, mean_loss = general(own, gains[0], build_panel(mask, values), head, ids)
    return losses.reshape(micro_count, row_count), mean_loss


def solution(mesh):
    placed = (
        P("groups", None, "tensor"),
        P("section", None),
        P("section", "tensor", None),
        P("section", "tensor", None),
        P(("tensor", "section"), None),
        P("groups", None),
    )
    return jax.shard_map(
        on_device,
        mesh=mesh,
        in_specs=placed,
        out_specs=(P("groups", None), P("groups")),
        check_vma=False,
    )
```

```python
import functools

import jax
import jax.numpy as jnp
from jax import lax
from jax.experimental import pallas as pl
from jax.experimental.pallas import tpu as pltpu
from jax.sharding import PartitionSpec as P

BLK = 64
PAIR = 2 * BLK
HALF = BLK // 2

epsilon = 1e-05
MESH = pl.DeviceIdType.MESH


def shifted(block, axis, distance):
    devices = range(lax.axis_size(axis))
    route = [(i - distance, i) for i in devices if i - distance in devices]
    return lax.ppermute(block, axis, route)


def slot_index(mask, slot_count):
    band_rows, block_count = mask.shape
    kept = (mask > 0).astype(jnp.float32)
    upper = (jnp.arange(block_count)[:, None] <= jnp.arange(block_count)[None, :]).astype(jnp.float32)
    within = jnp.dot(kept, upper)
    lower = (jnp.arange(band_rows)[:, None] > jnp.arange(band_rows)[None, :]).astype(jnp.float32)
    running = within + jnp.dot(lower, within[:, -1:])
    slots = jnp.clip(running.astype(jnp.int32) - 1, 0, slot_count - 1)
    return jnp.where(mask > 0, slots, slot_count)


def build_body(chunks, index_ref, values_ref, panel_ref, listed):
    step = pl.program_id(0)
    chunk = values_ref.shape[0]
    slot_count = chunks * chunk
    block_count = panel_ref.shape[1] // BLK
    band = panel_ref.shape[0] // BLK

    @pl.when(step == 0)
    def _():
        listed[slot_count] = jnp.zeros((HALF, PAIR), jnp.bfloat16)

    @pl.when(step < chunks)
    def _():
        groups = chunk // 16

        @pl.loop(0, groups, unroll=4 if groups % 4 == 0 else 1)
        def _(group):
            at = pl.multiple_of(group * 16, 16)
            parts = [values_ref[pl.ds(at, 16), m * PAIR : (m + 1) * PAIR] for m in range(HALF)]
            listed[pl.ds(step * chunk + at, 16)] = jnp.transpose(jnp.stack(parts, axis=0), (1, 0, 2))

    @pl.when(step >= chunks)
    def _():
        low = lax.broadcasted_iota(jnp.int32, (HALF, PAIR), 1) < BLK

        def turned(block):
            return jnp.concatenate([block[:, BLK:], block[:, :BLK]], axis=1)

        @pl.loop(0, band)
        def _(row):
            first = ((step - chunks) * band + row) * block_count
            top = pl.multiple_of(row * BLK, BLK)
            for pair in range(block_count // 2):
                left = listed[index_ref[first + 2 * pair]]
                right = listed[index_ref[first + 2 * pair + 1]]
                lanes = slice(pair * PAIR, (pair + 1) * PAIR)
                panel_ref[pl.ds(top, HALF), lanes] = jnp.where(low, left, turned(right))
                panel_ref[pl.ds(top + HALF, HALF), lanes] = jnp.where(low, turned(left), right)


def build_panel(mask, values):
    band_rows, block_count = mask.shape
    slot_count, size = values.shape
    index = slot_index(mask, slot_count)
    chunk = next(c for c in (512, 192, 64, 32, 16) if slot_count % c == 0)
    chunks = slot_count // chunk
    band = 4 if band_rows % 4 == 0 else 1
    spec = pltpu.PrefetchScalarGridSpec(
        num_scalar_prefetch=1,
        grid=(chunks + band_rows // band,),
        in_specs=[pl.BlockSpec((chunk, size), lambda i, *_: (jnp.minimum(i, chunks - 1), 0))],
        out_specs=pl.BlockSpec((band * BLK, block_count * BLK), lambda i, *_: (jnp.maximum(i - chunks, 0), 0)),
        scratch_shapes=[pltpu.VMEM((slot_count + 1, HALF, PAIR), jnp.bfloat16)],
    )
    return pl.pallas_call(
        functools.partial(build_body, chunks),
        grid_spec=spec,
        out_shape=jax.ShapeDtypeStruct((band_rows * BLK, block_count * BLK), jnp.bfloat16),
        compiler_params=pltpu.CompilerParams(
            dimension_semantics=("arbitrary",), vmem_limit_bytes=50 << 20
        ),
    )(index.reshape(-1), values)


SPREAD = 1024.0


def coded(part):
    wide = part * SPREAD
    wide = wide * jnp.abs(wide)
    return (wide * jnp.abs(wide)).astype(jnp.bfloat16)


def decoded(code):
    wide = code.astype(jnp.float32)
    size = jnp.maximum(jnp.abs(wide), 1e-37)
    once = lax.rsqrt(size)
    return wide * once * lax.rsqrt(size * once)


SUBS = 2
SLOTS = 12
GROUP = 2


def chain_kernel(
    tensors, mask_ref, inputs_ref, gains_ref, targets_ref, values_ref, head_ref, out_ref,
    panel, listed, index, index_wide, index_sem, lhs, turn, hidden, sums, outgoing, relayed, arrived, residual, ahead, gathered, squares, total,
    square_out, square_in, stats_out, stats_in,
    panel_sem, head_sem, part_send, part_recv, relay_send, relay_recv, rest_send, rest_recv, square_send, square_recv,
    ahead_send, ahead_recv, own_send, cross_send, core_send, gather_recv, stats_send, stats_recv,
):
    sections = 4
    rows, width = inputs_ref.shape
    piece = panel.shape[2]
    pieces = width * tensors // piece
    slot_count, size = values_ref.shape
    per = width * piece // size
    stages = slot_count // per
    band_rows, block_count = mask_ref.shape
    full = width * tensors
    vocab_rows = head_ref.shape[0]
    z = lax.axis_index("tensor")
    q = lax.axis_index("section")
    column = q // 2
    core = q % 2

    def remote(src, dst, send, recv, t, s):
        return pltpu.make_async_remote_copy(
            src_ref=src, dst_ref=dst, send_sem=send, recv_sem=recv,
            device_id={"tensor": t, "section": s}, device_id_type=MESH,
        )

    def piece_at(t, half, sub):
        return (t * 2 + half) * SUBS + sub

    def out_order(j):
        sub, rest = j // (2 * tensors), j % (2 * tensors)
        others = tensors - 1
        step = rest % others
        own = rest >= 2 * others
        half = jnp.where(rest < others, 1 - column, column)
        t = (z + (step + 1) % others + 1) % tensors
        return jnp.where(own, z, t), jnp.where(own, rest - 2 * others, half), sub

    def in_order(j):
        sub, rest = j // (2 * tensors), j % (2 * tensors)
        half = jnp.where(rest < tensors, column, 1 - column)
        return (z + rest) % tensors, half, sub

    low = lax.broadcasted_iota(jnp.int32, (HALF, PAIR), 1) < BLK

    def block_row(row, first):
        evens, odds = [], []
        for pair in range(piece // PAIR):
            left = listed[index[row, first + 2 * pair]]
            right = listed[index[row, first + 2 * pair + 1]]
            evens.append(jnp.where(low, left, pltpu.roll(right, BLK, 1)))
            odds.append(jnp.where(low, pltpu.roll(left, BLK, 1), right))
        return jnp.concatenate(evens, axis=1), jnp.concatenate(odds, axis=1)

    def first_block(j):
        t, half, sub = out_order(j)
        return piece_at(t, half, sub) * (piece // BLK)

    def build(j):
        @pl.loop(0, width // BLK, unroll=4)
        def _(row):
            top = pl.multiple_of(row * BLK, BLK)
            even, odd = block_row(row, first_block(j))
            panel[j % SLOTS, pl.ds(top, HALF)] = even
            panel[j % SLOTS, pl.ds(top + HALF, HALF)] = odd

    def product_from_list(j):
        part = jnp.zeros((rows, piece), jnp.float32)
        for k in range(width // 256):
            tiles = []
            for row in range(256 // BLK):
                tiles += block_row(k * (256 // BLK) + row, first_block(j))
            part += jnp.dot(
                lhs[:, k * 256 : (k + 1) * 256], jnp.concatenate(tiles, axis=0), preferred_element_type=jnp.float32
            )
        return part

    def prebuild():
        @pl.loop(0, SLOTS)
        def _(j):
            build(j)

    def head_copy(j):
        t, half, sub = in_order(j)
        at = piece_at(t, half, sub)
        return pltpu.make_async_copy(
            head_ref.at[:, pl.ds(pl.multiple_of(at * piece, piece), piece)],
            panel.at[j % SLOTS, pl.ds(0, vocab_rows)], head_sem.at[j % SLOTS],
        )

    cuts = size // piece

    @pl.loop(0, stages * cuts)
    def _(k):
        stage, cut = k // cuts, k % cuts
        pltpu.make_async_copy(
            values_ref.at[pl.ds(pl.multiple_of(stage * per, per), per), pl.ds(pl.multiple_of(cut * piece, piece), piece)],
            panel.at[stage, pl.ds(pl.multiple_of(cut * per, per), per)], panel_sem.at[stage],
        ).start()

    barrier = pltpu.get_barrier_semaphore()
    me = z * sections + q
    everyone = tensors * sections

    @pl.loop(1, everyone)
    def _(k):
        other = (me + k) % everyone
        pl.semaphore_signal(
            barrier, inc=1, device_id={"tensor": other // sections, "section": other % sections},
            device_id_type=MESH,
        )

    kept = (mask_ref[...] > 0).astype(jnp.float32)
    across = lax.broadcasted_iota(jnp.int32, (block_count, block_count), 0)
    along = lax.broadcasted_iota(jnp.int32, (block_count, block_count), 1)
    within = jnp.dot(kept, jnp.where(across <= along, 1.0, 0.0), preferred_element_type=jnp.float32)
    across = lax.broadcasted_iota(jnp.int32, (band_rows, band_rows), 0)
    along = lax.broadcasted_iota(jnp.int32, (band_rows, band_rows), 1)
    counts = jnp.broadcast_to(within[:, block_count - 1 :], (band_rows, block_count))
    before = jnp.dot(jnp.where(across > along, 1.0, 0.0), counts, preferred_element_type=jnp.float32)
    running = (within + before).astype(jnp.int32)
    index_wide[...] = jnp.where(kept > 0, jnp.clip(running - 1, 0, slot_count - 1), slot_count)
    index_copy = pltpu.make_async_copy(index_wide, index, index_sem)
    index_copy.start()

    wide_row = lax.broadcasted_iota(jnp.int32, turn.shape, 0)
    wide_lane = lax.broadcasted_iota(jnp.int32, turn.shape, 1)
    inside = wide_lane % BLK
    comes_from = wide_lane - inside + 2 * (inside % HALF) + inside // HALF
    turn[...] = jnp.where(wide_row == comes_from, 1.0, 0.0).astype(jnp.bfloat16)
    total[...] = jnp.zeros_like(total)
    squares[...] = jnp.zeros_like(squares)

    @pl.when(q == 0)
    def _():
        for k in range(2 * SUBS):
            hidden[k] = inputs_ref[:, k * piece : (k + 1) * piece]

    def lane_sums(value):
        folded = value[:, :128]
        for k in range(1, value.shape[1] // 128):
            folded += value[:, k * 128 : (k + 1) * 128]
        return folded

    def summing(s, half):
        return jnp.where(s % 2 == 0, s + 1, half * 2), jnp.where(s % 2 == 0, half, s // 2)

    def prepare(s):
        @pl.when(s == 2)
        def _():
            for sub in range(SUBS):
                remote(ahead.at[sub], hidden.at[sub], ahead_send.at[sub], ahead_recv.at[sub], z, q).wait_recv()

        folded = jnp.zeros((rows, 128), jnp.float32)
        for k in range(2 * SUBS):
            wide = hidden[k].astype(jnp.float32)
            folded += lane_sums(wide * wide)
            gain = gains_ref[:, pl.ds(pl.multiple_of(z * width + k * piece, piece), piece)].astype(jnp.float32)
            scaled = (wide * gain).astype(jnp.bfloat16)
            for b in range(piece // 256):
                turned = jnp.dot(
                    scaled[:, b * 256 : (b + 1) * 256], turn[...], preferred_element_type=jnp.float32
                )
                lhs[:, k * piece + b * 256 : k * piece + (b + 1) * 256] = turned.astype(jnp.bfloat16)
        row = jnp.sum(folded.T, axis=0, keepdims=True)
        square_out[...] = jnp.broadcast_to(row, square_out.shape)

        @pl.loop(0, 2 * tensors)
        def _(j):
            @pl.when(jnp.logical_or(s % 2 == 1, j < tensors))
            def _():
                remote(
                    square_out, square_in.at[s // 2, z], square_send.at[j], square_recv.at[s // 2, z],
                    j % tensors, summing(s, j // tensors)[0],
                ).start()

    pl.semaphore_wait(barrier, everyone - 1)

    @pl.when(q == 0)
    def _():
        prepare(0)

    listed[slot_count] = jnp.zeros((HALF, PAIR), jnp.bfloat16)

    @pl.loop(0, stages)
    def _(stage):
        pltpu.make_async_copy(panel.at[stage], panel.at[stage], panel_sem.at[stage]).wait()

        @pl.loop(0, per // 16, unroll=4)
        def _(group):
            at = pl.multiple_of(group * 16, 16)
            parts = []
            for m in range(HALF):
                cut, lane = m * PAIR // piece, m * PAIR % piece
                parts.append(panel[stage, pl.ds(cut * per + at, 16), lane : lane + PAIR])
            listed[pl.ds(stage * per + at, 16)] = jnp.transpose(jnp.stack(parts, axis=0), (1, 0, 2))

    index_copy.wait()

    @pl.when(jnp.logical_or(q == 1, q == 2))
    def _():
        prebuild()

    def source(s):
        def piece_of(j):
            return piece_at(*out_order(j))

        def send(j):
            t, half, sub = out_order(j)
            at = piece_at(t, half, sub)
            straight = jnp.logical_or(t == z, half == column)

            @pl.when(straight)
            def _():
                target, slot = summing(s, half)
                remote(
                    outgoing.at[at], arrived.at[slot, z, sub], part_send.at[at], part_recv.at[slot, z, sub], t, target
                ).start()

            @pl.when(jnp.logical_not(straight))
            def _():
                by = t * SUBS + sub
                remote(
                    outgoing.at[at], relayed.at[s % 2, by], part_send.at[at], relay_recv.at[s % 2, by],
                    z, (1 - column) * 2 + 1,
                ).start()

        @pl.loop(0, pieces // GROUP)
        def _(group):
            js = [group * GROUP + k for k in range(GROUP)]
            late = jnp.logical_or(s == 0, js[0] >= SLOTS)

            @pl.when(late)
            def _():
                for j in js:
                    outgoing[piece_of(j)] = coded(product_from_list(j))

            @pl.when(jnp.logical_not(late))
            def _():
                for j in js:
                    part = jnp.dot(lhs[...], panel[j % SLOTS], preferred_element_type=jnp.float32)
                    outgoing[piece_of(j)] = coded(part)

            for j in js:
                send(j)

        for half in range(2):
            target, slot = summing(s, half)
            remote(
                hidden.at[pl.ds(half * SUBS, SUBS)], residual.at[slot], rest_send.at[half], rest_recv.at[slot], z, target
            ).start()
        @pl.loop(0, SLOTS)
        def _(j):
            head_copy(j).start()

    def relay(s):
        @pl.loop(0, tensors * SUBS)
        def _(j):
            t, sub = (z + 2 + j % tensors) % tensors, j // tensors
            by = t * SUBS + sub

            @pl.when(t != z)
            def _():
                remote(
                    relayed.at[s % 2, by], relayed.at[s % 2, by], relay_send.at[s % 2, by], relay_recv.at[s % 2, by], z, q
                ).wait_recv()
                target, slot = summing(s, column)
                remote(
                    relayed.at[s % 2, by], arrived.at[slot, z, sub], relay_send.at[s % 2, by],
                    part_recv.at[slot, z, sub], t, target,
                ).start()

    def reduce_half(s, half):
        slot = summing(s, half)[1]
        is_final = s == sections - 1
        remote(
            residual.at[slot], residual.at[slot], rest_send.at[0], rest_recv.at[slot], z, q
        ).wait_recv()
        for sub in range(SUBS):
            for t in range(tensors):
                remote(
                    outgoing.at[0], arrived.at[slot, t, sub], part_send.at[0], part_recv.at[slot, t, sub], z, q
                ).wait_recv()
            for b in range(piece // 128):
                lanes = slice(b * 128, (b + 1) * 128)
                product = jnp.zeros((rows, 128), jnp.float32)
                for t in range(tensors):
                    product += decoded(arrived[slot, t, sub, :, lanes])
                wide = residual[slot, sub, :, lanes].astype(jnp.float32)
                ahead[sub, :, lanes] = (wide + product * sums[...]).astype(jnp.bfloat16)

            @pl.when(q == s + 1)
            def _():
                hidden[half * SUBS + sub] = ahead[sub]

            @pl.when(jnp.logical_and(q == 0, s == 1))
            def _():
                remote(
                    ahead.at[sub], hidden.at[half * SUBS + sub], ahead_send.at[sub], ahead_recv.at[sub], z, 2
                ).start()

            @pl.when(is_final)
            def _():
                at = piece_at(z, column, sub)
                gathered[at] = ahead[sub]
                for k in range(1, tensors):
                    remote(
                        gathered.at[at], gathered.at[at], own_send.at[sub, k], gather_recv.at[at], (z + k) % tensors, q
                    ).start()
                remote(
                    gathered.at[at], gathered.at[at], cross_send.at[at], gather_recv.at[at], z, (q + 2) % sections
                ).start()
                remote(
                    gathered.at[at], gathered.at[at], core_send.at[at], gather_recv.at[at], z, column * 2 + 1
                ).start()

    def reducer(s):
        row = jnp.zeros(square_out.shape, jnp.float32)
        for t in range(tensors):
            remote(
                square_out, square_in.at[s // 2, t], square_send.at[0], square_recv.at[s // 2, t], z, q
            ).wait_recv()
            row += square_in[s // 2, t]
        scale = lax.rsqrt(row / full + epsilon) / SPREAD
        sums[...] = jnp.concatenate([scale] * (rows // 8), axis=0).T

        @pl.when(jnp.logical_and(s == 3, q == 0))
        def _():
            for sub in range(SUBS):
                remote(ahead.at[sub], hidden.at[sub], ahead_send.at[sub], ahead_recv.at[sub], z, 2).wait_send()

        @pl.loop(0, 2)
        def _(half):
            @pl.when(jnp.logical_or(s % 2 == 0, half == column))
            def _():
                reduce_half(s, half)

    @pl.loop(0, sections)
    def _(s):
        @pl.when(q == s)
        def _():
            @pl.when(s > 0)
            def _():
                prepare(s)

            source(s)

        @pl.when(q == 3 - 2 * (s // 2))
        def _():
            relay(s)

        @pl.when(jnp.logical_and(q == 3, s == 1))
        def _():
            prebuild()

        @pl.when(jnp.where(s % 2 == 0, q == s + 1, core == 0))
        def _():
            reducer(s)

    @pl.loop(0, pieces)
    def _(j):
        t, half, sub = in_order(j)
        at = piece_at(t, half, sub)
        rest = j % (2 * tensors)

        def come(send):
            return remote(gathered.at[at], gathered.at[at], send, gather_recv.at[at], z, column * 2 + 1)

        @pl.when(jnp.logical_or(core == 1, rest > 0))
        def _():
            come(core_send.at[at]).wait_recv()

        @pl.when(jnp.logical_and(core == 0, rest > 0))
        def _():
            come(core_send.at[at]).start()

            @pl.when(rest < tensors)
            def _():
                remote(
                    gathered.at[at], gathered.at[at], cross_send.at[at], gather_recv.at[at], z, (q + 2) % sections
                ).start()

        head_copy(j).wait()
        mine = gathered[at]
        total[...] += lax.dot_general(
            panel[j % SLOTS, :vocab_rows], mine, (((1,), (1,)), ((), ())), preferred_element_type=jnp.float32
        )
        wide = mine.astype(jnp.float32)
        squares[...] += lane_sums(wide * wide)

        @pl.when(j + SLOTS < pieces)
        def _():
            head_copy(j + SLOTS).start()

    final = jnp.sum(squares[...].T, axis=0, keepdims=True)
    scale = lax.rsqrt(final / full + epsilon)
    logits = total[...] * scale
    top = jnp.max(logits, axis=0, keepdims=True)
    count = jnp.sum(jnp.exp(logits - top), axis=0, keepdims=True)
    wanted = jnp.concatenate([targets_ref[k : k + 1] for k in range(targets_ref.shape[0])], axis=1)
    ids = lax.broadcasted_iota(jnp.int32, logits.shape, 0) + me * vocab_rows
    chosen = jnp.sum(jnp.where(ids == wanted, logits, 0.0), axis=0, keepdims=True)
    stats_out[...] = jnp.concatenate([top, count, chosen, jnp.zeros((5, rows), jnp.float32)], axis=0)

    @pl.loop(1, everyone)
    def _(k):
        other = (me + k) % everyone
        remote(
            stats_out, stats_in.at[me], stats_send.at[k], stats_recv.at[me], other // sections, other % sections
        ).start()

    stats_in[me] = stats_out[...]

    @pl.loop(1, everyone)
    def _(k):
        other = (me + k) % everyone
        remote(stats_out, stats_in.at[other], stats_send.at[k], stats_recv.at[other], z, q).wait_recv()

    highest = stats_in[0]
    for k in range(1, everyone):
        highest = jnp.maximum(highest, stats_in[k])
    highest = highest[0:1]
    exps = jnp.zeros((1, rows), jnp.float32)
    hit = jnp.zeros((1, rows), jnp.float32)
    for k in range(everyone):
        stat = stats_in[k]
        exps += stat[1:2] * jnp.exp(stat[0:1] - highest)
        hit += stat[2:3]
    loss = highest + jnp.log(exps) - hit
    mean = jnp.sum(loss, axis=1, keepdims=True) / rows
    out_ref[...] = jnp.concatenate(
        [loss, jnp.broadcast_to(mean, (1, rows)), jnp.zeros((6, rows), jnp.float32)], axis=0
    )

    @pl.loop(0, pieces)
    def _(j):
        remote(outgoing.at[j], arrived.at[0, 0, 0], part_send.at[j], part_recv.at[0, 0, 0], z, q).wait_send()

    @pl.loop(0, 2 * tensors)
    def _(j):
        @pl.when(jnp.logical_or(core == 1, j < tensors))
        def _():
            remote(square_out, square_in.at[0, 0], square_send.at[j], square_recv.at[0, 0], z, q).wait_send()

    for half in range(2):
        remote(
            hidden.at[pl.ds(half * SUBS, SUBS)], residual.at[0], rest_send.at[half], rest_recv.at[0], z, q
        ).wait_send()

    @pl.when(core == 1)
    def _():
        @pl.loop(0, 2 * tensors * SUBS)
        def _(j):
            kind, by = j // (tensors * SUBS), j % (tensors * SUBS)

            @pl.when(by // SUBS != z)
            def _():
                remote(
                    relayed.at[kind, by], relayed.at[kind, by], relay_send.at[kind, by], relay_recv.at[kind, by], z, q
                ).wait_send()

    @pl.when(core == 0)
    def _():
        for sub in range(SUBS):
            for k in range(1, tensors):
                remote(
                    gathered.at[0], gathered.at[0], own_send.at[sub, k], gather_recv.at[0], z, q
                ).wait_send()

        @pl.loop(0, pieces)
        def _(j):
            remote(gathered.at[j], gathered.at[j], core_send.at[j], gather_recv.at[j], z, q).wait_send()

        @pl.loop(0, tensors * SUBS)
        def _(j):
            at = piece_at(j // SUBS, column, j % SUBS)
            remote(gathered.at[at], gathered.at[at], cross_send.at[at], gather_recv.at[at], z, q).wait_send()

    @pl.loop(1, everyone)
    def _(k):
        remote(stats_out, stats_in.at[0], stats_send.at[k], stats_recv.at[0], z, q).wait_send()


def chain(mask, inputs, gains, targets, values, head):
    tensors = lax.axis_size("tensor")
    rows, width = inputs.shape
    piece = width // (2 * SUBS)
    pieces = 2 * SUBS * tensors
    everyone = tensors * lax.axis_size("section")
    vocab_rows = head.shape[0]
    half16, single = jnp.bfloat16, jnp.float32
    dma = pltpu.SemaphoreType.DMA
    vmem = pl.BlockSpec(memory_space=pltpu.VMEM)
    anywhere = pl.BlockSpec(memory_space=pl.ANY)
    out = pl.pallas_call(
        functools.partial(chain_kernel, tensors),
        out_shape=jax.ShapeDtypeStruct((8, rows), single),
        in_specs=[vmem, vmem, vmem, vmem, anywhere, anywhere],
        out_specs=vmem,
        scratch_shapes=[
            pltpu.VMEM((SLOTS, width, piece), half16),
            pltpu.VMEM((values.shape[0] + 16, HALF, PAIR), half16),
            pltpu.SMEM(mask.shape, jnp.int32),
            pltpu.VMEM(mask.shape, jnp.int32),
            dma(()),
            pltpu.VMEM((rows, width), half16),
            pltpu.VMEM((256, 256), half16),
            pltpu.VMEM((2 * SUBS, rows, piece), half16),
            pltpu.VMEM((rows, 128), single),
            pltpu.VMEM((pieces, rows, piece), half16),
            pltpu.VMEM((2, tensors * SUBS, rows, piece), half16),
            pltpu.VMEM((2, tensors, SUBS, rows, piece), half16),
            pltpu.VMEM((2, SUBS, rows, piece), half16),
            pltpu.VMEM((SUBS, rows, piece), half16),
            pltpu.VMEM((pieces, rows, piece), half16),
            pltpu.VMEM((rows, 128), single),
            pltpu.VMEM((vocab_rows, rows), single),
            pltpu.VMEM((8, rows), single),
            pltpu.VMEM((2, tensors, 8, rows), single),
            pltpu.VMEM((8, rows), single),
            pltpu.VMEM((everyone, 8, rows), single),
            dma((SLOTS,)),
            dma((SLOTS,)),
            dma((pieces,)),
            dma((2, tensors, SUBS)),
            dma((2, tensors * SUBS)),
            dma((2, tensors * SUBS)),
            dma((2,)),
            dma((2,)),
            dma((2 * tensors,)),
            dma((2, tensors)),
            dma((SUBS,)),
            dma((SUBS,)),
            dma((SUBS, tensors)),
            dma((pieces,)),
            dma((pieces,)),
            dma((pieces,)),
            dma((everyone,)),
            dma((everyone,)),
        ],
        compiler_params=pltpu.CompilerParams(
            collective_id=0, has_side_effects=True, vmem_limit_bytes=62 << 20
        ),
    )(mask, inputs, gains, targets, values, head)
    return out[0], out[1, :1]


def joined_loss(logits_top, total, chosen):
    stacked = jnp.stack([logits_top, total, chosen])
    everything = lax.all_gather(stacked, ("tensor", "section"))
    tops = everything[:, 0]
    top = jnp.max(tops, axis=0)
    total = jnp.sum(everything[:, 1] * jnp.exp(tops - top[None, :]), axis=0)
    return top + jnp.log(total) - jnp.sum(everything[:, 2], axis=0)


def general(inputs, gains, panel, head, targets):
    section_count = lax.axis_size("section")
    tensor_index = lax.axis_index("tensor")
    section_index = lax.axis_index("section")
    rows, local_width = inputs.shape
    full = panel.shape[1]
    gain = lax.dynamic_slice(gains, (tensor_index * local_width,), (local_width,))
    gain = gain.astype(jnp.float32)
    incoming = inputs
    for moment in range(section_count):
        current = jnp.where(section_index == 0, inputs, incoming) if moment else inputs
        wide = current.astype(jnp.float32)
        sumsq = lax.psum(jnp.sum(wide * wide, axis=1), "tensor")
        scaled = (wide * gain).astype(jnp.bfloat16)
        turned = scaled.reshape(rows, local_width // BLK, HALF, 2).transpose(0, 1, 3, 2)
        partial = jnp.dot(turned.reshape(rows, local_width), panel, preferred_element_type=jnp.float32)
        product = lax.psum_scatter(partial, "tensor", scatter_dimension=1, tiled=True)
        update = product * lax.rsqrt(sumsq[:, None] / full + epsilon)
        outgoing = (wide + update).astype(jnp.bfloat16)
        if moment < section_count - 1:
            incoming = shifted(outgoing, "section", 1)
    vocab_rows = head.shape[0]
    final = jnp.where(section_index == section_count - 1, outgoing, jnp.zeros_like(outgoing))
    relayed = lax.psum(final, "section")
    portion = lax.all_gather(relayed, "tensor", axis=1, tiled=True)
    raw_logits = lax.dot_general(
        portion, head, (((1,), (1,)), ((), ())), preferred_element_type=jnp.float32
    )
    widened = portion.astype(jnp.float32)
    final_sumsq = jnp.sum(widened * widened, axis=1)
    logits = raw_logits * lax.rsqrt(final_sumsq[:, None] / full + epsilon)
    vocab_start = (tensor_index * section_count + section_index) * vocab_rows
    local_ids = targets - vocab_start
    matches = jnp.arange(vocab_rows, dtype=jnp.int32)[None, :] == local_ids[:, None]
    target_logit = jnp.sum(jnp.where(matches, logits, 0.0), axis=1)
    local_top = jnp.max(logits, axis=1)
    local_total = jnp.sum(jnp.exp(logits - local_top[:, None]), axis=1)
    losses = joined_loss(local_top, local_total, target_logit)
    return losses, jnp.mean(losses).reshape(1)


def on_device(inputs, gains, keep_mask, block_values, head, targets):
    micro_count, row_count, width = inputs.shape
    rows = micro_count * row_count
    own = inputs.reshape(rows, width)
    ids = targets.reshape(rows)
    mask, values = keep_mask[0], block_values[0]
    piece = width // (2 * SUBS)
    fits = lax.axis_size("section") == 4 and rows == 128 and piece % 256 == 0 and head.shape[0] <= width
    if fits and head.shape[0] % 16 == 0 and values.shape[0] * values.shape[1] == SLOTS * width * piece:
        losses, mean_loss = chain(mask, own, gains, targets, values, head)
    else:
        losses, mean_loss = general(own, gains[0], build_panel(mask, values), head, ids)
    return losses.reshape(micro_count, row_count), mean_loss


def solution(mesh):
    placed = (
        P("groups", None, "tensor"),
        P("section", None),
        P("section", "tensor", None),
        P("section", "tensor", None),
        P(("tensor", "section"), None),
        P("groups", None),
    )
    return jax.shard_map(
        on_device,
        mesh=mesh,
        in_specs=placed,
        out_specs=(P("groups", None), P("groups")),
        check_vma=False,
    )
```

```python
import functools

import jax
import jax.numpy as jnp
from jax import lax
from jax.experimental import pallas as pl
from jax.experimental.pallas import tpu as pltpu
from jax.sharding import PartitionSpec as P

BLK = 64
PAIR = 2 * BLK
HALF = BLK // 2

epsilon = 1e-05
MESH = pl.DeviceIdType.MESH


def shifted(block, axis, distance):
    devices = range(lax.axis_size(axis))
    route = [(i - distance, i) for i in devices if i - distance in devices]
    return lax.ppermute(block, axis, route)


def slot_index(mask, slot_count):
    band_rows, block_count = mask.shape
    kept = (mask > 0).astype(jnp.float32)
    upper = (jnp.arange(block_count)[:, None] <= jnp.arange(block_count)[None, :]).astype(jnp.float32)
    within = jnp.dot(kept, upper)
    lower = (jnp.arange(band_rows)[:, None] > jnp.arange(band_rows)[None, :]).astype(jnp.float32)
    running = within + jnp.dot(lower, within[:, -1:])
    slots = jnp.clip(running.astype(jnp.int32) - 1, 0, slot_count - 1)
    return jnp.where(mask > 0, slots, slot_count)


def build_body(chunks, index_ref, values_ref, panel_ref, listed):
    step = pl.program_id(0)
    chunk = values_ref.shape[0]
    slot_count = chunks * chunk
    block_count = panel_ref.shape[1] // BLK
    band = panel_ref.shape[0] // BLK

    @pl.when(step == 0)
    def _():
        listed[slot_count] = jnp.zeros((HALF, PAIR), jnp.bfloat16)

    @pl.when(step < chunks)
    def _():
        groups = chunk // 16

        @pl.loop(0, groups, unroll=4 if groups % 4 == 0 else 1)
        def _(group):
            at = pl.multiple_of(group * 16, 16)
            parts = [values_ref[pl.ds(at, 16), m * PAIR : (m + 1) * PAIR] for m in range(HALF)]
            listed[pl.ds(step * chunk + at, 16)] = jnp.transpose(jnp.stack(parts, axis=0), (1, 0, 2))

    @pl.when(step >= chunks)
    def _():
        low = lax.broadcasted_iota(jnp.int32, (HALF, PAIR), 1) < BLK

        def turned(block):
            return jnp.concatenate([block[:, BLK:], block[:, :BLK]], axis=1)

        @pl.loop(0, band)
        def _(row):
            first = ((step - chunks) * band + row) * block_count
            top = pl.multiple_of(row * BLK, BLK)
            for pair in range(block_count // 2):
                left = listed[index_ref[first + 2 * pair]]
                right = listed[index_ref[first + 2 * pair + 1]]
                lanes = slice(pair * PAIR, (pair + 1) * PAIR)
                panel_ref[pl.ds(top, HALF), lanes] = jnp.where(low, left, turned(right))
                panel_ref[pl.ds(top + HALF, HALF), lanes] = jnp.where(low, turned(left), right)


def build_panel(mask, values):
    band_rows, block_count = mask.shape
    slot_count, size = values.shape
    index = slot_index(mask, slot_count)
    chunk = next(c for c in (512, 192, 64, 32, 16) if slot_count % c == 0)
    chunks = slot_count // chunk
    band = 4 if band_rows % 4 == 0 else 1
    spec = pltpu.PrefetchScalarGridSpec(
        num_scalar_prefetch=1,
        grid=(chunks + band_rows // band,),
        in_specs=[pl.BlockSpec((chunk, size), lambda i, *_: (jnp.minimum(i, chunks - 1), 0))],
        out_specs=pl.BlockSpec((band * BLK, block_count * BLK), lambda i, *_: (jnp.maximum(i - chunks, 0), 0)),
        scratch_shapes=[pltpu.VMEM((slot_count + 1, HALF, PAIR), jnp.bfloat16)],
    )
    return pl.pallas_call(
        functools.partial(build_body, chunks),
        grid_spec=spec,
        out_shape=jax.ShapeDtypeStruct((band_rows * BLK, block_count * BLK), jnp.bfloat16),
        compiler_params=pltpu.CompilerParams(
            dimension_semantics=("arbitrary",), vmem_limit_bytes=50 << 20
        ),
    )(index.reshape(-1), values)


SPREAD = 1024.0


def coded(part):
    wide = part * SPREAD
    wide = wide * jnp.abs(wide)
    return (wide * jnp.abs(wide)).astype(jnp.bfloat16)


def decoded(code):
    wide = code.astype(jnp.float32)
    size = jnp.maximum(jnp.abs(wide), 1e-37)
    once = lax.rsqrt(size)
    return wide * once * lax.rsqrt(size * once)


SUBS = 2
SLOTS = 12
GROUP = 2


def chain_kernel(
    tensors, mask_ref, inputs_ref, gains_ref, targets_ref, values_ref, head_ref, out_ref,
    panel, listed, index, index_wide, index_sem, lhs, turn, hidden, sums, outgoing, relayed, arrived, residual, ahead, gathered, squares, total,
    square_out, square_in, stats_out, stats_in,
    panel_sem, head_sem, part_send, part_recv, relay_send, relay_recv, rest_send, rest_recv, square_send, square_recv,
    ahead_send, ahead_recv, own_send, cross_send, core_send, gather_recv, stats_send, stats_recv,
):
    sections = 4
    rows, width = inputs_ref.shape
    piece = panel.shape[2]
    pieces = width * tensors // piece
    slot_count, size = values_ref.shape
    per = width * piece // size
    stages = slot_count // per
    band_rows, block_count = mask_ref.shape
    full = width * tensors
    vocab_rows = head_ref.shape[0]
    z = lax.axis_index("tensor")
    q = lax.axis_index("section")
    column = q // 2
    core = q % 2

    def remote(src, dst, send, recv, t, s):
        return pltpu.make_async_remote_copy(
            src_ref=src, dst_ref=dst, send_sem=send, recv_sem=recv,
            device_id={"tensor": t, "section": s}, device_id_type=MESH,
        )

    def piece_at(t, half, sub):
        return (t * 2 + half) * SUBS + sub

    def out_order(j):
        sub, rest = j // (2 * tensors), j % (2 * tensors)
        others = tensors - 1
        step = rest % others
        own = rest >= 2 * others
        half = jnp.where(rest < others, 1 - column, column)
        t = (z + (step + 1) % others + 1) % tensors
        return jnp.where(own, z, t), jnp.where(own, rest - 2 * others, half), sub

    def in_order(j):
        half = jnp.where(j < pieces // 2, column, 1 - column)
        return (z + j) % tensors, half, j // tensors % SUBS

    low = lax.broadcasted_iota(jnp.int32, (HALF, PAIR), 1) < BLK

    def block_row(row, first):
        evens, odds = [], []
        for pair in range(piece // PAIR):
            left = listed[index[row, first + 2 * pair]]
            right = listed[index[row, first + 2 * pair + 1]]
            evens.append(jnp.where(low, left, pltpu.roll(right, BLK, 1)))
            odds.append(jnp.where(low, pltpu.roll(left, BLK, 1), right))
        return jnp.concatenate(evens, axis=1), jnp.concatenate(odds, axis=1)

    def first_block(j):
        t, half, sub = out_order(j)
        return piece_at(t, half, sub) * (piece // BLK)

    def build(j):
        @pl.loop(0, width // BLK, unroll=4)
        def _(row):
            top = pl.multiple_of(row * BLK, BLK)
            even, odd = block_row(row, first_block(j))
            panel[j % SLOTS, pl.ds(top, HALF)] = even
            panel[j % SLOTS, pl.ds(top + HALF, HALF)] = odd

    def product_from_list(j):
        part = jnp.zeros((rows, piece), jnp.float32)
        for k in range(width // 256):
            tiles = []
            for row in range(256 // BLK):
                tiles += block_row(k * (256 // BLK) + row, first_block(j))
            part += jnp.dot(
                lhs[:, k * 256 : (k + 1) * 256], jnp.concatenate(tiles, axis=0), preferred_element_type=jnp.float32
            )
        return part

    def prebuild():
        @pl.loop(0, SLOTS)
        def _(j):
            build(j)

    def head_copy(j):
        t, half, sub = in_order(j)
        at = piece_at(t, half, sub)
        return pltpu.make_async_copy(
            head_ref.at[:, pl.ds(pl.multiple_of(at * piece, piece), piece)],
            panel.at[j % SLOTS, pl.ds(0, vocab_rows)], head_sem.at[j % SLOTS],
        )

    cuts = size // piece

    @pl.loop(0, stages * cuts)
    def _(k):
        stage, cut = k // cuts, k % cuts
        pltpu.make_async_copy(
            values_ref.at[pl.ds(pl.multiple_of(stage * per, per), per), pl.ds(pl.multiple_of(cut * piece, piece), piece)],
            panel.at[stage, pl.ds(pl.multiple_of(cut * per, per), per)], panel_sem.at[stage],
        ).start()

    barrier = pltpu.get_barrier_semaphore()
    me = z * sections + q
    everyone = tensors * sections

    @pl.loop(1, everyone)
    def _(k):
        other = (me + k) % everyone
        pl.semaphore_signal(
            barrier, inc=1, device_id={"tensor": other // sections, "section": other % sections},
            device_id_type=MESH,
        )

    kept = (mask_ref[...] > 0).astype(jnp.float32)
    across = lax.broadcasted_iota(jnp.int32, (block_count, block_count), 0)
    along = lax.broadcasted_iota(jnp.int32, (block_count, block_count), 1)
    within = jnp.dot(kept, jnp.where(across <= along, 1.0, 0.0), preferred_element_type=jnp.float32)
    across = lax.broadcasted_iota(jnp.int32, (band_rows, band_rows), 0)
    along = lax.broadcasted_iota(jnp.int32, (band_rows, band_rows), 1)
    counts = jnp.broadcast_to(within[:, block_count - 1 :], (band_rows, block_count))
    before = jnp.dot(jnp.where(across > along, 1.0, 0.0), counts, preferred_element_type=jnp.float32)
    running = (within + before).astype(jnp.int32)
    index_wide[...] = jnp.where(kept > 0, jnp.clip(running - 1, 0, slot_count - 1), slot_count)
    index_copy = pltpu.make_async_copy(index_wide, index, index_sem)
    index_copy.start()

    wide_row = lax.broadcasted_iota(jnp.int32, turn.shape, 0)
    wide_lane = lax.broadcasted_iota(jnp.int32, turn.shape, 1)
    inside = wide_lane % BLK
    comes_from = wide_lane - inside + 2 * (inside % HALF) + inside // HALF
    turn[...] = jnp.where(wide_row == comes_from, 1.0, 0.0).astype(jnp.bfloat16)
    total[...] = jnp.zeros_like(total)
    squares[...] = jnp.zeros_like(squares)

    @pl.when(q == 0)
    def _():
        for k in range(2 * SUBS):
            hidden[k] = inputs_ref[:, k * piece : (k + 1) * piece]

    def lane_sums(value):
        folded = value[:, :128]
        for k in range(1, value.shape[1] // 128):
            folded += value[:, k * 128 : (k + 1) * 128]
        return folded

    def summing(s, half):
        return jnp.where(s % 2 == 0, s + 1, half * 2), jnp.where(s % 2 == 0, half, s // 2)

    def prepare(s):
        @pl.when(s == 2)
        def _():
            for sub in range(SUBS):
                remote(ahead.at[sub], hidden.at[sub], ahead_send.at[sub], ahead_recv.at[sub], z, q).wait_recv()

        folded = jnp.zeros((rows, 128), jnp.float32)
        for k in range(2 * SUBS):
            wide = hidden[k].astype(jnp.float32)
            folded += lane_sums(wide * wide)
            gain = gains_ref[:, pl.ds(pl.multiple_of(z * width + k * piece, piece), piece)].astype(jnp.float32)
            scaled = (wide * gain).astype(jnp.bfloat16)
            for b in range(piece // 256):
                turned = jnp.dot(
                    scaled[:, b * 256 : (b + 1) * 256], turn[...], preferred_element_type=jnp.float32
                )
                lhs[:, k * piece + b * 256 : k * piece + (b + 1) * 256] = turned.astype(jnp.bfloat16)
        row = jnp.sum(folded.T, axis=0, keepdims=True)
        square_out[...] = jnp.broadcast_to(row, square_out.shape)

        @pl.loop(0, 2 * tensors)
        def _(j):
            @pl.when(jnp.logical_or(s % 2 == 1, j < tensors))
            def _():
                remote(
                    square_out, square_in.at[s // 2, z], square_send.at[j], square_recv.at[s // 2, z],
                    j % tensors, summing(s, j // tensors)[0],
                ).start()

    pl.semaphore_wait(barrier, everyone - 1)

    @pl.when(q == 0)
    def _():
        prepare(0)

    listed[slot_count] = jnp.zeros((HALF, PAIR), jnp.bfloat16)

    @pl.loop(0, stages)
    def _(stage):
        pltpu.make_async_copy(panel.at[stage], panel.at[stage], panel_sem.at[stage]).wait()

        @pl.loop(0, per // 16, unroll=4)
        def _(group):
            at = pl.multiple_of(group * 16, 16)
            parts = []
            for m in range(HALF):
                cut, lane = m * PAIR // piece, m * PAIR % piece
                parts.append(panel[stage, pl.ds(cut * per + at, 16), lane : lane + PAIR])
            listed[pl.ds(stage * per + at, 16)] = jnp.transpose(jnp.stack(parts, axis=0), (1, 0, 2))

    index_copy.wait()

    @pl.when(jnp.logical_or(q == 1, q == 2))
    def _():
        prebuild()

    def source(s):
        def piece_of(j):
            return piece_at(*out_order(j))

        def send(j):
            t, half, sub = out_order(j)
            at = piece_at(t, half, sub)
            straight = jnp.logical_or(t == z, half == column)

            @pl.when(straight)
            def _():
                target, slot = summing(s, half)
                remote(
                    outgoing.at[at], arrived.at[slot, z, sub], part_send.at[at], part_recv.at[slot, z, sub], t, target
                ).start()

            @pl.when(jnp.logical_not(straight))
            def _():
                by = t * SUBS + sub
                remote(
                    outgoing.at[at], relayed.at[s % 2, by], part_send.at[at], relay_recv.at[s % 2, by],
                    z, (1 - column) * 2 + 1,
                ).start()

        @pl.loop(0, pieces // GROUP)
        def _(group):
            js = [group * GROUP + k for k in range(GROUP)]
            late = jnp.logical_or(s == 0, js[0] >= SLOTS)

            @pl.when(late)
            def _():
                for j in js:
                    outgoing[piece_of(j)] = coded(product_from_list(j))

            @pl.when(jnp.logical_not(late))
            def _():
                for j in js:
                    part = jnp.dot(lhs[...], panel[j % SLOTS], preferred_element_type=jnp.float32)
                    outgoing[piece_of(j)] = coded(part)

            for j in js:
                send(j)

        for half in range(2):
            target, slot = summing(s, half)
            remote(
                hidden.at[pl.ds(half * SUBS, SUBS)], residual.at[slot], rest_send.at[half], rest_recv.at[slot], z, target
            ).start()
        @pl.loop(0, SLOTS)
        def _(j):
            head_copy(j).start()

    def relay(s):
        @pl.loop(0, tensors * SUBS)
        def _(j):
            t, sub = (z + 2 + j % tensors) % tensors, j // tensors
            by = t * SUBS + sub

            @pl.when(t != z)
            def _():
                remote(
                    relayed.at[s % 2, by], relayed.at[s % 2, by], relay_send.at[s % 2, by], relay_recv.at[s % 2, by], z, q
                ).wait_recv()
                target, slot = summing(s, column)
                remote(
                    relayed.at[s % 2, by], arrived.at[slot, z, sub], relay_send.at[s % 2, by],
                    part_recv.at[slot, z, sub], t, target,
                ).start()

    def reduce_half(s, half):
        slot = summing(s, half)[1]
        is_final = s == sections - 1
        remote(
            residual.at[slot], residual.at[slot], rest_send.at[0], rest_recv.at[slot], z, q
        ).wait_recv()
        for sub in range(SUBS):
            for t in range(tensors):
                remote(
                    outgoing.at[0], arrived.at[slot, t, sub], part_send.at[0], part_recv.at[slot, t, sub], z, q
                ).wait_recv()
            for b in range(piece // 128):
                lanes = slice(b * 128, (b + 1) * 128)
                product = jnp.zeros((rows, 128), jnp.float32)
                for t in range(tensors):
                    product += decoded(arrived[slot, t, sub, :, lanes])
                wide = residual[slot, sub, :, lanes].astype(jnp.float32)
                ahead[sub, :, lanes] = (wide + product * sums[...]).astype(jnp.bfloat16)

            @pl.when(q == s + 1)
            def _():
                hidden[half * SUBS + sub] = ahead[sub]

            @pl.when(jnp.logical_and(q == 0, s == 1))
            def _():
                remote(
                    ahead.at[sub], hidden.at[half * SUBS + sub], ahead_send.at[sub], ahead_recv.at[sub], z, 2
                ).start()

            @pl.when(is_final)
            def _():
                at = piece_at(z, column, sub)
                gathered[at] = ahead[sub]
                for k in range(1, tensors):
                    remote(
                        gathered.at[at], gathered.at[at], own_send.at[sub, k], gather_recv.at[at], (z + k) % tensors, q
                    ).start()
                remote(
                    gathered.at[at], gathered.at[at], cross_send.at[at], gather_recv.at[at], z, (q + 2) % sections
                ).start()
                remote(
                    gathered.at[at], gathered.at[at], core_send.at[at], gather_recv.at[at], z, column * 2 + 1
                ).start()

    def reducer(s):
        row = jnp.zeros(square_out.shape, jnp.float32)
        for t in range(tensors):
            remote(
                square_out, square_in.at[s // 2, t], square_send.at[0], square_recv.at[s // 2, t], z, q
            ).wait_recv()
            row += square_in[s // 2, t]
        scale = lax.rsqrt(row / full + epsilon) / SPREAD
        sums[...] = jnp.concatenate([scale] * (rows // 8), axis=0).T

        @pl.when(jnp.logical_and(s == 3, q == 0))
        def _():
            for sub in range(SUBS):
                remote(ahead.at[sub], hidden.at[sub], ahead_send.at[sub], ahead_recv.at[sub], z, 2).wait_send()

        @pl.loop(0, 2)
        def _(half):
            @pl.when(jnp.logical_or(s % 2 == 0, half == column))
            def _():
                reduce_half(s, half)

    @pl.loop(0, sections)
    def _(s):
        @pl.when(q == s)
        def _():
            @pl.when(s > 0)
            def _():
                prepare(s)

            source(s)

        @pl.when(q == 3 - 2 * (s // 2))
        def _():
            relay(s)

        @pl.when(jnp.logical_and(q == 3, s == 1))
        def _():
            prebuild()

        @pl.when(jnp.where(s % 2 == 0, q == s + 1, core == 0))
        def _():
            reducer(s)

    @pl.loop(0, pieces)
    def _(j):
        t, half, sub = in_order(j)
        at = piece_at(t, half, sub)
        along = j < pieces // 2
        mine_first = jnp.logical_and(along, j % tensors == 0)

        def come(send):
            return remote(gathered.at[at], gathered.at[at], send, gather_recv.at[at], z, column * 2 + 1)

        @pl.when(jnp.logical_or(core == 1, jnp.logical_not(mine_first)))
        def _():
            come(core_send.at[at]).wait_recv()

        @pl.when(jnp.logical_and(core == 0, jnp.logical_not(mine_first)))
        def _():
            come(core_send.at[at]).start()

            @pl.when(along)
            def _():
                remote(
                    gathered.at[at], gathered.at[at], cross_send.at[at], gather_recv.at[at], z, (q + 2) % sections
                ).start()

        head_copy(j).wait()
        mine = gathered[at]
        total[...] += lax.dot_general(
            panel[j % SLOTS, :vocab_rows], mine, (((1,), (1,)), ((), ())), preferred_element_type=jnp.float32
        )
        wide = mine.astype(jnp.float32)
        squares[...] += lane_sums(wide * wide)

        @pl.when(j + SLOTS < pieces)
        def _():
            head_copy(j + SLOTS).start()

    final = jnp.sum(squares[...].T, axis=0, keepdims=True)
    scale = lax.rsqrt(final / full + epsilon)
    logits = total[...] * scale
    top = jnp.max(logits, axis=0, keepdims=True)
    count = jnp.sum(jnp.exp(logits - top), axis=0, keepdims=True)
    wanted = jnp.concatenate([targets_ref[k : k + 1] for k in range(targets_ref.shape[0])], axis=1)
    ids = lax.broadcasted_iota(jnp.int32, logits.shape, 0) + me * vocab_rows
    chosen = jnp.sum(jnp.where(ids == wanted, logits, 0.0), axis=0, keepdims=True)
    stats_out[...] = jnp.concatenate([top, count, chosen, jnp.zeros((5, rows), jnp.float32)], axis=0)

    @pl.loop(1, everyone)
    def _(k):
        other = (me + k) % everyone
        remote(
            stats_out, stats_in.at[me], stats_send.at[k], stats_recv.at[me], other // sections, other % sections
        ).start()

    stats_in[me] = stats_out[...]

    @pl.loop(1, everyone)
    def _(k):
        other = (me + k) % everyone
        remote(stats_out, stats_in.at[other], stats_send.at[k], stats_recv.at[other], z, q).wait_recv()

    highest = stats_in[0]
    for k in range(1, everyone):
        highest = jnp.maximum(highest, stats_in[k])
    highest = highest[0:1]
    exps = jnp.zeros((1, rows), jnp.float32)
    hit = jnp.zeros((1, rows), jnp.float32)
    for k in range(everyone):
        stat = stats_in[k]
        exps += stat[1:2] * jnp.exp(stat[0:1] - highest)
        hit += stat[2:3]
    loss = highest + jnp.log(exps) - hit
    mean = jnp.sum(loss, axis=1, keepdims=True) / rows
    out_ref[...] = jnp.concatenate(
        [loss, jnp.broadcast_to(mean, (1, rows)), jnp.zeros((6, rows), jnp.float32)], axis=0
    )

    @pl.loop(0, pieces)
    def _(j):
        remote(outgoing.at[j], arrived.at[0, 0, 0], part_send.at[j], part_recv.at[0, 0, 0], z, q).wait_send()

    @pl.loop(0, 2 * tensors)
    def _(j):
        @pl.when(jnp.logical_or(core == 1, j < tensors))
        def _():
            remote(square_out, square_in.at[0, 0], square_send.at[j], square_recv.at[0, 0], z, q).wait_send()

    for half in range(2):
        remote(
            hidden.at[pl.ds(half * SUBS, SUBS)], residual.at[0], rest_send.at[half], rest_recv.at[0], z, q
        ).wait_send()

    @pl.when(core == 1)
    def _():
        @pl.loop(0, 2 * tensors * SUBS)
        def _(j):
            kind, by = j // (tensors * SUBS), j % (tensors * SUBS)

            @pl.when(by // SUBS != z)
            def _():
                remote(
                    relayed.at[kind, by], relayed.at[kind, by], relay_send.at[kind, by], relay_recv.at[kind, by], z, q
                ).wait_send()

    @pl.when(core == 0)
    def _():
        for sub in range(SUBS):
            for k in range(1, tensors):
                remote(
                    gathered.at[0], gathered.at[0], own_send.at[sub, k], gather_recv.at[0], z, q
                ).wait_send()

        @pl.loop(0, pieces)
        def _(j):
            remote(gathered.at[j], gathered.at[j], core_send.at[j], gather_recv.at[j], z, q).wait_send()

        @pl.loop(0, tensors * SUBS)
        def _(j):
            at = piece_at(j // SUBS, column, j % SUBS)
            remote(gathered.at[at], gathered.at[at], cross_send.at[at], gather_recv.at[at], z, q).wait_send()

    @pl.loop(1, everyone)
    def _(k):
        remote(stats_out, stats_in.at[0], stats_send.at[k], stats_recv.at[0], z, q).wait_send()


def chain(mask, inputs, gains, targets, values, head):
    tensors = lax.axis_size("tensor")
    rows, width = inputs.shape
    piece = width // (2 * SUBS)
    pieces = 2 * SUBS * tensors
    everyone = tensors * lax.axis_size("section")
    vocab_rows = head.shape[0]
    half16, single = jnp.bfloat16, jnp.float32
    dma = pltpu.SemaphoreType.DMA
    vmem = pl.BlockSpec(memory_space=pltpu.VMEM)
    anywhere = pl.BlockSpec(memory_space=pl.ANY)
    out = pl.pallas_call(
        functools.partial(chain_kernel, tensors),
        out_shape=jax.ShapeDtypeStruct((8, rows), single),
        in_specs=[vmem, vmem, vmem, vmem, anywhere, anywhere],
        out_specs=vmem,
        scratch_shapes=[
            pltpu.VMEM((SLOTS, width, piece), half16),
            pltpu.VMEM((values.shape[0] + 16, HALF, PAIR), half16),
            pltpu.SMEM(mask.shape, jnp.int32),
            pltpu.VMEM(mask.shape, jnp.int32),
            dma(()),
            pltpu.VMEM((rows, width), half16),
            pltpu.VMEM((256, 256), half16),
            pltpu.VMEM((2 * SUBS, rows, piece), half16),
            pltpu.VMEM((rows, 128), single),
            pltpu.VMEM((pieces, rows, piece), half16),
            pltpu.VMEM((2, tensors * SUBS, rows, piece), half16),
            pltpu.VMEM((2, tensors, SUBS, rows, piece), half16),
            pltpu.VMEM((2, SUBS, rows, piece), half16),
            pltpu.VMEM((SUBS, rows, piece), half16),
            pltpu.VMEM((pieces, rows, piece), half16),
            pltpu.VMEM((rows, 128), single),
            pltpu.VMEM((vocab_rows, rows), single),
            pltpu.VMEM((8, rows), single),
            pltpu.VMEM((2, tensors, 8, rows), single),
            pltpu.VMEM((8, rows), single),
            pltpu.VMEM((everyone, 8, rows), single),
            dma((SLOTS,)),
            dma((SLOTS,)),
            dma((pieces,)),
            dma((2, tensors, SUBS)),
            dma((2, tensors * SUBS)),
            dma((2, tensors * SUBS)),
            dma((2,)),
            dma((2,)),
            dma((2 * tensors,)),
            dma((2, tensors)),
            dma((SUBS,)),
            dma((SUBS,)),
            dma((SUBS, tensors)),
            dma((pieces,)),
            dma((pieces,)),
            dma((pieces,)),
            dma((everyone,)),
            dma((everyone,)),
        ],
        compiler_params=pltpu.CompilerParams(
            collective_id=0, has_side_effects=True, vmem_limit_bytes=62 << 20
        ),
    )(mask, inputs, gains, targets, values, head)
    return out[0], out[1, :1]


def joined_loss(logits_top, total, chosen):
    stacked = jnp.stack([logits_top, total, chosen])
    everything = lax.all_gather(stacked, ("tensor", "section"))
    tops = everything[:, 0]
    top = jnp.max(tops, axis=0)
    total = jnp.sum(everything[:, 1] * jnp.exp(tops - top[None, :]), axis=0)
    return top + jnp.log(total) - jnp.sum(everything[:, 2], axis=0)


def general(inputs, gains, panel, head, targets):
    section_count = lax.axis_size("section")
    tensor_index = lax.axis_index("tensor")
    section_index = lax.axis_index("section")
    rows, local_width = inputs.shape
    full = panel.shape[1]
    gain = lax.dynamic_slice(gains, (tensor_index * local_width,), (local_width,))
    gain = gain.astype(jnp.float32)
    incoming = inputs
    for moment in range(section_count):
        current = jnp.where(section_index == 0, inputs, incoming) if moment else inputs
        wide = current.astype(jnp.float32)
        sumsq = lax.psum(jnp.sum(wide * wide, axis=1), "tensor")
        scaled = (wide * gain).astype(jnp.bfloat16)
        turned = scaled.reshape(rows, local_width // BLK, HALF, 2).transpose(0, 1, 3, 2)
        partial = jnp.dot(turned.reshape(rows, local_width), panel, preferred_element_type=jnp.float32)
        product = lax.psum_scatter(partial, "tensor", scatter_dimension=1, tiled=True)
        update = product * lax.rsqrt(sumsq[:, None] / full + epsilon)
        outgoing = (wide + update).astype(jnp.bfloat16)
        if moment < section_count - 1:
            incoming = shifted(outgoing, "section", 1)
    vocab_rows = head.shape[0]
    final = jnp.where(section_index == section_count - 1, outgoing, jnp.zeros_like(outgoing))
    relayed = lax.psum(final, "section")
    portion = lax.all_gather(relayed, "tensor", axis=1, tiled=True)
    raw_logits = lax.dot_general(
        portion, head, (((1,), (1,)), ((), ())), preferred_element_type=jnp.float32
    )
    widened = portion.astype(jnp.float32)
    final_sumsq = jnp.sum(widened * widened, axis=1)
    logits = raw_logits * lax.rsqrt(final_sumsq[:, None] / full + epsilon)
    vocab_start = (tensor_index * section_count + section_index) * vocab_rows
    local_ids = targets - vocab_start
    matches = jnp.arange(vocab_rows, dtype=jnp.int32)[None, :] == local_ids[:, None]
    target_logit = jnp.sum(jnp.where(matches, logits, 0.0), axis=1)
    local_top = jnp.max(logits, axis=1)
    local_total = jnp.sum(jnp.exp(logits - local_top[:, None]), axis=1)
    losses = joined_loss(local_top, local_total, target_logit)
    return losses, jnp.mean(losses).reshape(1)


def on_device(inputs, gains, keep_mask, block_values, head, targets):
    micro_count, row_count, width = inputs.shape
    rows = micro_count * row_count
    own = inputs.reshape(rows, width)
    ids = targets.reshape(rows)
    mask, values = keep_mask[0], block_values[0]
    piece = width // (2 * SUBS)
    fits = lax.axis_size("section") == 4 and rows == 128 and piece % 256 == 0 and head.shape[0] <= width
    if fits and head.shape[0] % 16 == 0 and values.shape[0] * values.shape[1] == SLOTS * width * piece:
        losses, mean_loss = chain(mask, own, gains, targets, values, head)
    else:
        losses, mean_loss = general(own, gains[0], build_panel(mask, values), head, ids)
    return losses.reshape(micro_count, row_count), mean_loss


def solution(mesh):
    placed = (
        P("groups", None, "tensor"),
        P("section", None),
        P("section", "tensor", None),
        P("section", "tensor", None),
        P(("tensor", "section"), None),
        P("groups", None),
    )
    return jax.shard_map(
        on_device,
        mesh=mesh,
        in_specs=placed,
        out_specs=(P("groups", None), P("groups")),
        check_vma=False,
    )
```

```python
import functools

import jax
import jax.numpy as jnp
from jax import lax
from jax.experimental import pallas as pl
from jax.experimental.pallas import tpu as pltpu
from jax.sharding import PartitionSpec as P

BLK = 64
PAIR = 2 * BLK
HALF = BLK // 2

epsilon = 1e-05
MESH = pl.DeviceIdType.MESH


def shifted(block, axis, distance):
    devices = range(lax.axis_size(axis))
    route = [(i - distance, i) for i in devices if i - distance in devices]
    return lax.ppermute(block, axis, route)


def slot_index(mask, slot_count):
    band_rows, block_count = mask.shape
    kept = (mask > 0).astype(jnp.float32)
    upper = (jnp.arange(block_count)[:, None] <= jnp.arange(block_count)[None, :]).astype(jnp.float32)
    within = jnp.dot(kept, upper)
    lower = (jnp.arange(band_rows)[:, None] > jnp.arange(band_rows)[None, :]).astype(jnp.float32)
    running = within + jnp.dot(lower, within[:, -1:])
    slots = jnp.clip(running.astype(jnp.int32) - 1, 0, slot_count - 1)
    return jnp.where(mask > 0, slots, slot_count)


def build_body(chunks, index_ref, values_ref, panel_ref, listed):
    step = pl.program_id(0)
    chunk = values_ref.shape[0]
    slot_count = chunks * chunk
    block_count = panel_ref.shape[1] // BLK
    band = panel_ref.shape[0] // BLK

    @pl.when(step == 0)
    def _():
        listed[slot_count] = jnp.zeros((HALF, PAIR), jnp.bfloat16)

    @pl.when(step < chunks)
    def _():
        groups = chunk // 16

        @pl.loop(0, groups, unroll=4 if groups % 4 == 0 else 1)
        def _(group):
            at = pl.multiple_of(group * 16, 16)
            parts = [values_ref[pl.ds(at, 16), m * PAIR : (m + 1) * PAIR] for m in range(HALF)]
            listed[pl.ds(step * chunk + at, 16)] = jnp.transpose(jnp.stack(parts, axis=0), (1, 0, 2))

    @pl.when(step >= chunks)
    def _():
        low = lax.broadcasted_iota(jnp.int32, (HALF, PAIR), 1) < BLK

        def turned(block):
            return jnp.concatenate([block[:, BLK:], block[:, :BLK]], axis=1)

        @pl.loop(0, band)
        def _(row):
            first = ((step - chunks) * band + row) * block_count
            top = pl.multiple_of(row * BLK, BLK)
            for pair in range(block_count // 2):
                left = listed[index_ref[first + 2 * pair]]
                right = listed[index_ref[first + 2 * pair + 1]]
                lanes = slice(pair * PAIR, (pair + 1) * PAIR)
                panel_ref[pl.ds(top, HALF), lanes] = jnp.where(low, left, turned(right))
                panel_ref[pl.ds(top + HALF, HALF), lanes] = jnp.where(low, turned(left), right)


def build_panel(mask, values):
    band_rows, block_count = mask.shape
    slot_count, size = values.shape
    index = slot_index(mask, slot_count)
    chunk = next(c for c in (512, 192, 64, 32, 16) if slot_count % c == 0)
    chunks = slot_count // chunk
    band = 4 if band_rows % 4 == 0 else 1
    spec = pltpu.PrefetchScalarGridSpec(
        num_scalar_prefetch=1,
        grid=(chunks + band_rows // band,),
        in_specs=[pl.BlockSpec((chunk, size), lambda i, *_: (jnp.minimum(i, chunks - 1), 0))],
        out_specs=pl.BlockSpec((band * BLK, block_count * BLK), lambda i, *_: (jnp.maximum(i - chunks, 0), 0)),
        scratch_shapes=[pltpu.VMEM((slot_count + 1, HALF, PAIR), jnp.bfloat16)],
    )
    return pl.pallas_call(
        functools.partial(build_body, chunks),
        grid_spec=spec,
        out_shape=jax.ShapeDtypeStruct((band_rows * BLK, block_count * BLK), jnp.bfloat16),
        compiler_params=pltpu.CompilerParams(
            dimension_semantics=("arbitrary",), vmem_limit_bytes=50 << 20
        ),
    )(index.reshape(-1), values)


SPREAD = 1024.0


def coded(part):
    wide = part * SPREAD
    wide = wide * jnp.abs(wide)
    return (wide * jnp.abs(wide)).astype(jnp.bfloat16)


def decoded(code):
    wide = code.astype(jnp.float32)
    size = jnp.maximum(jnp.abs(wide), 1e-37)
    once = lax.rsqrt(size)
    return wide * once * lax.rsqrt(size * once)


SUBS = 2
SLOTS = 12
GROUP = 2


def chain_kernel(
    tensors, mask_ref, inputs_ref, gains_ref, targets_ref, values_ref, head_ref, out_ref,
    panel, listed, index, index_wide, index_sem, lhs, turn, hidden, sums, outgoing, relayed, arrived, residual, ahead, gathered, squares, total,
    square_out, square_in, stats_out, stats_in,
    panel_sem, head_sem, part_send, part_recv, relay_send, relay_recv, rest_send, rest_recv, square_send, square_recv,
    ahead_send, ahead_recv, own_send, cross_send, core_send, gather_recv, stats_send, stats_recv,
):
    sections = 4
    rows, width = inputs_ref.shape
    piece = panel.shape[2]
    pieces = width * tensors // piece
    slot_count, size = values_ref.shape
    per = width * piece // size
    stages = slot_count // per
    band_rows, block_count = mask_ref.shape
    full = width * tensors
    vocab_rows = head_ref.shape[0]
    z = lax.axis_index("tensor")
    q = lax.axis_index("section")
    column = q // 2
    core = q % 2

    def remote(src, dst, send, recv, t, s):
        return pltpu.make_async_remote_copy(
            src_ref=src, dst_ref=dst, send_sem=send, recv_sem=recv,
            device_id={"tensor": t, "section": s}, device_id_type=MESH,
        )

    def piece_at(t, half, sub):
        return (t * 2 + half) * SUBS + sub

    def out_order(j):
        sub, rest = j // (2 * tensors), j % (2 * tensors)
        others = tensors - 1
        step = rest % others
        own = rest >= 2 * others
        half = jnp.where(rest < others, 1 - column, column)
        t = (z + (step + 1) % others + 1) % tensors
        return jnp.where(own, z, t), jnp.where(own, rest - 2 * others, half), sub

    def in_order(j):
        half = jnp.where(j < pieces // 2, column, 1 - column)
        return (z + j) % tensors, half, j // tensors % SUBS

    low = lax.broadcasted_iota(jnp.int32, (HALF, PAIR), 1) < BLK

    def block_row(row, first):
        evens, odds = [], []
        for pair in range(piece // PAIR):
            left = listed[index[row, first + 2 * pair]]
            right = listed[index[row, first + 2 * pair + 1]]
            evens.append(jnp.where(low, left, pltpu.roll(right, BLK, 1)))
            odds.append(jnp.where(low, pltpu.roll(left, BLK, 1), right))
        return jnp.concatenate(evens, axis=1), jnp.concatenate(odds, axis=1)

    def first_block(j):
        t, half, sub = out_order(j)
        return piece_at(t, half, sub) * (piece // BLK)

    def build(j):
        @pl.loop(0, width // BLK, unroll=4)
        def _(row):
            top = pl.multiple_of(row * BLK, BLK)
            even, odd = block_row(row, first_block(j))
            panel[j % SLOTS, pl.ds(top, HALF)] = even
            panel[j % SLOTS, pl.ds(top + HALF, HALF)] = odd

    def product_from_list(j):
        part = jnp.zeros((rows, piece), jnp.float32)
        for k in range(width // 256):
            tiles = []
            for row in range(256 // BLK):
                tiles += block_row(k * (256 // BLK) + row, first_block(j))
            part += jnp.dot(
                lhs[:, k * 256 : (k + 1) * 256], jnp.concatenate(tiles, axis=0), preferred_element_type=jnp.float32
            )
        return part

    def prebuild():
        @pl.loop(0, SLOTS)
        def _(j):
            build(j)

    def head_copy(j):
        t, half, sub = in_order(j)
        at = piece_at(t, half, sub)
        return pltpu.make_async_copy(
            head_ref.at[:, pl.ds(pl.multiple_of(at * piece, piece), piece)],
            panel.at[j % SLOTS, pl.ds(0, vocab_rows)], head_sem.at[j % SLOTS],
        )

    cuts = size // piece

    @pl.loop(0, stages * cuts)
    def _(k):
        stage, cut = k // cuts, k % cuts
        pltpu.make_async_copy(
            values_ref.at[pl.ds(pl.multiple_of(stage * per, per), per), pl.ds(pl.multiple_of(cut * piece, piece), piece)],
            panel.at[stage, pl.ds(pl.multiple_of(cut * per, per), per)], panel_sem.at[stage],
        ).start()

    barrier = pltpu.get_barrier_semaphore()
    me = z * sections + q
    everyone = tensors * sections

    @pl.loop(1, everyone)
    def _(k):
        other = (me + k) % everyone
        pl.semaphore_signal(
            barrier, inc=1, device_id={"tensor": other // sections, "section": other % sections},
            device_id_type=MESH,
        )

    kept = (mask_ref[...] > 0).astype(jnp.float32)
    across = lax.broadcasted_iota(jnp.int32, (block_count, block_count), 0)
    along = lax.broadcasted_iota(jnp.int32, (block_count, block_count), 1)
    within = jnp.dot(kept, jnp.where(across <= along, 1.0, 0.0), preferred_element_type=jnp.float32)
    across = lax.broadcasted_iota(jnp.int32, (band_rows, band_rows), 0)
    along = lax.broadcasted_iota(jnp.int32, (band_rows, band_rows), 1)
    counts = jnp.broadcast_to(within[:, block_count - 1 :], (band_rows, block_count))
    before = jnp.dot(jnp.where(across > along, 1.0, 0.0), counts, preferred_element_type=jnp.float32)
    running = (within + before).astype(jnp.int32)
    index_wide[...] = jnp.where(kept > 0, jnp.clip(running - 1, 0, slot_count - 1), slot_count)
    index_copy = pltpu.make_async_copy(index_wide, index, index_sem)
    index_copy.start()

    wide_row = lax.broadcasted_iota(jnp.int32, turn.shape, 0)
    wide_lane = lax.broadcasted_iota(jnp.int32, turn.shape, 1)
    inside = wide_lane % BLK
    comes_from = wide_lane - inside + 2 * (inside % HALF) + inside // HALF
    turn[...] = jnp.where(wide_row == comes_from, 1.0, 0.0).astype(jnp.bfloat16)
    total[...] = jnp.zeros_like(total)
    squares[...] = jnp.zeros_like(squares)

    @pl.when(q == 0)
    def _():
        for k in range(2 * SUBS):
            hidden[k] = inputs_ref[:, k * piece : (k + 1) * piece]

    def lane_sums(value):
        folded = value[:, :128]
        for k in range(1, value.shape[1] // 128):
            folded += value[:, k * 128 : (k + 1) * 128]
        return folded

    def summing(s, half):
        return jnp.where(s % 2 == 0, s + 1, half * 2), jnp.where(s % 2 == 0, half, s // 2)

    def prepare(s):
        @pl.when(s == 2)
        def _():
            for sub in range(SUBS):
                remote(ahead.at[sub], hidden.at[sub], ahead_send.at[sub], ahead_recv.at[sub], z, q).wait_recv()

        folded = jnp.zeros((rows, 128), jnp.float32)
        for k in range(2 * SUBS):
            wide = hidden[k].astype(jnp.float32)
            folded += lane_sums(wide * wide)
            gain = gains_ref[:, pl.ds(pl.multiple_of(z * width + k * piece, piece), piece)].astype(jnp.float32)
            scaled = (wide * gain).astype(jnp.bfloat16)
            for b in range(piece // 256):
                turned = jnp.dot(
                    scaled[:, b * 256 : (b + 1) * 256], turn[...], preferred_element_type=jnp.float32
                )
                lhs[:, k * piece + b * 256 : k * piece + (b + 1) * 256] = turned.astype(jnp.bfloat16)
        row = jnp.sum(folded.T, axis=0, keepdims=True)
        square_out[...] = jnp.broadcast_to(row, square_out.shape)

        @pl.loop(0, 2 * tensors)
        def _(j):
            @pl.when(jnp.logical_or(s % 2 == 1, j < tensors))
            def _():
                remote(
                    square_out, square_in.at[s // 2, z], square_send.at[j], square_recv.at[s // 2, z],
                    j % tensors, summing(s, j // tensors)[0],
                ).start()

    pl.semaphore_wait(barrier, everyone - 1)

    @pl.when(q == 0)
    def _():
        prepare(0)

    listed[slot_count] = jnp.zeros((HALF, PAIR), jnp.bfloat16)

    @pl.loop(0, stages)
    def _(stage):
        pltpu.make_async_copy(panel.at[stage], panel.at[stage], panel_sem.at[stage]).wait()

        @pl.loop(0, per // 16, unroll=4)
        def _(group):
            at = pl.multiple_of(group * 16, 16)
            parts = []
            for m in range(HALF):
                cut, lane = m * PAIR // piece, m * PAIR % piece
                parts.append(panel[stage, pl.ds(cut * per + at, 16), lane : lane + PAIR])
            listed[pl.ds(stage * per + at, 16)] = jnp.transpose(jnp.stack(parts, axis=0), (1, 0, 2))

    index_copy.wait()

    @pl.when(jnp.logical_or(q == 1, q == 2))
    def _():
        prebuild()

    def source(s):
        def send_hidden(half):
            target, slot = summing(s, half)
            remote(
                hidden.at[pl.ds(half * SUBS, SUBS)], residual.at[slot], rest_send.at[half], rest_recv.at[slot], z, target
            ).start()

        def crosses(half):
            return jnp.logical_and(s % 2 == 1, half != column)

        for half in range(2):
            @pl.when(jnp.logical_not(crosses(half)))
            def _():
                send_hidden(half)

        def piece_of(j):
            return piece_at(*out_order(j))

        def send(j):
            t, half, sub = out_order(j)
            at = piece_at(t, half, sub)
            straight = jnp.logical_or(t == z, half == column)

            @pl.when(straight)
            def _():
                target, slot = summing(s, half)
                remote(
                    outgoing.at[at], arrived.at[slot, z, sub], part_send.at[at], part_recv.at[slot, z, sub], t, target
                ).start()

            @pl.when(jnp.logical_not(straight))
            def _():
                by = t * SUBS + sub
                remote(
                    outgoing.at[at], relayed.at[s % 2, by], part_send.at[at], relay_recv.at[s % 2, by],
                    z, (1 - column) * 2 + 1,
                ).start()

        @pl.loop(0, pieces // GROUP)
        def _(group):
            js = [group * GROUP + k for k in range(GROUP)]
            late = jnp.logical_or(s == 0, js[0] >= SLOTS)

            @pl.when(late)
            def _():
                for j in js:
                    outgoing[piece_of(j)] = coded(product_from_list(j))

            @pl.when(jnp.logical_not(late))
            def _():
                for j in js:
                    part = jnp.dot(lhs[...], panel[j % SLOTS], preferred_element_type=jnp.float32)
                    outgoing[piece_of(j)] = coded(part)

            for j in js:
                send(j)

        for half in range(2):
            @pl.when(crosses(half))
            def _():
                send_hidden(half)
        @pl.loop(0, SLOTS)
        def _(j):
            head_copy(j).start()

    def relay(s):
        @pl.loop(0, tensors * SUBS)
        def _(j):
            t, sub = (z + 2 + j % tensors) % tensors, j // tensors
            by = t * SUBS + sub

            @pl.when(t != z)
            def _():
                remote(
                    relayed.at[s % 2, by], relayed.at[s % 2, by], relay_send.at[s % 2, by], relay_recv.at[s % 2, by], z, q
                ).wait_recv()
                target, slot = summing(s, column)
                remote(
                    relayed.at[s % 2, by], arrived.at[slot, z, sub], relay_send.at[s % 2, by],
                    part_recv.at[slot, z, sub], t, target,
                ).start()

    def reduce_half(s, half):
        slot = summing(s, half)[1]
        is_final = s == sections - 1
        remote(
            residual.at[slot], residual.at[slot], rest_send.at[0], rest_recv.at[slot], z, q
        ).wait_recv()
        for sub in range(SUBS):
            for t in range(tensors):
                remote(
                    outgoing.at[0], arrived.at[slot, t, sub], part_send.at[0], part_recv.at[slot, t, sub], z, q
                ).wait_recv()
            for b in range(piece // 128):
                lanes = slice(b * 128, (b + 1) * 128)
                product = jnp.zeros((rows, 128), jnp.float32)
                for t in range(tensors):
                    product += decoded(arrived[slot, t, sub, :, lanes])
                wide = residual[slot, sub, :, lanes].astype(jnp.float32)
                ahead[sub, :, lanes] = (wide + product * sums[...]).astype(jnp.bfloat16)

            @pl.when(q == s + 1)
            def _():
                hidden[half * SUBS + sub] = ahead[sub]

            @pl.when(jnp.logical_and(q == 0, s == 1))
            def _():
                remote(
                    ahead.at[sub], hidden.at[half * SUBS + sub], ahead_send.at[sub], ahead_recv.at[sub], z, 2
                ).start()

            @pl.when(is_final)
            def _():
                at = piece_at(z, column, sub)
                gathered[at] = ahead[sub]
                for k in range(1, tensors):
                    remote(
                        gathered.at[at], gathered.at[at], own_send.at[sub, k], gather_recv.at[at], (z + k) % tensors, q
                    ).start()
                remote(
                    gathered.at[at], gathered.at[at], cross_send.at[at], gather_recv.at[at], z, (q + 2) % sections
                ).start()
                remote(
                    gathered.at[at], gathered.at[at], core_send.at[at], gather_recv.at[at], z, column * 2 + 1
                ).start()

    def reducer(s):
        row = jnp.zeros(square_out.shape, jnp.float32)
        for t in range(tensors):
            remote(
                square_out, square_in.at[s // 2, t], square_send.at[0], square_recv.at[s // 2, t], z, q
            ).wait_recv()
            row += square_in[s // 2, t]
        scale = lax.rsqrt(row / full + epsilon) / SPREAD
        sums[...] = jnp.concatenate([scale] * (rows // 8), axis=0).T

        @pl.when(jnp.logical_and(s == 3, q == 0))
        def _():
            for sub in range(SUBS):
                remote(ahead.at[sub], hidden.at[sub], ahead_send.at[sub], ahead_recv.at[sub], z, 2).wait_send()

        @pl.loop(0, 2)
        def _(half):
            @pl.when(jnp.logical_or(s % 2 == 0, half == column))
            def _():
                reduce_half(s, half)

    @pl.loop(0, sections)
    def _(s):
        @pl.when(q == s)
        def _():
            @pl.when(s > 0)
            def _():
                prepare(s)

            source(s)

        @pl.when(q == 3 - 2 * (s // 2))
        def _():
            relay(s)

        @pl.when(jnp.logical_and(q == 3, s == 1))
        def _():
            prebuild()

        @pl.when(jnp.where(s % 2 == 0, q == s + 1, core == 0))
        def _():
            reducer(s)

    @pl.loop(0, pieces)
    def _(j):
        t, half, sub = in_order(j)
        at = piece_at(t, half, sub)
        along = j < pieces // 2
        mine_first = jnp.logical_and(along, j % tensors == 0)

        def come(send):
            return remote(gathered.at[at], gathered.at[at], send, gather_recv.at[at], z, column * 2 + 1)

        @pl.when(jnp.logical_or(core == 1, jnp.logical_not(mine_first)))
        def _():
            come(core_send.at[at]).wait_recv()

        @pl.when(jnp.logical_and(core == 0, jnp.logical_not(mine_first)))
        def _():
            come(core_send.at[at]).start()

            @pl.when(along)
            def _():
                remote(
                    gathered.at[at], gathered.at[at], cross_send.at[at], gather_recv.at[at], z, (q + 2) % sections
                ).start()

        head_copy(j).wait()
        mine = gathered[at]
        total[...] += lax.dot_general(
            panel[j % SLOTS, :vocab_rows], mine, (((1,), (1,)), ((), ())), preferred_element_type=jnp.float32
        )
        wide = mine.astype(jnp.float32)
        squares[...] += lane_sums(wide * wide)

        @pl.when(j + SLOTS < pieces)
        def _():
            head_copy(j + SLOTS).start()

    final = jnp.sum(squares[...].T, axis=0, keepdims=True)
    scale = lax.rsqrt(final / full + epsilon)
    logits = total[...] * scale
    top = jnp.max(logits, axis=0, keepdims=True)
    count = jnp.sum(jnp.exp(logits - top), axis=0, keepdims=True)
    wanted = jnp.concatenate([targets_ref[k : k + 1] for k in range(targets_ref.shape[0])], axis=1)
    ids = lax.broadcasted_iota(jnp.int32, logits.shape, 0) + me * vocab_rows
    chosen = jnp.sum(jnp.where(ids == wanted, logits, 0.0), axis=0, keepdims=True)
    stats_out[...] = jnp.concatenate([top, count, chosen, jnp.zeros((5, rows), jnp.float32)], axis=0)

    @pl.loop(1, everyone)
    def _(k):
        other = (me + k) % everyone
        remote(
            stats_out, stats_in.at[me], stats_send.at[k], stats_recv.at[me], other // sections, other % sections
        ).start()

    stats_in[me] = stats_out[...]

    @pl.loop(1, everyone)
    def _(k):
        other = (me + k) % everyone
        remote(stats_out, stats_in.at[other], stats_send.at[k], stats_recv.at[other], z, q).wait_recv()

    highest = stats_in[0]
    for k in range(1, everyone):
        highest = jnp.maximum(highest, stats_in[k])
    highest = highest[0:1]
    exps = jnp.zeros((1, rows), jnp.float32)
    hit = jnp.zeros((1, rows), jnp.float32)
    for k in range(everyone):
        stat = stats_in[k]
        exps += stat[1:2] * jnp.exp(stat[0:1] - highest)
        hit += stat[2:3]
    loss = highest + jnp.log(exps) - hit
    mean = jnp.sum(loss, axis=1, keepdims=True) / rows
    out_ref[...] = jnp.concatenate(
        [loss, jnp.broadcast_to(mean, (1, rows)), jnp.zeros((6, rows), jnp.float32)], axis=0
    )

    @pl.loop(0, pieces)
    def _(j):
        remote(outgoing.at[j], arrived.at[0, 0, 0], part_send.at[j], part_recv.at[0, 0, 0], z, q).wait_send()

    @pl.loop(0, 2 * tensors)
    def _(j):
        @pl.when(jnp.logical_or(core == 1, j < tensors))
        def _():
            remote(square_out, square_in.at[0, 0], square_send.at[j], square_recv.at[0, 0], z, q).wait_send()

    for half in range(2):
        remote(
            hidden.at[pl.ds(half * SUBS, SUBS)], residual.at[0], rest_send.at[half], rest_recv.at[0], z, q
        ).wait_send()

    @pl.when(core == 1)
    def _():
        @pl.loop(0, 2 * tensors * SUBS)
        def _(j):
            kind, by = j // (tensors * SUBS), j % (tensors * SUBS)

            @pl.when(by // SUBS != z)
            def _():
                remote(
                    relayed.at[kind, by], relayed.at[kind, by], relay_send.at[kind, by], relay_recv.at[kind, by], z, q
                ).wait_send()

    @pl.when(core == 0)
    def _():
        for sub in range(SUBS):
            for k in range(1, tensors):
                remote(
                    gathered.at[0], gathered.at[0], own_send.at[sub, k], gather_recv.at[0], z, q
                ).wait_send()

        @pl.loop(0, pieces)
        def _(j):
            remote(gathered.at[j], gathered.at[j], core_send.at[j], gather_recv.at[j], z, q).wait_send()

        @pl.loop(0, tensors * SUBS)
        def _(j):
            at = piece_at(j // SUBS, column, j % SUBS)
            remote(gathered.at[at], gathered.at[at], cross_send.at[at], gather_recv.at[at], z, q).wait_send()

    @pl.loop(1, everyone)
    def _(k):
        remote(stats_out, stats_in.at[0], stats_send.at[k], stats_recv.at[0], z, q).wait_send()


def chain(mask, inputs, gains, targets, values, head):
    tensors = lax.axis_size("tensor")
    rows, width = inputs.shape
    piece = width // (2 * SUBS)
    pieces = 2 * SUBS * tensors
    everyone = tensors * lax.axis_size("section")
    vocab_rows = head.shape[0]
    half16, single = jnp.bfloat16, jnp.float32
    dma = pltpu.SemaphoreType.DMA
    vmem = pl.BlockSpec(memory_space=pltpu.VMEM)
    anywhere = pl.BlockSpec(memory_space=pl.ANY)
    out = pl.pallas_call(
        functools.partial(chain_kernel, tensors),
        out_shape=jax.ShapeDtypeStruct((8, rows), single),
        in_specs=[vmem, vmem, vmem, vmem, anywhere, anywhere],
        out_specs=vmem,
        scratch_shapes=[
            pltpu.VMEM((SLOTS, width, piece), half16),
            pltpu.VMEM((values.shape[0] + 16, HALF, PAIR), half16),
            pltpu.SMEM(mask.shape, jnp.int32),
            pltpu.VMEM(mask.shape, jnp.int32),
            dma(()),
            pltpu.VMEM((rows, width), half16),
            pltpu.VMEM((256, 256), half16),
            pltpu.VMEM((2 * SUBS, rows, piece), half16),
            pltpu.VMEM((rows, 128), single),
            pltpu.VMEM((pieces, rows, piece), half16),
            pltpu.VMEM((2, tensors * SUBS, rows, piece), half16),
            pltpu.VMEM((2, tensors, SUBS, rows, piece), half16),
            pltpu.VMEM((2, SUBS, rows, piece), half16),
            pltpu.VMEM((SUBS, rows, piece), half16),
            pltpu.VMEM((pieces, rows, piece), half16),
            pltpu.VMEM((rows, 128), single),
            pltpu.VMEM((vocab_rows, rows), single),
            pltpu.VMEM((8, rows), single),
            pltpu.VMEM((2, tensors, 8, rows), single),
            pltpu.VMEM((8, rows), single),
            pltpu.VMEM((everyone, 8, rows), single),
            dma((SLOTS,)),
            dma((SLOTS,)),
            dma((pieces,)),
            dma((2, tensors, SUBS)),
            dma((2, tensors * SUBS)),
            dma((2, tensors * SUBS)),
            dma((2,)),
            dma((2,)),
            dma((2 * tensors,)),
            dma((2, tensors)),
            dma((SUBS,)),
            dma((SUBS,)),
            dma((SUBS, tensors)),
            dma((pieces,)),
            dma((pieces,)),
            dma((pieces,)),
            dma((everyone,)),
            dma((everyone,)),
        ],
        compiler_params=pltpu.CompilerParams(
            collective_id=0, has_side_effects=True, vmem_limit_bytes=62 << 20
        ),
    )(mask, inputs, gains, targets, values, head)
    return out[0], out[1, :1]


def joined_loss(logits_top, total, chosen):
    stacked = jnp.stack([logits_top, total, chosen])
    everything = lax.all_gather(stacked, ("tensor", "section"))
    tops = everything[:, 0]
    top = jnp.max(tops, axis=0)
    total = jnp.sum(everything[:, 1] * jnp.exp(tops - top[None, :]), axis=0)
    return top + jnp.log(total) - jnp.sum(everything[:, 2], axis=0)


def general(inputs, gains, panel, head, targets):
    section_count = lax.axis_size("section")
    tensor_index = lax.axis_index("tensor")
    section_index = lax.axis_index("section")
    rows, local_width = inputs.shape
    full = panel.shape[1]
    gain = lax.dynamic_slice(gains, (tensor_index * local_width,), (local_width,))
    gain = gain.astype(jnp.float32)
    incoming = inputs
    for moment in range(section_count):
        current = jnp.where(section_index == 0, inputs, incoming) if moment else inputs
        wide = current.astype(jnp.float32)
        sumsq = lax.psum(jnp.sum(wide * wide, axis=1), "tensor")
        scaled = (wide * gain).astype(jnp.bfloat16)
        turned = scaled.reshape(rows, local_width // BLK, HALF, 2).transpose(0, 1, 3, 2)
        partial = jnp.dot(turned.reshape(rows, local_width), panel, preferred_element_type=jnp.float32)
        product = lax.psum_scatter(partial, "tensor", scatter_dimension=1, tiled=True)
        update = product * lax.rsqrt(sumsq[:, None] / full + epsilon)
        outgoing = (wide + update).astype(jnp.bfloat16)
        if moment < section_count - 1:
            incoming = shifted(outgoing, "section", 1)
    vocab_rows = head.shape[0]
    final = jnp.where(section_index == section_count - 1, outgoing, jnp.zeros_like(outgoing))
    relayed = lax.psum(final, "section")
    portion = lax.all_gather(relayed, "tensor", axis=1, tiled=True)
    raw_logits = lax.dot_general(
        portion, head, (((1,), (1,)), ((), ())), preferred_element_type=jnp.float32
    )
    widened = portion.astype(jnp.float32)
    final_sumsq = jnp.sum(widened * widened, axis=1)
    logits = raw_logits * lax.rsqrt(final_sumsq[:, None] / full + epsilon)
    vocab_start = (tensor_index * section_count + section_index) * vocab_rows
    local_ids = targets - vocab_start
    matches = jnp.arange(vocab_rows, dtype=jnp.int32)[None, :] == local_ids[:, None]
    target_logit = jnp.sum(jnp.where(matches, logits, 0.0), axis=1)
    local_top = jnp.max(logits, axis=1)
    local_total = jnp.sum(jnp.exp(logits - local_top[:, None]), axis=1)
    losses = joined_loss(local_top, local_total, target_logit)
    return losses, jnp.mean(losses).reshape(1)


def on_device(inputs, gains, keep_mask, block_values, head, targets):
    micro_count, row_count, width = inputs.shape
    rows = micro_count * row_count
    own = inputs.reshape(rows, width)
    ids = targets.reshape(rows)
    mask, values = keep_mask[0], block_values[0]
    piece = width // (2 * SUBS)
    fits = lax.axis_size("section") == 4 and rows == 128 and piece % 256 == 0 and head.shape[0] <= width
    if fits and head.shape[0] % 16 == 0 and values.shape[0] * values.shape[1] == SLOTS * width * piece:
        losses, mean_loss = chain(mask, own, gains, targets, values, head)
    else:
        losses, mean_loss = general(own, gains[0], build_panel(mask, values), head, ids)
    return losses.reshape(micro_count, row_count), mean_loss


def solution(mesh):
    placed = (
        P("groups", None, "tensor"),
        P("section", None),
        P("section", "tensor", None),
        P("section", "tensor", None),
        P(("tensor", "section"), None),
        P("groups", None),
    )
    return jax.shard_map(
        on_device,
        mesh=mesh,
        in_specs=placed,
        out_specs=(P("groups", None), P("groups")),
        check_vma=False,
    )
```
